32 devices in a mesh: fsdp: 4 (over x, core), ctx: 4 (over z), tp: 2 (over y).
Axes of the slice: x: 2, y: 2, z: 4, core: 2. Of those that a mesh axis runs over, the one named last changes fastest.
Arguments:
- x_in: bfloat16 [8, 1024, 768], P('fsdp', 'ctx'), may hold values from -6 to 6
- out_cot: bfloat16 [8, 1024, 768], P('fsdp', 'ctx'), may hold values from -6 to 6
- seg_ids: int32 [8, 1024], P('fsdp', 'ctx'), may hold values from 0 to 16, as said below
- land_doc: int32 [8, 64], P('fsdp', 'ctx'), may hold values from 0 to 16, as said below
- w_qkv: bfloat16 [768, 3, 768], P(('fsdp', 'ctx'), None, 'tp'), may hold values from -0.21875 to 0.21875
- w_out: bfloat16 [768, 768], P(('fsdp', 'ctx'), 'tp'), may hold values from -0.4375 to 0.4375
- w_up: bfloat16 [768, 3072], P(('fsdp', 'ctx'), 'tp'), may hold values from -0.21875 to 0.21875
- w_down: bfloat16 [768, 3072], P(('fsdp', 'ctx'), 'tp'), may hold values from -0.109375 to 0.109375
- conv_taps: float32 [33, 12], P(None, 'tp'), may hold values from -2 to 2
- head_bias: float32 [2, 768], P(None, 'tp'), may hold values from -6 to 6
- ffn_bias: float32 [3072], P('tp'), may hold values from -4 to 4
- gains: float32 [2, 768], replicated, may hold values from 0.5 to 1.5
- offsets: float32 [4, 768], replicated, may hold values from -4 to 4
Outputs:
- y_out: bfloat16 [8, 1024, 768], P('fsdp', 'ctx')
- x_grad: bfloat16 [8, 1024, 768], P('fsdp', 'ctx')
- w_qkv_grad: float32 [768, 3, 768], P(('fsdp', 'ctx'), None, 'tp')
- w_out_grad: float32 [768, 768], P(('fsdp', 'ctx'), 'tp')
- w_up_grad: float32 [768, 3072], P(('fsdp', 'ctx'), 'tp')
- w_down_grad: float32 [768, 3072], P(('fsdp', 'ctx'), 'tp')
- conv_grad: float32 [33, 12], P(None, 'tp')
- head_bias_grad: float32 [2, 768], P(None, 'tp')
- ffn_bias_grad: float32 [3072], P('tp')
- gains_grad: float32 [2, 768], replicated
- offsets_grad: float32 [4, 768], replicated
The draws below stay inside these ranges and needn't reach their ends.
Inputs may be any that keep to these rules, and one draw needn't show every extreme that they name: `seg_ids`: within each sequence the ids start at 0, never fall and rise by one where a new document begins; every document covers 60 or more consecutive positions, so no id exceeds 1024 // 60 - 1, and some sequence reaches that id. `land_doc`: landmark j of a sequence carries the seg_ids of that sequence's position j * 16.
All inputs are finite; a program needn't handle non-finite values.
Results may differ from the reference program's by a relative error of at most 0.029.
Values may be sent and summed in bfloat16 or wider, within the bound.
No kernel may reach another device: no remote copies, remote signals or barrier semaphores. Data moves between devices by JAX's collectives and lax.ppermute only.
A program may use at most 128 MiB of HBM per device.

```python
import jax
import jax.numpy as jnp
from jax import lax

D = 768
HEADS = 12
HEAD_DIM = 64
FF = 3072
LAND = 64
KW = 33
NEWTON = 6
SEQ_LEN = 1024
DOC_MIN = 60
DOC_LONG = 400
SEQS = 8


def doc_layout(key):
    slot_count = SEQ_LEN // DOC_MIN + 1
    lengths = jax.random.randint(key, (SEQS, slot_count), DOC_MIN, DOC_LONG + 1)
    lengths = lengths.at[0].set(DOC_MIN)
    doc_ends = jnp.cumsum(lengths, axis=1)
    usable = doc_ends <= SEQ_LEN - DOC_MIN
    position = jnp.arange(SEQ_LEN)
    passed = usable[:, None, :] & (doc_ends[:, None, :] <= position[None, :, None])
    return jnp.sum(passed.astype(jnp.int32), axis=2).astype(jnp.int32)


def draw_seg_ids(key, part):
    return doc_layout(jax.random.fold_in(key, 7))


def draw_land_doc(key, part):
    return doc_layout(jax.random.fold_in(key, 7))[:, ::SEQ_LEN // LAND]


def strengthened(values, stream_key, source, target, shards_of, factor):
    def block_of(dim):
        return (jnp.arange(values.shape[dim]) // (values.shape[dim] // shards_of)).reshape((-1,) + (1,) * (values.ndim - 1 - dim))

    first = jax.random.permutation(stream_key, shards_of)[block_of(target)]
    second = (block_of(target) + shards_of // 2) % shards_of
    return jnp.where((block_of(source) == first) | (block_of(source) == second), factor * values, values)


def block_scale(stream_key, shape, shards, low, top_value):
    def one(dim, blocks):
        steps = jax.random.uniform(jax.random.fold_in(jax.random.fold_in(stream_key, 6), dim), (blocks,), jnp.float32, low / len(shards), top_value / len(shards))
        return jnp.repeat(jnp.exp(steps), shape[dim] // blocks).reshape((-1,) + (1,) * (len(shape) - dim - 1))

    level = one(*shards[0])
    for cut in shards[1:]:
        level = level * one(*cut)
    return level


def gaussian(rng, dims, scale, most, pieces=(), held_as=jnp.bfloat16):
    drawn = scale * jax.random.normal(rng, dims, jnp.float32)
    if pieces:
        drawn = drawn * block_scale(rng, dims, pieces, -0.22, 0.18)
    return jnp.clip(drawn, -most, most).astype(held_as)


def heavy_noise(key, shape, scale, reach, split, heavy, kind=jnp.bfloat16):
    values = scale * jax.random.normal(key, shape, jnp.float32)
    if split:
        values = values * block_scale(key, shape, split, -0.22, 0.18)
    return jnp.clip(strengthened(values, jax.random.fold_in(key, 3), *heavy), -reach, reach).astype(kind)


def setup_inputs(seed: int = 0) -> dict:
    arg_keys = jax.random.split(jax.random.key(seed), 14)
    x_in = heavy_noise(arg_keys[0], (SEQS, SEQ_LEN, D), 1.0, 6.0, ((0, 4), (1, 4)), (0, 2, 4, 2.0))
    out_cot = heavy_noise(arg_keys[1], (SEQS, SEQ_LEN, D), 1.0, 6.0, ((0, 4), (1, 4)), (0, 2, 4, 2.0))
    seg_ids = draw_seg_ids(jax.random.fold_in(arg_keys[13], 71), 0)
    land_doc = draw_land_doc(jax.random.fold_in(arg_keys[13], 71), 0)
    w_qkv = gaussian(arg_keys[4], (D, 3, D), D ** -0.5, 0.21875, ((0, 16), (2, 2)))
    w_out = gaussian(arg_keys[5], (D, D), (D // 4) ** -0.5, 0.4375, ((0, 16), (1, 2)))
    w_up = gaussian(arg_keys[6], (D, FF), D ** -0.5, 0.21875, ((0, 16), (1, 2)))
    w_down = gaussian(arg_keys[7], (D, FF), FF ** -0.5, 0.109375, ((0, 16), (1, 2)))
    conv_taps = gaussian(arg_keys[8], (KW, HEADS), 0.15, 2.0, ((1, 2),), jnp.float32)
    head_bias = gaussian(arg_keys[9], (2, D), 0.5, 6.0, ((1, 2),), jnp.float32)
    ffn_bias = gaussian(arg_keys[10], (FF,), 0.3, 4.0, ((0, 2),), jnp.float32)
    gains = jnp.clip(1.0 + 0.1 * jax.random.normal(arg_keys[11], (2, D), jnp.float32), 0.5, 1.5)
    offsets = gaussian(arg_keys[12], (4, D), 0.3, 4.0, (), jnp.float32)
    return dict(x_in=x_in, out_cot=out_cot, seg_ids=seg_ids, land_doc=land_doc, w_qkv=w_qkv, w_out=w_out, w_up=w_up, w_down=w_down, conv_taps=conv_taps, head_bias=head_bias, ffn_bias=ffn_bias, gains=gains, offsets=offsets)


@jax.custom_vjp
def low(v):
    return lax.optimization_barrier(v.astype(jnp.bfloat16)).astype(jnp.float32)

@jax.custom_vjp
def low_back(v):
    return v

def low_keep(v):
    return (low(v), None)

def low_pass(kept, grad):
    return (grad,)

def back_keep(v):
    return (v, None)

def back_low(kept, grad):
    return (low(grad),)
low.defvjp(low_keep, low_pass)
low_back.defvjp(back_keep, back_low)
highest_precision = lax.Precision.HIGHEST
epsilon = 1e-05

def norm_rows(matrix_rows, norm_gain, norm_shift):
    center = matrix_rows - lax.optimization_barrier(jnp.mean(matrix_rows, axis=-1, keepdims=True))
    spread = lax.optimization_barrier(jnp.mean(center * center, axis=-1, keepdims=True))
    return center * lax.rsqrt(spread + epsilon) * norm_gain + norm_shift

def softmax_with_mask(score_matrix, allowed):
    row_top = lax.optimization_barrier(jnp.max(jnp.where(allowed, score_matrix, -1e+30), axis=-1, keepdims=True))
    raised = jnp.where(allowed, jnp.exp(jnp.where(allowed, score_matrix - row_top, 0.0)), 0.0)
    return raised / lax.optimization_barrier(jnp.sum(raised, axis=-1, keepdims=True))

def newton_schulz_inverse(matrix):
    identity = jnp.eye(matrix.shape[-1], dtype=matrix.dtype)
    frobenius = lax.optimization_barrier(jnp.sum(matrix * matrix, axis=(1, 2), keepdims=True))
    approx = jnp.swapaxes(matrix, 1, 2) / frobenius
    for sweep_index in range(NEWTON):
        product = jnp.einsum('hij,hjk->hik', matrix, approx, precision=highest_precision)
        factor = 7.0 * identity - product
        factor = 15.0 * identity - jnp.einsum('hij,hjk->hik', product, factor, precision=highest_precision)
        factor = 13.0 * identity - jnp.einsum('hij,hjk->hik', product, factor, precision=highest_precision)
        approx = 0.25 * jnp.einsum('hij,hjk->hik', approx, factor, precision=highest_precision)
    return approx

def split_heads(matrix):
    return matrix.reshape(matrix.shape[0], HEADS, HEAD_DIM).transpose(1, 0, 2)

def layer(tokens, token_docs, land_ids, w_qkv, w_out, w_up, w_down, conv_taps, head_bias, ffn_bias, gains, offsets):
    length = tokens.shape[0]
    scores_scale_factor = HEAD_DIM ** (-0.5)
    conv_reach = KW // 2
    projected = jnp.einsum('td,dce->tce', tokens, w_qkv, precision=highest_precision)
    queries = low(low_back(projected[:, 0] + head_bias[0]))
    key_rows = low(low_back(projected[:, 1]))
    values = low(low_back(projected[:, 2] + head_bias[1]))
    land_query = low(lax.optimization_barrier(jnp.mean(queries.reshape(LAND, length // LAND, D), axis=1)))
    land_key = low(lax.optimization_barrier(jnp.mean(key_rows.reshape(LAND, length // LAND, D), axis=1)))
    heads_of_queries = split_heads(queries)
    heads_of_keys = split_heads(key_rows)
    heads_of_values = split_heads(values)
    landmark_queries = split_heads(land_query)
    landmark_keys = split_heads(land_key)
    token_mask = token_docs[:, None] == land_ids[None, :]
    landmark_mask = land_ids[:, None] == land_ids[None, :]
    token_kernel = softmax_with_mask(scores_scale_factor * jnp.einsum('ane,ape->anp', heads_of_queries, landmark_keys, precision=highest_precision), token_mask)
    landmark_kernel = softmax_with_mask(scores_scale_factor * jnp.einsum('fbi,fpi->fbp', landmark_queries, landmark_keys, precision=highest_precision), landmark_mask)
    keys_kernel_matrix = softmax_with_mask(scores_scale_factor * jnp.einsum('pon,pwn->pow', landmark_queries, heads_of_keys, precision=highest_precision), token_mask.T)
    landmark_values = jnp.einsum('yxc,ycg->yxg', keys_kernel_matrix, heads_of_values, precision=highest_precision)
    mixing_weights = jnp.einsum('ugy,uyx->ugx', newton_schulz_inverse(landmark_kernel), landmark_values, precision=highest_precision)
    attended_output = jnp.einsum('zcn,znp->zcp', token_kernel, mixing_weights, precision=highest_precision)
    padded_values = jnp.pad(heads_of_values, ((0, 0), (conv_reach, conv_reach), (0, 0)))
    padded_docs = jnp.pad(token_docs, conv_reach, constant_values=-1)
    conv_sum = jnp.zeros_like(attended_output)
    for tap_index in range(KW):
        same_doc = (padded_docs[tap_index:tap_index + length] == token_docs).astype(jnp.float32)
        conv_sum = conv_sum + conv_taps[tap_index][:, None, None] * padded_values[:, tap_index:tap_index + length, :] * same_doc[None, :, None]
    mixed_rows = low(low_back((attended_output + conv_sum).transpose(1, 0, 2).reshape(length, D)))
    branch = low_back(jnp.einsum('te,de->td', mixed_rows, w_out, precision=highest_precision) + offsets[2])
    hidden = norm_rows(tokens + branch, gains[0], offsets[0])
    upward = low_back(jnp.einsum('td,df->tf', low(hidden), w_up, precision=highest_precision) + ffn_bias)
    active = low(jax.nn.gelu(upward, approximate=True))
    ffn_out = low_back(jnp.einsum('tf,df->td', active, w_down, precision=highest_precision) + offsets[3])
    return norm_rows(hidden + ffn_out, gains[1], offsets[1])

def reference(x_in, out_cot, seg_ids, land_doc, w_qkv, w_out, w_up, w_down, conv_taps, head_bias, ffn_bias, gains, offsets):
    params = tuple((weight.astype(jnp.float32) for weight in (w_qkv, w_out, w_up, w_down, conv_taps, head_bias, ffn_bias, gains, offsets)))

    def one_sequence(running, batch_item):
        tokens, cotangent, token_docs, land_ids = batch_item

        def forward(inputs, *weights):
            return layer(inputs, token_docs, land_ids, *weights)
        output, pullback = jax.vjp(forward, tokens.astype(jnp.float32), *params)
        updates = pullback(cotangent.astype(jnp.float32))
        running = tuple((total_now + update for total_now, update in zip(running, updates[1:])))
        return (running, (output.astype(jnp.bfloat16), updates[0].astype(jnp.bfloat16)))
    starting = tuple((jnp.zeros(weight.shape, jnp.float32) for weight in params))
    summed, (outputs, input_grads) = lax.scan(one_sequence, starting, (x_in, out_cot, seg_ids, land_doc))
    return (outputs, input_grads, summed[0], summed[1], summed[2], summed[3], summed[4], summed[5], summed[6], summed[7], summed[8])
```

```python
import jax
import jax.numpy as jnp
from jax import lax
from jax.experimental import pallas as pl
from jax.experimental.pallas import tpu as pltpu
from jax.sharding import PartitionSpec as P

HEAD_DIM = 64
KW = 33
REACH = KW // 2
NEWTON = 6
EPS = 1e-05
SCALE = HEAD_DIM**-0.5
BLOCK = 256
PACK = BLOCK // HEAD_DIM
BF = jnp.bfloat16
F32 = jnp.float32
HI = lax.Precision.HIGHEST


def dot(spec, a, b):
    return jnp.einsum(spec, a, b, preferred_element_type=F32)


def hdot(spec, a, b):
    return jnp.einsum(spec, a, b, preferred_element_type=F32, precision=HI)


def swap(a, axis, mask):
    return lax.ppermute(a, axis, [(i, i ^ mask) for i in range(lax.axis_size(axis))])


def grow(a, bit):
    return jnp.concatenate([a, swap(a, *bit)], axis=0)


def shrink(a, bit):
    half = a.shape[0] // 2
    got = swap(a[half:], *bit)
    return (a[:half].astype(F32) + got.astype(F32)).astype(a.dtype)


def nn(a, b):
    return lax.dot_general(a, b, (((1,), (0,)), ((), ())), preferred_element_type=F32)


def nt(a, b):
    return lax.dot_general(a, b, (((1,), (1,)), ((), ())), preferred_element_type=F32)


def tn(a, b):
    return lax.dot_general(a, b, (((0,), (0,)), ((), ())), preferred_element_type=F32)


def lane_head(rows):
    return lax.broadcasted_iota(jnp.int32, (rows, BLOCK), 1) // HEAD_DIM


def expand(r):
    head = lane_head(HEAD_DIM)
    wide = r.astype(F32)
    return jnp.concatenate([jnp.where(head == i, wide, 0.0) for i in range(PACK)], 0).astype(r.dtype)


def compress(full):
    head = lane_head(HEAD_DIM)
    out = jnp.zeros((HEAD_DIM, BLOCK), F32)
    for i in range(PACK):
        out = jnp.where(head == i, full[i * HEAD_DIM : (i + 1) * HEAD_DIM], out)
    return out


def split(a):
    high = a.astype(BF)
    return high, (a - high.astype(F32)).astype(BF)


def mm3(a, b):
    ah, al = split(a)
    bh, bl = split(b)
    wide = expand(bh)
    return nn(ah, wide) + nn(al, wide) + nn(ah, expand(bl))


def tn3(a, b):
    ah, al = split(a)
    bh, bl = split(b)
    return compress(tn(ah, bh) + tn(al, bh) + tn(ah, bl))


def eye_row():
    row = lax.broadcasted_iota(jnp.int32, (HEAD_DIM, BLOCK), 0)
    lane = lax.broadcasted_iota(jnp.int32, (HEAD_DIM, BLOCK), 1)
    return jnp.where(row == lane % HEAD_DIM, 1.0, 0.0)


def head_total(a):
    head = lane_head(1)
    col = jnp.sum(a, axis=0, keepdims=True)
    out = jnp.zeros_like(col)
    for i in range(PACK):
        one = jnp.sum(jnp.where(head == i, col, 0.0), axis=1, keepdims=True)
        out = jnp.where(head == i, one, out)
    return out


def heads_sum(a):
    parts = a.reshape(PACK, HEAD_DIM, a.shape[1])
    return jnp.broadcast_to(jnp.sum(parts, axis=1, keepdims=True), parts.shape).reshape(a.shape)


def heads_max(a):
    parts = a.reshape(PACK, HEAD_DIM, a.shape[1])
    return jnp.broadcast_to(jnp.max(parts, axis=1, keepdims=True), parts.shape).reshape(a.shape)


def tall(mask):
    return jnp.concatenate([mask] * PACK, 0) > 0.5


def group(g):
    return slice(g * BLOCK, (g + 1) * BLOCK)


def scores_body(q_ref, k_ref, v_ref, land_ref, mask_ref, ktok_ref, ekey_ref, pack_ref):
    E = q_ref.shape[1]
    allowed = tall(mask_ref[...])
    lane = lax.broadcasted_iota(jnp.int32, (HEAD_DIM, 128), 1)
    stats = jnp.zeros((HEAD_DIM, 128), F32)
    heads = E // HEAD_DIM
    for g in range(E // BLOCK):
        s = group(g)
        lq, lk = land_ref[:, s], land_ref[:, E + g * BLOCK : E + (g + 1) * BLOCK]
        z = nt(expand(lk), q_ref[:, s]) * SCALE
        z = jnp.where(allowed, z, -1e30)
        e = jnp.where(allowed, jnp.exp(z - heads_max(z)), 0.0)
        ktok_ref[s, :] = (e / heads_sum(e)).astype(BF)
        z = nt(expand(lq), k_ref[:, s]) * SCALE
        z = jnp.where(allowed, z, -1e30)
        top = jnp.max(z, axis=1, keepdims=True)
        e = jnp.where(allowed, jnp.exp(z - top), 0.0)
        total = jnp.sum(e, axis=1, keepdims=True)
        low = e.astype(BF)
        ekey_ref[s, :] = low
        pack_ref[:, s] = compress(nn(low, v_ref[:, s])).astype(BF)
        for i in range(PACK):
            h = g * PACK + i
            rows = slice(i * HEAD_DIM, (i + 1) * HEAD_DIM)
            stats = jnp.where(lane == h, top[rows], stats)
            stats = jnp.where(lane == heads + h, total[rows], stats)
    first = stats.astype(BF).astype(F32)
    second = (stats - first).astype(BF).astype(F32)
    third = stats - first - second
    pack_ref[:, E:] = (first + pltpu.roll(second, 2 * heads, 1) + pltpu.roll(third, 4 * heads, 1)).astype(BF)


def newton_body(land_ref, lmask_ref, kt_ref, mixer_ref, p_ref, w_ref, pi_ref):
    E = kt_ref.shape[1]
    eye = eye_row()
    allowed = jnp.concatenate([lmask_ref[...]] * PACK, 1) > 0.5
    for g in range(E // BLOCK):
        s = group(g)
        lq, lk = land_ref[:, s], land_ref[:, E + g * BLOCK : E + (g + 1) * BLOCK]
        z = nt(lk, expand(lq)) * SCALE
        z = jnp.where(allowed, z, -1e30)
        e = jnp.where(allowed, jnp.exp(z - jnp.max(z, axis=0, keepdims=True)), 0.0)
        kt = e / jnp.sum(e, axis=0, keepdims=True)
        inv = 1.0 / head_total(kt * kt)
        kt_ref[:, s] = kt
        p = tn3(kt, kt) * inv
        pi = None
        for step in range(NEWTON):
            p_ref[step, :, s] = p
            p2 = mm3(p, p)
            w = 0.25 * (13.0 * eye - 15.0 * p + mm3(p2, 7.0 * eye - p))
            w_ref[step, :, s] = w
            if step < NEWTON - 1:
                p = mm3(p, w)
            pi = w if pi is None else mm3(pi, w)
            pi_ref[step, :, s] = pi
        mixer_ref[:, s] = mm3(kt, pi) * inv


def newton_back_body(land_ref, kt_ref, p_ref, w_ref, pi_ref, mixer_ref, gmix_ref, lval_ref, lq_ref, lk_ref):
    E = kt_ref.shape[1]
    for g in range(E // BLOCK):
        s = group(g)
        lq, lk = land_ref[:, s], land_ref[:, E + g * BLOCK : E + (g + 1) * BLOCK]
        kt = kt_ref[:, s]
        inv = 1.0 / head_total(kt * kt)
        gh, gl = split(gmix_ref[:, s])
        vh, vl = split(lval_ref[:, s])
        wide = expand(vh)
        grad = nt(gh, wide) + nt(gl, wide) + nt(gh, expand(vl))
        d_pi = tn3(kt, grad) * inv
        d_kt = mm3(grad, pi_ref[NEWTON - 1, :, s]) * inv
        d_c = -head_total(grad * mixer_ref[:, s]) * inv
        d_p = None
        for step in reversed(range(NEWTON)):
            p, w = p_ref[step, :, s], w_ref[step, :, s]
            d_w = d_pi if step == 0 else mm3(pi_ref[step - 1, :, s], d_pi)
            if d_p is not None:
                d_w = d_w + mm3(p, d_p)
                d_p = mm3(d_p, w)
            if step > 0:
                d_pi = mm3(d_pi, w)
            a = mm3(p, d_w)
            ab = a + mm3(d_w, p)
            more = 0.25 * (7.0 * ab - 15.0 * d_w - mm3(p, a) - mm3(ab, p))
            d_p = more if d_p is None else d_p + more
        d_c = d_c - head_total(d_p * p_ref[0, :, s]) * inv
        d_s = d_p * inv
        kh, kl = split(kt)
        sh, sl = split(d_s)
        wide = expand(sh)
        thin = expand(sl)
        d_kt = d_kt + nn(kh, wide) + nn(kl, wide) + nn(kh, thin) + nt(kh, wide) + nt(kl, wide) + nt(kh, thin)
        d_kt = d_kt + 2.0 * d_c * kt
        dz = kt * (d_kt - jnp.sum(kt * d_kt, axis=0, keepdims=True)) * SCALE
        zh, zl = split(dz)
        wide = expand(lq)
        lk_ref[:, s] = nn(zh, wide) + nn(zl, wide)
        lq_ref[:, s] = compress(tn(zh, lk) + tn(zl, lk))


def mix_body(*refs):
    n = len(refs) - 7
    packs = refs[:n]
    mixer_ref, ktok_ref, conv_ref, mixing_ref, lval_ref, scale_ref, mixed_ref = refs[n:]
    E = mixer_ref.shape[1]
    heads = E // HEAD_DIM
    stats = []
    for p in packs:
        tile = p[:, E:].astype(F32)
        stats.append(tile + pltpu.roll(tile, 128 - 2 * heads, 1) + pltpu.roll(tile, 128 - 4 * heads, 1))
    top = stats[0]
    for t in stats[1:]:
        top = jnp.maximum(top, t)
    lane = lax.broadcasted_iota(jnp.int32, (HEAD_DIM, 128), 1)
    weights = [jnp.where(lane < heads, jnp.exp(jnp.minimum(t - top, 0.0)), 0.0) for t in stats]
    total = sum(w * pltpu.roll(t, 128 - heads, 1) for w, t in zip(weights, stats))
    total = jnp.where(lane < heads, total, 1.0)
    weights = [w / total for w in weights]
    scale_ref[...] = weights[0]
    head = lane_head(HEAD_DIM)
    for g in range(E // BLOCK):
        s = group(g)
        lval = jnp.zeros((HEAD_DIM, BLOCK), F32)
        for w, p in zip(weights, packs):
            spread = jnp.zeros((HEAD_DIM, BLOCK), F32)
            for i in range(PACK):
                h = g * PACK + i
                spread = jnp.where(head == i, w[:, h : h + 1], spread)
            lval = lval + spread * p[:, s].astype(F32)
        lval_ref[:, s] = lval
        mixing = mm3(mixer_ref[:, s], lval)
        mixing_ref[:, s] = mixing
        mh, ml = split(mixing)
        tok = ktok_ref[s, :]
        mixed_ref[:, s] = (tn(tok, expand(mh)) + tn(tok, expand(ml)) + conv_ref[:, s]).astype(BF)


def pair_pick(first, second):
    lane = lax.broadcasted_iota(jnp.int32, first.shape, 1)
    return jnp.where(lane < HEAD_DIM, first, second)


def band_apply(row, band, edge, a_ref, rim_ref, cols):
    T = a_ref.shape[0]
    wide = pltpu.roll(jnp.broadcast_to(row, (T, T)), 0, 1, stride=1, stride_axis=0)
    wide = jnp.where(band, wide, 0.0).astype(BF)
    short = jnp.broadcast_to(row, (REACH, T))
    rims = jnp.concatenate(
        [
            pltpu.roll(short, REACH, 1, stride=1, stride_axis=0),
            pltpu.roll(short, 0, 1, stride=1, stride_axis=0),
        ],
        0,
    )[:, :128]
    rims = jnp.where(edge, rims, 0.0).astype(BF)
    return nn(wide, a_ref[:, cols]), nn(rims, rim_ref[:, cols])


def conv_pair(rows_ref, band, edge, a_ref, rim_ref, out_ref, j):
    T = a_ref.shape[0]
    cols = slice(j * 128, (j + 1) * 128)
    one, one_rim = band_apply(rows_ref[2 * j : 2 * j + 1, :], band, edge, a_ref, rim_ref, cols)
    two, two_rim = band_apply(rows_ref[2 * j + 1 : 2 * j + 2, :], band, edge, a_ref, rim_ref, cols)
    both, rim = pair_pick(one, two), pair_pick(one_rim, two_rim)
    out_ref[:REACH, cols] = both[:REACH] + rim[:REACH]
    out_ref[REACH : T - REACH, cols] = both[REACH : T - REACH]
    out_ref[T - REACH :, cols] = both[T - REACH :] + rim[REACH:]


def conv_body(rows_ref, band_ref, edge_ref, v_ref, rim_ref, out_ref):
    band = band_ref[...] > 0.5
    edge = edge_ref[...] > 0.5
    for j in range(v_ref.shape[1] // 128):
        conv_pair(rows_ref, band, edge, v_ref, rim_ref, out_ref, j)


def conv_back_body(
    rows_ref, band_ref, edge_ref, band_rev_ref, edge_rev_ref, g_ref, g_rim_ref, v_ref, v_rim_ref, out_ref, tap_ref, tap_before_ref, tap_after_ref
):
    T = g_ref.shape[0]
    band = band_ref[...] > 0.5
    edge = edge_ref[...] > 0.5
    band_rev = band_rev_ref[...] > 0.5
    edge_rev = edge_rev_ref[...] > 0.5
    a = lax.broadcasted_iota(jnp.int32, (T, T), 0)
    b = lax.broadcasted_iota(jnp.int32, (T, T), 1)
    flip = jnp.where(a + b == T - 1, 1.0, 0.0).astype(BF)
    a = lax.broadcasted_iota(jnp.int32, (128, 128), 0)
    b = lax.broadcasted_iota(jnp.int32, (128, 128), 1)
    flip_before = jnp.where(a + b == REACH - 1, 1.0, 0.0).astype(BF)
    flip_after = jnp.where((a + b == 2 * REACH - 1) & (a < REACH), 1.0, 0.0).astype(BF)
    for j in range(g_ref.shape[1] // 128):
        cols = slice(j * 128, (j + 1) * 128)
        conv_pair(rows_ref, band, edge, g_ref, g_rim_ref, out_ref, j)
        v_rev = nn(flip, v_ref[:, cols]).astype(BF)
        before = nn(flip_before, v_rim_ref[:, cols]).astype(BF)
        after = nn(flip_after, v_rim_ref[:, cols]).astype(BF)
        g = g_ref[:, cols].astype(F32)
        lane = lax.broadcasted_iota(jnp.int32, g.shape, 1)
        for i in range(2):
            mine = jnp.where((lane < HEAD_DIM) == (i == 0), g, 0.0).astype(BF)
            h = 2 * j + i
            cross = jnp.where(band_rev, nt(mine, v_rev), 0.0)
            cross = pltpu.roll(cross, 0, 1, stride=1, stride_axis=0)
            tap_ref[h : h + 1, :] = jnp.sum(cross, axis=0, keepdims=True)
            low = jnp.where(edge_rev[:REACH], nt(mine[:REACH], before), 0.0)
            low = pltpu.roll(low, 0, 1, stride=1, stride_axis=0)
            tap_before_ref[h : h + 1, :] = jnp.sum(low, axis=0, keepdims=True)
            high = jnp.where(edge_rev[REACH:], nt(mine[T - REACH :], after), 0.0)
            high = pltpu.roll(high, 0, 1, stride=1, stride_axis=0)
            tap_after_ref[h : h + 1, :] = jnp.sum(high, axis=0, keepdims=True)


def gmix_body(ktok_ref, gm_ref, out_ref):
    for g in range(gm_ref.shape[1] // BLOCK):
        s = group(g)
        out_ref[:, s] = compress(nn(ktok_ref[s, :], gm_ref[:, s])).astype(BF)


def tok_back_body(ktok_ref, mixing_ref, gm_ref, q_ref, land_ref, gq_ref, lk_ref):
    E = gm_ref.shape[1]
    for g in range(E // BLOCK):
        s = group(g)
        lk = land_ref[:, E + g * BLOCK : E + (g + 1) * BLOCK]
        mh, ml = split(mixing_ref[:, s])
        gm = gm_ref[:, s]
        gk = nt(expand(mh), gm) + nt(expand(ml), gm)
        tok = ktok_ref[s, :].astype(F32)
        gz = (tok * (gk - heads_sum(tok * gk)) * SCALE).astype(BF)
        gq_ref[:, s] = tn(gz, expand(lk))
        lk_ref[:, s] = compress(nn(gz, q_ref[:, s]))


def key_back_body(*refs):
    n = len(refs) - 12
    gmixes = refs[:n]
    mixer_ref, lval_ref, ekey_ref, scale_ref, v_ref, k_ref, land_ref, gvc_ref, gmix_ref, gv_ref, gk_ref, lq_ref = refs[n:]
    E = v_ref.shape[1]
    for g in range(E // BLOCK):
        s = group(g)
        gmix = gmixes[0][:, s].astype(F32)
        for other in gmixes[1:]:
            gmix = gmix + other[:, s].astype(F32)
        gmix_ref[:, s] = gmix
        lval = lval_ref[:, s]
        glval = tn3(mixer_ref[:, s], gmix)
        gh, gl = split(glval)
        wide = expand(gh)
        v = v_ref[:, s]
        gkk = nt(wide, v) + nt(expand(gl), v)
        center = jnp.sum(expand(glval * lval), axis=1, keepdims=True)
        scale = jnp.concatenate([scale_ref[:, g * PACK + i : g * PACK + i + 1] for i in range(PACK)], 0)
        kk = ekey_ref[s, :].astype(F32) * scale
        gz = (kk * (gkk - center) * SCALE).astype(BF)
        gv_ref[:, s] = (tn(kk.astype(BF), wide) + gvc_ref[:, s]).astype(BF)
        gk_ref[:, s] = tn(gz, expand(land_ref[:, s]))
        lq_ref[:, s] = compress(nn(gz, k_ref[:, s]))


def call(body, outs, *args, flops=2e9):
    shapes = [jax.ShapeDtypeStruct(*o) for o in outs]
    size = sum(a.size * a.dtype.itemsize for a in args) + sum(a.size * a.dtype.itemsize for a in shapes)
    return pl.pallas_call(
        body,
        out_shape=shapes,
        compiler_params=pltpu.CompilerParams(vmem_limit_bytes=40 << 20),
        cost_estimate=pl.CostEstimate(flops=int(flops), bytes_accessed=size, transcendentals=0),
        name=body.__name__,
    )(*args)


def norm_rows(rows, gain, shift):
    center = rows - jnp.mean(rows, axis=-1, keepdims=True)
    spread = jnp.mean(center * center, axis=-1, keepdims=True)
    return center * lax.rsqrt(spread + EPS) * gain + shift


def local(x_in, out_cot, seg_ids, land_doc, w_qkv, w_out, w_up, w_down, conv_taps, head_bias, ffn_bias, gains, offsets):
    nf, nc, nt = lax.axis_size("fsdp"), lax.axis_size("ctx"), lax.axis_size("tp")
    f_i, c_i, t_i = lax.axis_index("fsdp"), lax.axis_index("ctx"), lax.axis_index("tp")
    assert nt == 2 and x_in.shape[0] == 2
    ctx_bits = [("ctx", 1 << b) for b in range(nc.bit_length() - 1)]
    chip_bits = [("fsdp", 1 << b) for b in range(1, nf.bit_length() - 1)]
    core_bits = [("fsdp", 1)]
    row_bits = ctx_bits + chip_bits + core_bits
    T, D = x_in.shape[1:]
    R = w_qkv.shape[0]
    C = w_qkv.shape[2]
    FL = w_up.shape[1]
    HL = C // HEAD_DIM
    H = 2 * HL
    LL = land_doc.shape[1]
    L = LL * nc
    seg_len = T // LL

    q_pos = jnp.arange(D, dtype=jnp.int32)
    piece, inner = q_pos // R, q_pos % R
    mf = jnp.zeros_like(piece)
    mc = jnp.zeros_like(piece)
    for i, (axis, mask) in enumerate(row_bits):
        bit = ((piece >> i) & 1) * mask
        if axis == "fsdp":
            mf = mf ^ bit
        else:
            mc = mc ^ bit
    true_pos = ((f_i ^ mf) * nc + (c_i ^ mc)) * R + inner
    perm = (jnp.arange(D, dtype=jnp.int32)[:, None] == true_pos[None, :]).astype(BF)

    def pick(a):
        return lax.dynamic_index_in_dim(a, t_i, 0, False)

    seg = pick(seg_ids)
    doc = pick(land_doc)
    x = dot("td,dq->tq", pick(x_in), perm).astype(BF)
    cot = dot("td,dq->tq", pick(out_cot), perm).astype(BF)
    vec = hdot("vd,dq->vq", jnp.concatenate([gains, offsets], 0), perm.astype(F32))
    gain = vec[:2]
    shift = vec[2:]

    up = [(i, i + 1) for i in range(nc - 1)]
    down = [(i + 1, i) for i in range(nc - 1)]
    seg_before = jnp.where(c_i == 0, -1, lax.ppermute(seg[T - REACH :], "ctx", up))
    seg_after = jnp.where(c_i == nc - 1, -1, lax.ppermute(seg[:REACH], "ctx", down))
    docs = doc[None]
    for bit in ctx_bits:
        docs = grow(docs, bit)
    l_pos = jnp.arange(L, dtype=jnp.int32)
    l_true = (c_i ^ (l_pos // LL)) * LL + l_pos % LL
    l_perm = l_pos[:, None] == l_true[None, :]
    docs = jnp.sum(jnp.where(l_perm, docs.reshape(1, L), 0), axis=1)
    par = jnp.concatenate([conv_taps.reshape(-1), head_bias.reshape(-1), ffn_bias.reshape(-1)])
    par2 = jnp.stack([par, swap(par, "tp", 1)])
    taps = par2[:, : KW * HL].reshape(2, KW, HL).transpose(1, 0, 2).reshape(KW, H)
    hb = par2[:, KW * HL : KW * HL + 2 * C].reshape(2, 2, C).transpose(1, 0, 2).reshape(2, 2 * C)
    fb = par2[:, KW * HL + 2 * C :].reshape(2 * FL)

    def gather(pack):
        for bit in ctx_bits:
            pack = grow(pack, bit)
        half = pack.shape[1] // 2
        one, two = pack[:, :half], pack[:, half:]
        for bit in chip_bits:
            one = grow(one, bit)
        one = jnp.concatenate([one, swap(one, "tp", 1)], axis=1)
        two = jnp.concatenate([two, swap(two, "tp", 1)], axis=1)
        for bit in chip_bits:
            two = grow(two, bit)
        return grow(one, core_bits[0]), grow(two, core_bits[0])

    w1, w2 = gather(jnp.concatenate([w_qkv.reshape(R, 3 * C), w_out], axis=1))
    wu, wd = gather(jnp.concatenate([w_up, w_down], axis=1))
    wq = jnp.concatenate([w1[:, :C], w1[:, 2 * C : 3 * C]], 1)
    wk = jnp.concatenate([w1[:, C : 2 * C], w1[:, 3 * C :]], 1)
    wv = jnp.concatenate([w2[:, :C], w2[:, 2 * C : 3 * C]], 1)
    wo = jnp.concatenate([w2[:, C : 2 * C], w2[:, 3 * C :]], 1)

    q = (dot("td,de->te", x, wq) + hb[0]).astype(BF)
    k = dot("td,de->te", x, wk).astype(BF)
    v = (dot("td,de->te", x, wv) + hb[1]).astype(BF)
    E = q.shape[1]
    mean_mat = (jnp.arange(T)[:, None] // seg_len == jnp.arange(LL)[None, :]).astype(BF) / seg_len
    piece0 = jnp.concatenate([dot("ta,te->ae", mean_mat, q), dot("ta,te->ae", mean_mat, k)], 1).astype(BF)

    def rims(a):
        before = lax.ppermute(a[T - REACH :], "ctx", up)
        after = lax.ppermute(a[:REACH], "ctx", down)
        return jnp.concatenate([before, after, jnp.zeros((128 - 2 * REACH, a.shape[1]), a.dtype)], 0)

    pieces = [piece0] + [swap(piece0, "ctx", p) for p in range(1, nc)]
    land = jnp.concatenate(
        [sum(jnp.where((c_i ^ p) == a, pieces[p], 0) for p in range(nc)) for a in range(nc)], 0
    ).astype(BF)
    mask = (docs[:, None] == seg[None, :]).astype(F32)
    lmask = (docs[:, None] == docs[None, :]).astype(F32)
    ktok, ekey, pack = call(scores_body, [((E, T), BF), ((E, T), BF), ((L, E + 128), BF)], q, k, v, land, mask)
    packs = [pack] + [swap(pack, "ctx", p) for p in range(1, nc)]
    v_rim = rims(v)
    kt, mixer, p_all, w_all, pi_all = call(
        newton_body,
        [((L, E), F32), ((L, E), F32)] + [((NEWTON, L, E), F32)] * 3,
        land,
        lmask,
    )

    t_pos = jnp.arange(T)
    diff = t_pos[None, :] - t_pos[:, None]
    band = ((jnp.abs(diff) <= REACH) & (seg[None, :] == seg[:, None])).astype(F32)
    r_pos = jnp.arange(REACH)
    edge_before = (r_pos[None, :] >= r_pos[:, None]) & (seg_before[None, :] == seg[:REACH, None])
    edge_after = (r_pos[None, :] <= r_pos[:, None]) & (seg_after[None, :] == seg[T - REACH :, None])
    none = jnp.zeros((REACH, REACH), bool)
    zero = jnp.zeros((2 * REACH, 128 - 2 * REACH), F32)
    edge = jnp.concatenate(
        [jnp.concatenate([jnp.concatenate([edge_before, none], 1), jnp.concatenate([none, edge_after], 1)], 0).astype(F32), zero], 1
    )
    gap = jnp.zeros((H, T - KW), F32)
    tap_t = taps.T
    row_fwd = jnp.concatenate([tap_t[:, REACH:], gap, tap_t[:, :REACH]], 1)
    tap_r = tap_t[:, ::-1]
    row_back = jnp.concatenate([tap_r[:, REACH:], gap, tap_r[:, :REACH]], 1)
    (conv,) = call(conv_body, [((T, E), F32)], row_fwd, band, edge, v, v_rim)
    mixing, lval, land_scale, mixed = call(
        mix_body, [((L, E), F32), ((L, E), F32), ((L, 128), F32), ((T, E), BF)], *packs, mixer, ktok, conv
    )

    branch = dot("te,de->td", mixed, wo) + shift[2]
    hidden, pull_first = jax.vjp(norm_rows, x.astype(F32) + branch, gain[0], shift[0])
    hidden_low = hidden.astype(BF)
    upward = dot("td,df->tf", hidden_low, wu) + fb
    active, gelu_pull = jax.vjp(lambda u: jax.nn.gelu(u, approximate=True), upward)
    active_low = active.astype(BF)
    ffn = dot("tf,df->td", active_low, wd) + shift[3]
    output, pull_second = jax.vjp(norm_rows, hidden + ffn, gain[1], shift[1])
    grad_second, gain_second, shift_second = pull_second(cot.astype(F32))
    grad_ffn = grad_second.astype(BF)
    d_down = dot("td,tf->df", grad_ffn, active_low).astype(BF)
    grad_up = gelu_pull(dot("td,df->tf", grad_ffn, wd))[0].astype(BF)
    d_up = dot("td,tf->df", hidden_low, grad_up).astype(BF)
    grad_hidden = dot("tf,df->td", grad_up, wu) + grad_second
    grad_first, gain_first, shift_first = pull_first(grad_hidden)
    grad_branch = grad_first.astype(BF)
    d_out = dot("td,te->de", grad_branch, mixed).astype(BF)
    gm = dot("td,de->te", grad_branch, wo).astype(BF)

    def scatter(one, two):
        one = shrink(one, core_bits[0])
        two = shrink(two, core_bits[0])

        def fold(a):
            half = a.shape[1] // 2
            return (a[:, :half].astype(F32) + swap(a[:, half:], "tp", 1).astype(F32)).astype(BF)

        one = fold(one)
        for bit in reversed(chip_bits):
            one = shrink(one, bit)
        for bit in reversed(chip_bits):
            two = shrink(two, bit)
        two = fold(two)
        both = jnp.concatenate([one, two], 1)
        for bit in reversed(ctx_bits):
            both = shrink(both, bit)
        return both.astype(F32)

    ud = scatter(d_up, d_down)

    (gmix0,) = call(gmix_body, [((L, E), BF)], ktok, gm)
    gmixes = [gmix0] + [swap(gmix0, "ctx", p) for p in range(1, nc)]
    gm_rim = rims(gm)
    gq, lk_part = call(tok_back_body, [((T, E), F32), ((L, E), F32)], ktok, mixing, gm, q, land)
    band_rev = band[:, ::-1]
    zero = jnp.zeros((REACH, 128 - REACH), F32)
    edge_rev = jnp.concatenate(
        [jnp.concatenate([edge_before[:, ::-1].astype(F32), zero], 1), jnp.concatenate([edge_after[:, ::-1].astype(F32), zero], 1)], 0
    )
    gvc, tap_main, tap_before, tap_after = call(
        conv_back_body,
        [((T, E), F32), ((H, T), F32), ((H, 128), F32), ((H, 128), F32)],
        row_back, band, edge, band_rev, edge_rev, gm, gm_rim, v, v_rim,
    )
    tap_grad = jnp.concatenate([tap_main[:, REACH - 1 :: -1], tap_main[:, : T - REACH - 2 : -1]], 1)
    tap_grad = tap_grad + jnp.concatenate([tap_before[:, REACH - 1 :: -1], tap_after[:, 2 * REACH - 1 : REACH - 2 : -1]], 1)
    tap_grad = tap_grad.T
    gmix, gv, gk, lq_part = call(
        key_back_body, [((L, E), F32), ((T, E), BF), ((T, E), F32), ((L, E), F32)],
        *gmixes, mixer, lval, ekey, land_scale, v, k, land, gvc,
    )
    lq_mix, lk_mix = call(
        newton_back_body, [((L, E), F32), ((L, E), F32)], land, kt, p_all, w_all, pi_all, mixer, gmix, lval
    )
    part = jnp.concatenate([lq_part, lk_part], 1).reshape(nc, LL, 2 * E)
    lmix = jnp.concatenate([lq_mix, lk_mix], 1).reshape(nc, LL, 2 * E)

    def piece_of(a, p):
        return lax.dynamic_index_in_dim(a, c_i ^ p, 0, False)

    own = piece_of(part, 0) + piece_of(lmix, 0)
    for p in range(1, nc):
        own = own + swap(piece_of(part, p).astype(BF), "ctx", p).astype(F32)
    spread = jnp.repeat(own / seg_len, seg_len, axis=0)
    gq = (gq + spread[:, :E]).astype(BF)
    gk = (gk + spread[:, E:]).astype(BF)
    d_q = dot("td,te->de", x, gq).astype(BF)
    d_k = dot("td,te->de", x, gk).astype(BF)
    d_v = dot("td,te->de", x, gv).astype(BF)
    d1 = jnp.concatenate([d_q[:, :C], d_k[:, :C], d_q[:, C:], d_k[:, C:]], 1)
    d2 = jnp.concatenate([d_v[:, :C], d_out[:, :C], d_v[:, C:], d_out[:, C:]], 1)
    qo = scatter(d1, d2)
    gx = dot("te,de->td", gq, wq) + dot("te,de->td", gk, wk) + dot("te,de->td", gv, wv) + grad_first

    hb_grad = jnp.stack([jnp.sum(gq.astype(F32), 0), jnp.sum(gv.astype(F32), 0)])
    fb_grad = jnp.sum(grad_up.astype(F32), 0)
    vec_grad = jnp.stack(
        [gain_first, gain_second, shift_first, shift_second, jnp.sum(grad_branch.astype(F32), 0), jnp.sum(grad_ffn.astype(F32), 0)]
    )
    vec_grad = hdot("vq,dq->vd", vec_grad, perm.astype(F32)).reshape(-1)

    def side(s):
        return jnp.concatenate(
            [tap_grad[:, s * HL : (s + 1) * HL].reshape(-1), hb_grad[:, s * C : (s + 1) * C].reshape(-1), fb_grad[s * FL : (s + 1) * FL]]
        )

    small = jnp.concatenate([side(0), vec_grad])
    small = small + swap(jnp.concatenate([side(1), vec_grad]), "tp", 1)
    for bit in row_bits:
        small = small + swap(small, *bit)
    n0, n1, n2 = KW * HL, KW * HL + 2 * C, KW * HL + 2 * C + FL
    vec_sum = small[n2:].reshape(6, D)

    def place(rows):
        mine = dot("tq,dq->td", rows.astype(BF), perm).astype(BF)
        other = swap(mine, "tp", 1)
        first = t_i == 0
        return jnp.stack([jnp.where(first, mine, other), jnp.where(first, other, mine)])

    return (
        place(output),
        place(gx),
        qo[:, : 3 * C].reshape(R, 3, C),
        qo[:, 3 * C :],
        ud[:, :FL],
        ud[:, FL:],
        small[:n0].reshape(KW, HL),
        small[n0:n1].reshape(2, C),
        small[n1:n2],
        vec_sum[:2],
        vec_sum[2:],
    )


def solution(mesh):
    placed = (
        P("fsdp", "ctx", None),
        P("fsdp", "ctx", None),
        P("fsdp", "ctx"),
        P("fsdp", "ctx"),
        P(("fsdp", "ctx"), None, "tp"),
        P(("fsdp", "ctx"), "tp"),
        P(("fsdp", "ctx"), "tp"),
        P(("fsdp", "ctx"), "tp"),
        P(None, "tp"),
        P(None, "tp"),
        P("tp"),
        P(),
        P(),
    )
    return jax.shard_map(
        local,
        mesh=mesh,
        in_specs=placed,
        out_specs=placed[:2] + placed[4:],
        check_vma=False,
    )
```

```python
import functools

import jax
import jax.numpy as jnp
from jax import lax
from jax.experimental import pallas as pl
from jax.experimental.pallas import tpu as pltpu
from jax.sharding import PartitionSpec as P

HEAD_DIM = 64
KW = 33
REACH = KW // 2
NEWTON = 6
EPS = 1e-05
SCALE = HEAD_DIM**-0.5
BLOCK = 256
PACK = BLOCK // HEAD_DIM
META = 128
BF = jnp.bfloat16
F32 = jnp.float32
HI = lax.Precision.HIGHEST


def dot(spec, a, b):
    return jnp.einsum(spec, a, b, preferred_element_type=F32)


def hdot(spec, a, b):
    return jnp.einsum(spec, a, b, preferred_element_type=F32, precision=HI)


def swap(a, axis, mask):
    return lax.ppermute(a, axis, [(i, i ^ mask) for i in range(lax.axis_size(axis))])


def swap_both(a, mask):
    nf = lax.axis_size("fsdp")
    return lax.ppermute(a, ("fsdp", "tp"), [(2 * i + j, 2 * (i ^ mask) + (j ^ 1)) for i in range(nf) for j in range(2)])


def add(*terms):
    return sum(t.astype(F32) for t in terms).astype(BF)


def later(value, *after):
    return lax.optimization_barrier((value, after))[0]


def nn(a, b):
    return lax.dot_general(a, b, (((1,), (0,)), ((), ())), preferred_element_type=F32)


def nt(a, b):
    return lax.dot_general(a, b, (((1,), (1,)), ((), ())), preferred_element_type=F32)


def tn(a, b):
    return lax.dot_general(a, b, (((0,), (0,)), ((), ())), preferred_element_type=F32)


def lane_head(rows):
    return lax.broadcasted_iota(jnp.int32, (rows, BLOCK), 1) // HEAD_DIM


def expand(r):
    head = lane_head(HEAD_DIM)
    wide = r.astype(F32)
    return jnp.concatenate([jnp.where(head == i, wide, 0.0) for i in range(PACK)], 0).astype(r.dtype)


def compress(full):
    head = lane_head(HEAD_DIM)
    out = jnp.zeros((HEAD_DIM, BLOCK), F32)
    for i in range(PACK):
        out = jnp.where(head == i, full[i * HEAD_DIM : (i + 1) * HEAD_DIM], out)
    return out


def split(a):
    high = a.astype(BF)
    return high, (a - high.astype(F32)).astype(BF)


def mm3(a, b):
    ah, al = split(a)
    bh, bl = split(b)
    wide = expand(bh)
    return nn(ah, wide) + nn(al, wide) + nn(ah, expand(bl))


def tn3(a, b):
    ah, al = split(a)
    bh, bl = split(b)
    return compress(tn(ah, bh) + tn(al, bh) + tn(ah, bl))


def eye_row():
    row = lax.broadcasted_iota(jnp.int32, (HEAD_DIM, BLOCK), 0)
    lane = lax.broadcasted_iota(jnp.int32, (HEAD_DIM, BLOCK), 1)
    return jnp.where(row == lane % HEAD_DIM, 1.0, 0.0)


def head_total(a):
    head = lane_head(1)
    col = jnp.sum(a, axis=0, keepdims=True)
    out = jnp.zeros_like(col)
    for i in range(PACK):
        one = jnp.sum(jnp.where(head == i, col, 0.0), axis=1, keepdims=True)
        out = jnp.where(head == i, one, out)
    return out


def heads_sum(a):
    parts = a.reshape(PACK, HEAD_DIM, a.shape[1])
    return jnp.broadcast_to(jnp.sum(parts, axis=1, keepdims=True), parts.shape).reshape(a.shape)


def heads_max(a):
    parts = a.reshape(PACK, HEAD_DIM, a.shape[1])
    return jnp.broadcast_to(jnp.max(parts, axis=1, keepdims=True), parts.shape).reshape(a.shape)


def tall(mask):
    return jnp.concatenate([mask] * PACK, 0) > 0.5


def group(g):
    return slice(g * BLOCK, (g + 1) * BLOCK)


def as_row(col, lanes, shift=0, flip=False):
    n = col.shape[0]
    row = lax.broadcasted_iota(jnp.int32, (n, lanes), 0)
    lane = lax.broadcasted_iota(jnp.int32, (n, lanes), 1) - shift
    hit = (row + lane == n - 1) if flip else (row == lane)
    return jnp.sum(jnp.where(hit, col, 0.0), axis=0, keepdims=True)


def rows_at(ref, index, count):
    return ref[pl.ds(pl.multiple_of(index * count, count), count), :]


def call(body, outs, *args, us=2.0, raw_in=(), raw_out=(), far_in=(), far_out=(), smem=(), scratch=(), mem=8, name=None):
    n, m = len(args), len(outs)
    far_in, far_out = list(far_in), list(far_out)

    def space(outside):
        return pltpu.HBM if outside else pltpu.VMEM

    ins = [space(i in raw_in or i in far_in) for i in range(n)]
    res = [space(i in raw_out or i in far_out) for i in range(m)]

    def inner(*refs):
        given, made, extra = list(refs[:n]), list(refs[n : n + m]), refs[n + m :]
        vm_in, extra = extra[: len(far_in)], extra[len(far_in) :]
        vm_out, extra = extra[: len(far_out)], extra[len(far_out) :]
        sem_in, sem_out, rest = extra[0], extra[1], extra[2:]
        loads = [pltpu.make_async_copy(given[i], v, sem_in.at[j]) for j, (i, v) in enumerate(zip(far_in, vm_in))]
        stores = [pltpu.make_async_copy(v, made[i], sem_out.at[j]) for j, (i, v) in enumerate(zip(far_out, vm_out))]
        for c in loads:
            c.start()
        for i, v in zip(far_in, vm_in):
            given[i] = v
        for i, v in zip(far_out, vm_out):
            made[i] = v

        def ready():
            for c in loads:
                c.wait()

        body(ready, *given, *made, *rest)
        for c in stores:
            c.start()
        for c in stores:
            c.wait()

    return pl.pallas_call(
        inner,
        out_shape=[r(*o) for r, o in zip(res, outs)],
        in_specs=[pl.BlockSpec(memory_space=pltpu.SMEM if i in smem else ins[i]) for i in range(n)],
        out_specs=[pl.BlockSpec(memory_space=r) for r in res],
        scratch_shapes=[pltpu.VMEM(args[i].shape, args[i].dtype) for i in far_in]
        + [pltpu.VMEM(*outs[i]) for i in far_out]
        + [pltpu.SemaphoreType.DMA((max(len(far_in), 1),)), pltpu.SemaphoreType.DMA((max(len(far_out), 1),))]
        + list(scratch),
        compiler_params=pltpu.CompilerParams(vmem_limit_bytes=mem << 20),
        cost_estimate=pl.CostEstimate(flops=int(us * 1e7), bytes_accessed=1024, transcendentals=0),
        name=name or body.__name__,
    )(*[a if i in smem else pltpu.with_memory_space_constraint(a, ins[i]) for i, a in enumerate(args)])


def combine(plan, *arrays, near=True, far_in=()):
    shapes = [
        (arrays[parts[0][0][0]][parts[0][0][1]].shape[:-1], [arrays[p[0][0]][p[0][1]].shape[-1] for p in parts]) for parts in plan
    ]
    if not near:
        return [
            jnp.concatenate([add(*[arrays[i][at] for i, at in terms]) for terms in parts], -1) if len(parts) > 1
            else add(*[arrays[i][at] for i, at in parts[0]])
            for parts in plan
        ]

    def sum_body(ready, *refs):
        ready()
        ins, res = refs[: len(arrays)], refs[len(arrays) :]
        for parts, (_, widths), out in zip(plan, shapes, res):
            col = 0
            for terms, width in zip(parts, widths):
                total = sum(ins[i][at].astype(F32) for i, at in terms).astype(BF)
                out[..., col : col + width] = total
                col += width

    return call(sum_body, [(lead + (sum(w),), BF) for lead, w in shapes], *arrays, far_in=far_in, mem=16)


def simple(body):
    def run(ready, *refs):
        ready()
        body(*refs)

    run.__name__ = body.__name__
    return run


def proj_body(ready, x_ref, hb_ref, doc_ref, first_ref, last_ref, *refs):
    parts, refs = refs[:8], refs[8:]
    q_ref, k_ref, v_ref, qkv_hbm, piece_ref, vfirst_ref, vlast_ref, w_hbm, w_ref, sem, sem_w, sem_f = refs
    rows = parts[0].shape[0]
    loads = [
        pltpu.make_async_copy(parts[i], w_ref.at[i // 4, pl.ds((i % 4) * rows, rows)], sem.at[i]) for i in range(8)
    ]
    for c in loads:
        c.start()
    ready()
    T, D = x_ref.shape
    C = D // 2
    x = x_ref[...]
    LL = piece_ref.shape[0]
    seg_len = T // LL
    row = lax.broadcasted_iota(jnp.int32, (LL, T), 0)
    col = lax.broadcasted_iota(jnp.int32, (LL, T), 1)
    mean = jnp.where(col // seg_len == row, 1.0 / seg_len, 0.0).astype(BF)
    store = pltpu.make_async_copy(w_ref, w_hbm, sem_w)
    for c in loads:
        c.wait()
    store.start()
    for side in range(2):
        cols = slice(side * C, (side + 1) * C)
        q = (nn(x, w_ref[side, :, :C]) + hb_ref[0:1, cols]).astype(BF)
        k = nn(x, w_ref[side, :, C : 2 * C]).astype(BF)
        v = (nn(x, w_ref[side, :, 2 * C : 3 * C]) + hb_ref[1:2, cols]).astype(BF)
        q_ref[:, cols] = q
        k_ref[:, cols] = k
        v_ref[:, cols] = v
        vfirst_ref[:, cols] = v[:REACH]
        vlast_ref[:, cols] = v[T - REACH :]
        piece_ref[:, cols] = nn(mean, q).astype(BF)
        piece_ref[:, D + side * C : D + (side + 1) * C] = nn(mean, k).astype(BF)
    piece_ref[:, 2 * D :] = doc_ref[...]
    vfirst_ref[:, D:] = first_ref[...]
    vlast_ref[:, D:] = last_ref[...]
    extra = [pltpu.make_async_copy(r, qkv_hbm.at[i], sem_f.at[i]) for i, r in enumerate((q_ref, k_ref, v_ref))]
    for c in extra:
        c.start()
    for c in extra:
        c.wait()
    store.wait()


def scores_body(n, ready, where_ref, q_ref, k_ref, v_ref, seg_ref, *refs):
    pieces, (ktok_ref, ekey_ref, pack_ref, land_ref, land_far_ref) = refs[:n], refs[n:]
    ready()
    LL = pieces[0].shape[0]
    E = q_ref.shape[1]
    for p in range(n):
        at = pl.multiple_of((where_ref[1] ^ p) * LL, LL)
        land_ref[pl.ds(at, LL), :] = pieces[p][...]
    doc = land_ref[:, 2 * E : 2 * E + 1].astype(F32)
    land_far_ref[...] = land_ref[...]
    allowed = tall((doc == as_row(seg_ref[...], q_ref.shape[0])).astype(F32))
    lane = lax.broadcasted_iota(jnp.int32, (HEAD_DIM, META), 1)
    stats = jnp.zeros((HEAD_DIM, META), F32)
    heads = E // HEAD_DIM
    for g in range(E // BLOCK):
        s = group(g)
        lq, lk = land_ref[:, s], land_ref[:, E + g * BLOCK : E + (g + 1) * BLOCK]
        z = nt(expand(lk), q_ref[:, s]) * SCALE
        z = jnp.where(allowed, z, -1e30)
        e = jnp.where(allowed, jnp.exp(z - heads_max(z)), 0.0)
        ktok_ref[s, :] = (e / heads_sum(e)).astype(BF)
        z = nt(expand(lq), k_ref[:, s]) * SCALE
        z = jnp.where(allowed, z, -1e30)
        top = jnp.max(z, axis=1, keepdims=True)
        e = jnp.where(allowed, jnp.exp(z - top), 0.0)
        total = jnp.sum(e, axis=1, keepdims=True)
        low = e.astype(BF)
        ekey_ref[s, :] = low
        pack_ref[:, s] = compress(nn(low, v_ref[:, s])).astype(BF)
        for i in range(PACK):
            h = g * PACK + i
            rows = slice(i * HEAD_DIM, (i + 1) * HEAD_DIM)
            stats = jnp.where(lane == h, top[rows], stats)
            stats = jnp.where(lane == heads + h, total[rows], stats)
    first = stats.astype(BF).astype(F32)
    second = (stats - first).astype(BF).astype(F32)
    third = stats - first - second
    pack_ref[:, E:] = (first + pltpu.roll(second, 2 * heads, 1) + pltpu.roll(third, 4 * heads, 1)).astype(BF)


def newton_body(land_ref, kt_ref, mixer_ref, p_ref, w_ref, pi_ref):
    E = kt_ref.shape[1]
    eye = eye_row()
    doc = land_ref[:, 2 * E : 2 * E + 1].astype(F32)
    allowed = jnp.concatenate([(doc == as_row(doc, HEAD_DIM)).astype(F32)] * PACK, 1) > 0.5
    groups = [group(g) for g in range(E // BLOCK)]
    kts, invs, ps, pis = [], [], [], []
    for s in groups:
        lq, lk = land_ref[:, s], land_ref[:, E + s.start : E + s.stop]
        z = nt(lk, expand(lq)) * SCALE
        z = jnp.where(allowed, z, -1e30)
        e = jnp.where(allowed, jnp.exp(z - jnp.max(z, axis=0, keepdims=True)), 0.0)
        kt = e / jnp.sum(e, axis=0, keepdims=True)
        kts.append(kt)
        invs.append(1.0 / head_total(kt * kt))
        kt_ref[:, s] = kt
    ps = [tn3(kt, kt) * inv for kt, inv in zip(kts, invs)]
    for step in range(NEWTON):
        for s, p in zip(groups, ps):
            p_ref[step, :, s] = p
        p2s = [mm3(p, p) for p in ps]
        ws = [0.25 * (13.0 * eye - 15.0 * p + mm3(p2, 7.0 * eye - p)) for p, p2 in zip(ps, p2s)]
        if step < NEWTON - 1:
            ps = [mm3(p, w) for p, w in zip(ps, ws)]
        pis = [mm3(pi, w) for pi, w in zip(pis, ws)] if step else ws
        for s, w, pi in zip(groups, ws, pis):
            w_ref[step, :, s] = w
            pi_ref[step, :, s] = pi
    for s, kt, pi, inv in zip(groups, kts, pis, invs):
        mixer_ref[:, s] = mm3(kt, pi) * inv


def newton_back_body(land_ref, kt_ref, p_ref, w_ref, pi_ref, mixer_ref, gmix_ref, lval_ref, where_ref, own_ref, full_ref):
    E = kt_ref.shape[1]
    groups = [group(g) for g in range(E // BLOCK)]
    many = range(len(groups))
    kts = [kt_ref[:, s] for s in groups]
    invs = [1.0 / head_total(kt * kt) for kt in kts]
    grads = []
    for s in groups:
        gh, gl = split(gmix_ref[:, s])
        vh, vl = split(lval_ref[:, s])
        wide = expand(vh)
        grads.append(nt(gh, wide) + nt(gl, wide) + nt(gh, expand(vl)))
    d_pis = [tn3(kts[i], grads[i]) * invs[i] for i in many]
    d_kts = [mm3(grads[i], pi_ref[NEWTON - 1, :, groups[i]]) * invs[i] for i in many]
    d_cs = [-head_total(grads[i] * mixer_ref[:, groups[i]]) * invs[i] for i in many]
    d_ps = None
    for step in reversed(range(NEWTON)):
        ps = [p_ref[step, :, s] for s in groups]
        ws = [w_ref[step, :, s] for s in groups]
        d_ws = [mm3(pi_ref[step - 1, :, groups[i]], d_pis[i]) for i in many] if step else d_pis
        if d_ps is not None:
            d_ws = [d_ws[i] + mm3(ps[i], d_ps[i]) for i in many]
            d_ps = [mm3(d_ps[i], ws[i]) for i in many]
        if step:
            d_pis = [mm3(d_pis[i], ws[i]) for i in many]
        ones = [mm3(ps[i], d_ws[i]) for i in many]
        twos = [ones[i] + mm3(d_ws[i], ps[i]) for i in many]
        more = [
            0.25 * (7.0 * twos[i] - 15.0 * d_ws[i] - mm3(ps[i], ones[i]) - mm3(twos[i], ps[i])) for i in many
        ]
        d_ps = more if d_ps is None else [d_ps[i] + more[i] for i in many]
    for i in many:
        s, kt, inv = groups[i], kts[i], invs[i]
        lq, lk = land_ref[:, s], land_ref[:, E + s.start : E + s.stop]
        d_c = d_cs[i] - head_total(d_ps[i] * p_ref[0, :, s]) * inv
        kh, kl = split(kt)
        sh, sl = split(d_ps[i] * inv)
        wide = expand(sh)
        thin = expand(sl)
        d_kt = d_kts[i] + nn(kh, wide) + nn(kl, wide) + nn(kh, thin) + nt(kh, wide) + nt(kl, wide) + nt(kh, thin)
        d_kt = d_kt + 2.0 * d_c * kt
        dz = kt * (d_kt - jnp.sum(kt * d_kt, axis=0, keepdims=True)) * SCALE
        zh, zl = split(dz)
        wide = expand(lq)
        full_ref[:, E + s.start : E + s.stop] = nn(zh, wide) + nn(zl, wide)
        full_ref[:, s] = compress(tn(zh, lk) + tn(zl, lk))
    own_ref[...] = rows_at(full_ref, where_ref[1], own_ref.shape[0])


def mix_part(packs, mixer_ref, ktok_ref, conv_ref, mixing_ref, lval_ref, scale_ref, mixed_ref):
    E = mixer_ref.shape[1]
    heads = E // HEAD_DIM
    stats = []
    for p in packs:
        tile = p[:, E:].astype(F32)
        stats.append(tile + pltpu.roll(tile, 128 - 2 * heads, 1) + pltpu.roll(tile, 128 - 4 * heads, 1))
    top = stats[0]
    for t in stats[1:]:
        top = jnp.maximum(top, t)
    lane = lax.broadcasted_iota(jnp.int32, (HEAD_DIM, 128), 1)
    weights = [jnp.where(lane < heads, jnp.exp(jnp.minimum(t - top, 0.0)), 0.0) for t in stats]
    total = sum(w * pltpu.roll(t, 128 - heads, 1) for w, t in zip(weights, stats))
    total = jnp.where(lane < heads, total, 1.0)
    weights = [w / total for w in weights]
    scale_ref[...] = weights[0]
    head = lane_head(HEAD_DIM)
    for g in range(E // BLOCK):
        s = group(g)
        lval = jnp.zeros((HEAD_DIM, BLOCK), F32)
        for w, p in zip(weights, packs):
            spread = jnp.zeros((HEAD_DIM, BLOCK), F32)
            for i in range(PACK):
                h = g * PACK + i
                spread = jnp.where(head == i, w[:, h : h + 1], spread)
            lval = lval + spread * p[:, s].astype(F32)
        lval_ref[:, s] = lval
        mixing = mm3(mixer_ref[:, s], lval)
        mixing_ref[:, s] = mixing
        mh, ml = split(mixing)
        tok = ktok_ref[s, :]
        mixed_ref[:, s] = (tn(tok, expand(mh)) + tn(tok, expand(ml)) + conv_ref[:, s].astype(F32)).astype(BF)


def norm_part(r):
    center = r - jnp.mean(r, axis=1, keepdims=True)
    inv = lax.rsqrt(jnp.mean(center * center, axis=1, keepdims=True) + EPS)
    return center * inv, inv


def norm_back(e, n, inv, gain):
    eg = e * gain
    return (eg - jnp.mean(eg, axis=1, keepdims=True) - n * jnp.mean(eg * n, axis=1, keepdims=True)) * inv


def pair_pick(first, second):
    lane = lax.broadcasted_iota(jnp.int32, first.shape, 1)
    return jnp.where(lane < HEAD_DIM, first, second)


def band_apply(row, band, edge, a_ref, rim_ref, cols):
    T = a_ref.shape[0]
    wide = pltpu.roll(jnp.broadcast_to(row, (T, T)), 0, 1, stride=1, stride_axis=0)
    wide = jnp.where(band, wide, 0.0).astype(BF)
    short = jnp.broadcast_to(row, (REACH, T))
    rims = jnp.concatenate(
        [
            pltpu.roll(short, REACH, 1, stride=1, stride_axis=0),
            pltpu.roll(short, 0, 1, stride=1, stride_axis=0),
        ],
        0,
    )[:, :128]
    rims = jnp.where(edge, rims, 0.0).astype(BF)
    return nn(wide, a_ref[:, cols]), nn(rims, rim_ref[:, cols])


def conv_pair(rows_ref, band, edge, a_ref, rim_ref, out_ref, j):
    T = a_ref.shape[0]
    cols = slice(j * 128, (j + 1) * 128)
    one, one_rim = band_apply(rows_ref[2 * j : 2 * j + 1, :], band, edge, a_ref, rim_ref, cols)
    two, two_rim = band_apply(rows_ref[2 * j + 1 : 2 * j + 2, :], band, edge, a_ref, rim_ref, cols)
    both, rim = pair_pick(one, two), pair_pick(one_rim, two_rim)
    out_ref[:REACH, cols] = (both[:REACH] + rim[:REACH]).astype(BF)
    out_ref[REACH : T - REACH, cols] = both[REACH : T - REACH].astype(BF)
    out_ref[T - REACH :, cols] = (both[T - REACH :] + rim[REACH:]).astype(BF)


def band_of(col_ref, flip):
    T = col_ref.shape[0]
    a = lax.broadcasted_iota(jnp.int32, (T, T), 0)
    b = lax.broadcasted_iota(jnp.int32, (T, T), 1)
    gap = (T - 1 - b - a) if flip else (b - a)
    return (jnp.abs(gap) <= REACH) & (as_row(col_ref[...], T, 0, flip) == col_ref[...])


def edge_of(col_ref, before, after, flip):
    T = col_ref.shape[0]
    row = lax.broadcasted_iota(jnp.int32, (REACH, META), 0)
    lane = lax.broadcasted_iota(jnp.int32, (REACH, META), 1)
    shift = 0 if flip else REACH
    i = (REACH - 1 - lane) if flip else lane
    j = (REACH - 1 - lane) if flip else lane - REACH
    low = (i >= row) & (i < REACH) & (as_row(before, META, 0, flip) == col_ref[:REACH] + 1.0)
    high = (j <= row) & (j >= 0) & (as_row(after, META, shift, flip) == col_ref[T - REACH :] + 1.0)
    return jnp.concatenate([low.astype(F32), high.astype(F32)], 0) > 0.5


def rim_of(before_ref, after_ref, E):
    return jnp.concatenate([before_ref[:, :E], after_ref[:, :E], jnp.zeros((META - 2 * REACH, E), BF)], 0)


def conv_body(rows_ref, seg_col_ref, v_ref, before_ref, after_ref, out_ref):
    E = v_ref.shape[1]
    band = band_of(seg_col_ref, False)
    edge = edge_of(seg_col_ref, before_ref[:, E : E + 1].astype(F32), after_ref[:, E : E + 1].astype(F32), False)
    rim = rim_of(before_ref, after_ref, E)
    for j in range(E // 128):
        conv_pair(rows_ref, band, edge, v_ref, rim, out_ref, j)


def conv_back_body(
    rows_ref, seg_col_ref, g_ref, g_before_ref, g_after_ref, qkv_ref, before_ref, after_ref, out_ref, tap_ref
):
    T, E = g_ref.shape
    v_ref = qkv_ref.at[2]
    seg_before, seg_after = before_ref[:, E : E + 1].astype(F32), after_ref[:, E : E + 1].astype(F32)
    band = band_of(seg_col_ref, False)
    edge = edge_of(seg_col_ref, seg_before, seg_after, False)
    band_rev = band_of(seg_col_ref, True)
    edge_rev = edge_of(seg_col_ref, seg_before, seg_after, True)
    g_rim = rim_of(g_before_ref, g_after_ref, E)
    v_rim = rim_of(before_ref, after_ref, E)
    a = lax.broadcasted_iota(jnp.int32, (T, T), 0)
    b = lax.broadcasted_iota(jnp.int32, (T, T), 1)
    flip = jnp.where(a + b == T - 1, 1.0, 0.0).astype(BF)
    a = lax.broadcasted_iota(jnp.int32, (META, META), 0)
    b = lax.broadcasted_iota(jnp.int32, (META, META), 1)
    flip_before = jnp.where(a + b == REACH - 1, 1.0, 0.0).astype(BF)
    flip_after = jnp.where((a + b == 2 * REACH - 1) & (a < REACH), 1.0, 0.0).astype(BF)
    for j in range(E // 128):
        cols = slice(j * 128, (j + 1) * 128)
        conv_pair(rows_ref, band, edge, g_ref, g_rim, out_ref, j)
        v_rev = nn(flip, v_ref[:, cols]).astype(BF)
        before = nn(flip_before, v_rim[:, cols]).astype(BF)
        after = nn(flip_after, v_rim[:, cols]).astype(BF)
        g = g_ref[:, cols].astype(F32)
        lane = lax.broadcasted_iota(jnp.int32, g.shape, 1)
        for i in range(2):
            mine = jnp.where((lane < HEAD_DIM) == (i == 0), g, 0.0).astype(BF)
            h = 2 * j + i
            cross = jnp.where(band_rev, nt(mine, v_rev), 0.0)
            cross = pltpu.roll(cross, 0, 1, stride=1, stride_axis=0)
            tap_ref[h : h + 1, :T] = jnp.sum(cross, axis=0, keepdims=True)
            low = jnp.where(edge_rev[:REACH], nt(mine[:REACH], before), 0.0)
            low = pltpu.roll(low, 0, 1, stride=1, stride_axis=0)
            tap_ref[h : h + 1, T : T + META] = jnp.sum(low, axis=0, keepdims=True)
            high = jnp.where(edge_rev[REACH:], nt(mine[T - REACH :], after), 0.0)
            high = pltpu.roll(high, 0, 1, stride=1, stride_axis=0)
            tap_ref[h : h + 1, T + META :] = jnp.sum(high, axis=0, keepdims=True)


def piece_at(where_ref, p, row_bits, nc):
    f, c = where_ref[0], where_ref[1]
    for i, (axis, mask) in enumerate(row_bits):
        if p >> i & 1:
            if axis == "fsdp":
                f = f ^ mask
            else:
                c = c ^ mask
    return f * nc + c


def mid_body(n, pieces, row_bits, nc, ready, where_ref, *refs):
    packs, refs = refs[:n], refs[n:]
    mixer_ref, ktok_ref, conv_ref, land_ref, x_ref, cot_ref, perm_ref, vec_ref, fb_ref, qkv_hbm, w_hbm, ud_hbm = refs[:12]
    refs = refs[12:]
    gq_ref, lk_ref, lval_ref, scale_ref, mixed_ref, y_ref, gm_ref, gfirst_ref, glast_ref, gmix_ref, first_ref, gb_ref, sums_ref, fbg_ref = refs[:14]
    ku_ref, su_ref, kd_ref, sd_ref = refs[14:18]
    wo, wu, wd, act_ref, dg_ref, mixing_ref, q_ref, sem_in, sem_o = refs[18:]
    T, D = x_ref.shape
    half = D // 2
    FL = wu.shape[2]
    R = D // pieces
    loads = []
    for side in range(2):
        ups, downs = [], []
        for p in range(pieces):
            if pieces > 1:
                at, half_at = piece_at(where_ref, p, row_bits, nc), where_ref[2] ^ side
            else:
                at, half_at = 0, side
            rows = pl.ds(p * R, R)
            k = side * pieces + p
            ups.append(pltpu.make_async_copy(ud_hbm.at[at, half_at, :, pl.ds(0, FL)], wu.at[side, rows], sem_in.at[0, k]))
            downs.append(pltpu.make_async_copy(ud_hbm.at[at, half_at, :, pl.ds(FL, FL)], wd.at[side, rows], sem_in.at[1, k]))
        loads.append((ups, downs))
    load_o = pltpu.make_async_copy(w_hbm.at[:, :, pl.ds(3 * half, half)], wo, sem_o.at[0])
    load_q = pltpu.make_async_copy(qkv_hbm.at[pl.ds(0, 1)], q_ref, sem_o.at[1])
    load_o.start()
    load_q.start()
    for ups, downs in loads:
        for c in ups + downs:
            c.start()
    ready()
    mix_part(packs, mixer_ref, ktok_ref, conv_ref, mixing_ref, lval_ref, scale_ref, mixed_ref)
    gain0, gain1 = vec_ref[0:1], vec_ref[1:2]
    mixed = mixed_ref[...]
    load_o.wait()
    branch = nt(mixed[:, :half], wo[0]) + nt(mixed[:, half:], wo[1])
    n1, inv1 = norm_part(x_ref[...].astype(F32) + branch + vec_ref[4:5])
    hidden = n1 * gain0 + vec_ref[2:3]
    low = hidden.astype(BF)
    step = 512
    ffn = jnp.zeros((T, D), F32)
    cubic, lead = 0.044715, 0.7978845608028654
    for side in range(2):
        for c in loads[side][0] + loads[side][1]:
            c.wait()
        for j in range(FL // step):
            cols = slice(j * step, (j + 1) * step)
            at = slice(side * FL + j * step, side * FL + (j + 1) * step)
            u = nn(low, wu[side, :, cols]) + fb_ref[:, at]
            sq = u * u
            t = jnp.tanh(lead * u * (1.0 + cubic * sq))
            act = (0.5 * u * (1.0 + t)).astype(BF)
            dg_ref[:, at] = 0.5 * (1.0 + t) + 0.5 * u * (1.0 - t * t) * lead * (1.0 + 3.0 * cubic * sq)
            act_ref[:, at] = act
            ffn = ffn + nt(act, wd[side, :, cols])
    n2, inv2 = norm_part(hidden + ffn + vec_ref[5:6])
    y_ref[...] = nt((n2 * gain1 + vec_ref[3:4]).astype(BF), perm_ref[...]).astype(BF)
    cot = cot_ref[...].astype(F32)
    second = norm_back(cot, n2, inv2, gain1)
    sums_ref[1:2] = jnp.sum(cot * n2, axis=0, keepdims=True)
    sums_ref[3:4] = jnp.sum(cot, axis=0, keepdims=True)
    gf = second.astype(BF)
    sums_ref[5:6] = jnp.sum(gf.astype(F32), axis=0, keepdims=True)
    gt = gf.astype(F32).T.astype(BF)
    ht = low.astype(F32).T.astype(BF)
    gh = second
    for side in range(2):
        for j in range(FL // step):
            cols = slice(j * step, (j + 1) * step)
            at = slice(side * FL + j * step, side * FL + (j + 1) * step)
            gu = (nn(gf, wd[side, :, cols]) * dg_ref[:, at]).astype(BF)
            fbg_ref[:, at] = jnp.sum(gu.astype(F32), axis=0, keepdims=True)
            ku_ref[side, :, cols] = nn(ht[:half], gu).astype(BF)
            su_ref[side, :, cols] = nn(ht[half:], gu).astype(BF)
            gh = gh + nt(gu, wu[side, :, cols])
            kd_ref[side, :, cols] = nn(gt[:half], act_ref[:, at]).astype(BF)
            sd_ref[side, :, cols] = nn(gt[half:], act_ref[:, at]).astype(BF)
    first = norm_back(gh, n1, inv1, gain0)
    sums_ref[0:1] = jnp.sum(gh * n1, axis=0, keepdims=True)
    sums_ref[2:3] = jnp.sum(gh, axis=0, keepdims=True)
    first_ref[...] = first
    low = first.astype(BF)
    gb_ref[...] = low
    sums_ref[4:5] = jnp.sum(low.astype(F32), axis=0, keepdims=True)
    sums_ref[6:8] = jnp.zeros((2, D), F32)
    for side in range(2):
        gm = nn(low, wo[side]).astype(BF)
        cols = slice(side * half, (side + 1) * half)
        gm_ref[:, cols] = gm
        gfirst_ref[:, cols] = gm[:REACH]
        glast_ref[:, cols] = gm[T - REACH :]
    load_q.wait()
    for g in range(D // BLOCK):
        s = group(g)
        gm = gm_ref[:, s]
        gmix_ref[:, s] = compress(nn(ktok_ref[s, :], gm)).astype(BF)
        mh, ml = split(mixing_ref[:, s])
        gk = nt(expand(mh), gm) + nt(expand(ml), gm)
        tok = ktok_ref[s, :].astype(F32)
        gz = (tok * (gk - heads_sum(tok * gk)) * SCALE).astype(BF)
        gq_ref[:, s] = tn(gz, expand(land_ref[:, D + s.start : D + s.stop])).astype(BF)
        lk_ref[:, s] = compress(nn(gz, q_ref[0, :, s]))


def key_back_body(n, ready, where_ref, *refs):
    gmixes, refs = refs[:n], refs[n:]
    mixer_ref, lval_ref, ekey_ref, scale_ref, qkv_ref, land_ref, lk_ref = refs[:7]
    gmix_ref, gv_ref, gk_ref, own_ref = refs[7:11]
    sends, full_ref = refs[11:-1], refs[-1]
    k_ref, v_ref = qkv_ref.at[1], qkv_ref.at[2]
    ready()
    E = v_ref.shape[1]
    for g in range(E // BLOCK):
        s = group(g)
        gmix = gmixes[0][:, s].astype(F32)
        for other in gmixes[1:]:
            gmix = gmix + other[:, s].astype(F32)
        gmix_ref[:, s] = gmix
        lval = lval_ref[:, s]
        glval = tn3(mixer_ref[:, s], gmix)
        gh, gl = split(glval)
        wide = expand(gh)
        v = v_ref[:, s]
        gkk = nt(wide, v) + nt(expand(gl), v)
        center = jnp.sum(expand(glval * lval), axis=1, keepdims=True)
        scale = jnp.concatenate([scale_ref[:, g * PACK + i : g * PACK + i + 1] for i in range(PACK)], 0)
        kk = ekey_ref[s, :].astype(F32) * scale
        gz = (kk * (gkk - center) * SCALE).astype(BF)
        gv_ref[:, s] = tn(kk.astype(BF), wide).astype(BF)
        gk_ref[:, s] = tn(gz, expand(land_ref[:, s])).astype(BF)
        full_ref[:, s] = compress(nn(gz, k_ref[:, s]))
    full_ref[:, E:] = lk_ref[...]
    LL = own_ref.shape[0]
    own_ref[...] = rows_at(full_ref, where_ref[1], LL)
    for p, ref in enumerate(sends):
        ref[...] = rows_at(full_ref, where_ref[1] ^ (p + 1), LL).astype(BF)


def grad_body(n, ready, *refs):
    owns, refs = refs[: n + 1], refs[n + 1 :]
    gqt_ref, gkt_ref, gvk_ref, gvc_ref, x_ref, gb_ref, mixed_ref = refs[:7]
    gq_ref, gk_ref, gv_ref, hbg_ref = refs[7:11]
    outs = refs[11:15]
    ready()
    T, D = x_ref.shape
    half = D // 2
    own = owns[0][...]
    for other in owns[1:]:
        own = own + other[...].astype(F32)
    LL = own.shape[0]
    seg_len = T // LL
    own = own * (1.0 / seg_len)
    spread = jnp.broadcast_to(own[:, None, :], (LL, seg_len, 2 * D)).reshape(T, 2 * D)
    gq = (gqt_ref[...].astype(F32) + spread[:, :D]).astype(BF)
    gk = (gkt_ref[...].astype(F32) + spread[:, D:]).astype(BF)
    gv = (gvk_ref[...].astype(F32) + gvc_ref[...].astype(F32)).astype(BF)
    gv_ref[...] = gv
    gq_ref[...] = gq
    gk_ref[...] = gk
    hbg_ref[0:1] = jnp.sum(gq.astype(F32), axis=0, keepdims=True)
    hbg_ref[1:2] = jnp.sum(gv.astype(F32), axis=0, keepdims=True)
    xt = x_ref[...].astype(F32).T.astype(BF)
    gt = gb_ref[...].astype(F32).T.astype(BF)
    mixed = mixed_ref[...]
    for side in range(2):
        cols = slice(side * half, (side + 1) * half)
        for r in range(2):
            rows = slice(r * half, (r + 1) * half)
            outs[r][side, :, :half] = nn(xt[rows], gq[:, cols]).astype(BF)
            outs[r][side, :, half:] = nn(xt[rows], gk[:, cols]).astype(BF)
            outs[2 + r][side, :, :half] = nn(xt[rows], gv[:, cols]).astype(BF)
            outs[2 + r][side, :, half:] = nn(gt[rows], mixed[:, cols]).astype(BF)


def input_grad_body(gq_ref, gk_ref, gv_ref, first_ref, perm_ref, w_ref, out_ref):
    half = first_ref.shape[1] // 2
    total = first_ref[...]
    for side in range(2):
        cols = slice(side * half, (side + 1) * half)
        total = total + nt(gq_ref[:, cols], w_ref[side, :, :half])
        total = total + nt(gk_ref[:, cols], w_ref[side, :, half : 2 * half])
        total = total + nt(gv_ref[:, cols], w_ref[side, :, 2 * half : 3 * half])
    out_ref[...] = nt(total.astype(BF), perm_ref[...]).astype(BF)


def back_body(n, ready, *refs):
    first, second, rest = refs[:n], refs[n : n + 8], refs[n + 8 :]
    ready()
    conv_back_body(*second, rest[1], rest[2])
    newton_back_body(*first, rest[0], rest[3])


def small_body(rows, ready, tap_ref, hbg_ref, fbg_ref, sums_ref, perm_ref, out_ref):
    ready()
    heads, width = tap_ref.shape
    T = width - 2 * META
    D = sums_ref.shape[1]
    top = rows - 7 * D // META - fbg_ref.shape[1] // 2 // META
    t = lax.broadcasted_iota(jnp.int32, (top, T), 0)
    lane = lax.broadcasted_iota(jnp.int32, (top, T), 1)
    main = ((lane + t - (REACH - 1)) % T == 0) & (t < KW)
    t = lax.broadcasted_iota(jnp.int32, (top, META), 0)
    lane = lax.broadcasted_iota(jnp.int32, (top, META), 1)
    before = (lane + t == REACH - 1) & (t < REACH)
    after = (lane + t == 3 * REACH - 1) & (t < KW)
    out = [jnp.zeros((top, META), F32), jnp.zeros((top, META), F32)]
    half = heads // 2
    for h in range(heads):
        row = tap_ref[h : h + 1, :]
        col = jnp.sum(jnp.where(main, row[:, :T], 0.0), axis=1, keepdims=True)
        col = col + jnp.sum(jnp.where(before, row[:, T : T + META], 0.0), axis=1, keepdims=True)
        col = col + jnp.sum(jnp.where(after, row[:, T + META :], 0.0), axis=1, keepdims=True)
        out[h // half] = jnp.where(lane == h % half, col, out[h // half])
    first = sums_ref[...].astype(BF)
    rest = sums_ref[...] - first.astype(F32)
    second = rest.astype(BF)
    third = (rest - second.astype(F32)).astype(BF)
    perm = perm_ref[...]
    sums = nt(first, perm) + nt(second, perm) + nt(third, perm)
    FL = fbg_ref.shape[1] // 2
    for side in range(2):
        ref = out_ref.at[side]
        ref[:top, :] = out[side]
        at = top
        for i in range(2):
            for j in range(D // 2 // META):
                col = side * (D // 2) + j * META
                ref[at : at + 1, :] = hbg_ref[i : i + 1, col : col + META]
                at += 1
        for j in range(FL // META):
            ref[at : at + 1, :] = fbg_ref[:, side * FL + j * META : side * FL + (j + 1) * META]
            at += 1
        for i in range(6):
            for j in range(D // META):
                ref[at : at + 1, :] = sums[i : i + 1, j * META : (j + 1) * META]
                at += 1


def small_out_body(a_ref, b_ref, c_ref, d_ref, conv_ref, hb_ref, fb_ref, gains_ref, offsets_ref):
    total = (a_ref[0] + b_ref[...]) + (c_ref[...] + d_ref[...])
    rows = total.shape[0]
    D = gains_ref.shape[1]
    FL = fb_ref.shape[1]
    at = rows - 7 * D // META - FL // META
    conv_ref[...] = total[:KW, : conv_ref.shape[1]]
    for i in range(2):
        for j in range(D // 2 // META):
            hb_ref[i : i + 1, j * META : (j + 1) * META] = total[at : at + 1]
            at += 1
    for j in range(FL // META):
        fb_ref[:, j * META : (j + 1) * META] = total[at : at + 1]
        at += 1
    for i in range(6):
        ref, r = (gains_ref, i) if i < 2 else (offsets_ref, i - 2)
        for j in range(D // META):
            ref[r : r + 1, j * META : (j + 1) * META] = total[at : at + 1]
            at += 1


def local(x_in, out_cot, seg_ids, land_doc, w_qkv, w_out, w_up, w_down, conv_taps, head_bias, ffn_bias, gains, offsets):
    nf, nc, nt_ = lax.axis_size("fsdp"), lax.axis_size("ctx"), lax.axis_size("tp")
    f_i, c_i, t_i = lax.axis_index("fsdp"), lax.axis_index("ctx"), lax.axis_index("tp")
    assert nt_ == 2 and x_in.shape[0] == 2
    ctx_bits = [("ctx", 1 << b) for b in range(nc.bit_length() - 1)]
    chip_bits = [("fsdp", 1 << b) for b in range(1, nf.bit_length() - 1)]
    core_bit = ("fsdp", 1)
    row_bits = ctx_bits + chip_bits + [core_bit]
    T, D = x_in.shape[1:]
    R = w_qkv.shape[0]
    C = w_qkv.shape[2]
    E = 2 * C
    FL = w_up.shape[1]
    HL = C // HEAD_DIM
    H = 2 * HL
    LL = land_doc.shape[1]
    L = LL * nc
    where = jnp.stack([f_i, c_i, t_i]).astype(jnp.int32)

    def along_ctx(own):
        return [own] + [swap(own, "ctx", p) for p in range(1, nc)]

    ud = lax.all_gather(jnp.concatenate([w_up, w_down], axis=1), ("fsdp", "ctx", "tp"), axis=0, tiled=True)
    ud = ud.reshape(nf * nc, 2, R, 2 * FL)

    zq = along_ctx(jnp.concatenate([w_qkv.reshape(R, 3 * C), w_out], axis=1))
    x_in, out_cot = later((x_in, out_cot), zq[0])

    q_pos = jnp.arange(D, dtype=jnp.int32)
    piece, inner = q_pos // R, q_pos % R
    mf = jnp.zeros_like(piece)
    mc = jnp.zeros_like(piece)
    for i, (axis, mask) in enumerate(row_bits):
        bit = ((piece >> i) & 1) * mask
        if axis == "fsdp":
            mf = mf ^ bit
        else:
            mc = mc ^ bit
    true_piece = (f_i ^ mf) * nc + (c_i ^ mc)
    perm = (jnp.arange(D, dtype=jnp.int32)[:, None] == (true_piece * R + inner)[None, :]).astype(BF)
    aligned = R % 16 == 0
    if not aligned:
        order = true_piece[::R]
        sides = jnp.stack([t_i, 1 - t_i])
        ud = ud[order][:, sides].transpose(1, 0, 2, 3).reshape(1, 2, D, 2 * FL)

    def pick(a):
        return lax.dynamic_index_in_dim(a, t_i, 0, False)

    x = dot("td,dq->tq", pick(x_in), perm).astype(BF)
    cot = dot("td,dq->tq", pick(out_cot), perm).astype(BF)

    own = jnp.concatenate(zq, 0)
    for bit in chip_bits[:-1]:
        own = jnp.concatenate([own, swap(own, *bit)], 0)
    last_bit = chip_bits[-1]
    plane = [own, swap(own, *last_bit), swap(own, "tp", 1), swap_both(own, last_bit[1])]

    seg_ids, land_doc, conv_taps, head_bias, ffn_bias = later((seg_ids, land_doc, conv_taps, head_bias, ffn_bias), zq[0])
    seg = pick(seg_ids).astype(F32)
    doc = pick(land_doc).astype(F32)
    seg_col = seg[:, None]

    def meta(col):
        return jnp.where(jnp.arange(META)[None, :] == 0, col[:, None], 0.0).astype(BF)

    par = jnp.concatenate([conv_taps.reshape(-1), head_bias.reshape(-1), ffn_bias.reshape(-1)])
    par2 = jnp.stack([par, swap(par, "tp", 1)])
    taps = par2[:, : KW * HL].reshape(2, KW, HL).transpose(0, 2, 1).reshape(H, KW)
    hb = par2[:, KW * HL : KW * HL + 2 * C].reshape(2, 2, C).transpose(1, 0, 2).reshape(2, 2 * C)
    fb = par2[:, KW * HL + 2 * C :].reshape(1, 2 * FL)
    vec = hdot("vd,dq->vq", jnp.concatenate([gains, offsets], 0), perm.astype(F32))
    gap = jnp.zeros((H, T - KW), F32)
    taps_rev = taps[:, ::-1]
    row_fwd = jnp.concatenate([taps[:, REACH:], gap, taps[:, :REACH]], 1)
    row_back = jnp.concatenate([taps_rev[:, REACH:], gap, taps_rev[:, :REACH]], 1)

    mine, other = plane[:2], plane[2:]
    parts = mine + [swap(a, *core_bit) for a in mine] + other + [swap(a, *core_bit) for a in other]
    parts = later(parts, hb, fb, vec, row_fwd, row_back, cot)
    q, k, v, qkv, piece0, vfirst, vlast, w_full = call(
        proj_body,
        [((T, E), BF)] * 3 + [((3, T, E), BF), ((LL, 2 * E + META), BF)] + [((REACH, E + META), BF)] * 2 + [((2, D, 4 * C), BF)],
        x, hb, meta(doc), meta(seg[:REACH] + 1.0), meta(seg[T - REACH :] + 1.0), *parts,
        raw_in=range(5, 13),
        raw_out=(3, 7),
        scratch=[pltpu.VMEM((2, D, 4 * C), BF), pltpu.SemaphoreType.DMA((8,)), pltpu.SemaphoreType.DMA, pltpu.SemaphoreType.DMA((3,))],
        mem=14,
    )

    up = [(i, i + 1) for i in range(nc - 1)]
    down = [(i + 1, i) for i in range(nc - 1)]
    pieces = along_ctx(piece0)
    ktok, ekey, pack, land, land_far = call(
        functools.partial(scores_body, nc),
        [((E, T), BF), ((E, T), BF), ((L, E + META), BF), ((L, 2 * E + META), BF), ((L, 2 * E + META), BF)],
        where, q, k, v, seg_col, *pieces, smem=(0,), far_out=(0, 1, 4), name="scores_body",
    )
    packs = along_ctx(pack)
    v_before, v_after = lax.ppermute(vlast, "ctx", up), lax.ppermute(vfirst, "ctx", down)
    (conv,) = call(simple(conv_body), [((T, E), BF)], row_fwd, seg_col, v, v_before, v_after, far_in=(0, 1), far_out=(0,))
    kt, mixer, p_all, w_all, pi_all = call(
        simple(newton_body), [((L, E), F32), ((L, E), F32)] + [((NEWTON, L, E), F32)] * 3, land, far_out=range(5), us=5.5, mem=10
    )
    n_pieces = D // R if aligned else 1
    res = call(
        functools.partial(mid_body, nc, n_pieces, row_bits, nc),
        [((T, E), BF), ((L, E), F32), ((L, E), F32), ((L, META), F32), ((T, E), BF), ((T, D), BF), ((T, E), BF)]
        + [((REACH, E), BF)] * 2
        + [((L, E), BF), ((T, D), F32), ((T, D), BF), ((8, D), F32), ((1, 2 * FL), F32)]
        + [((2, D // 2, FL), BF)] * 4,
        where, *packs, mixer, ktok, conv, land_far, x, cot, perm, vec, fb, qkv, w_full, ud,
        us=24.0,
        mem=30,
        smem=(0,),
        far_in=range(1, nc + 10),
        raw_in=(nc + 10, nc + 11, nc + 12),
        far_out=(5,),
        scratch=[
            pltpu.VMEM((2, D, C), BF),
            pltpu.VMEM((2, D, FL), BF),
            pltpu.VMEM((2, D, FL), BF),
            pltpu.VMEM((T, 2 * FL), BF),
            pltpu.VMEM((T, 2 * FL), F32),
            pltpu.VMEM((L, E), F32),
            pltpu.VMEM((1, T, E), BF),
            pltpu.SemaphoreType.DMA((2, 2 * n_pieces)),
            pltpu.SemaphoreType.DMA((2,)),
        ],
        name="mid_body",
    )
    gq, lk_part, lval, land_scale, mixed, y, gm, gfirst, glast, gmix0, grad_first, grad_branch, sums, fb_grad = res[:14]
    keep_up, send_up, keep_down, send_down = res[14:]

    every = slice(None)

    def cores_sum(keep, send):
        got = swap(send, *core_bit)
        for bit in reversed(chip_bits[1:]):
            half = keep.shape[1] // 2
            more = swap(add(keep[:, half:], got[:, half:]), *bit)
            keep, got = add(keep[:, :half], got[:, :half]), more
        return keep, got

    bit = chip_bits[0]
    low_rows, high_rows = slice(0, nc * R), slice(nc * R, 2 * nc * R)

    def one_start(keep, got):
        (other,) = combine([[[(0, (1,)), (1, (1,))]]], keep, got, near=aligned)
        return other, swap(other, "tp", 1)

    def two_start(keep, got):
        (send,) = combine([[[(0, (every, high_rows)), (1, (every, high_rows))]]], keep, got, near=aligned)
        return send, swap(send, *bit)

    def one_next(keep, got, more):
        (send,) = combine([[[(0, (0, high_rows)), (1, (0, high_rows)), (2, (high_rows,))]]], keep, got, more, near=aligned)
        return send, swap(send, *bit)

    def two_next(keep, got, more):
        (send,) = combine([[[(0, (1, low_rows)), (1, (1, low_rows)), (2, (1,))]]], keep, got, more, near=aligned)
        return send, swap(send, "tp", 1)

    def ctx_cuts(one, two):
        plan = []
        for p in range(nc):
            rows = slice(p * R, (p + 1) * R)
            plan.append(
                [
                    [(0, (0, rows)), (1, (0, rows)), (2, (rows,)), (3, (rows,))],
                    [(4, (0, rows)), (5, (0, rows)), (6, (0, rows)), (7, (rows,))],
                ]
            )
        return combine(plan, *one, *two, near=aligned)

    def ctx_swap(cuts):
        return [cuts[0]] + [swap(cuts[p], "ctx", p) for p in range(1, nc)]

    def pairs(values):
        while len(values) > 1:
            values = [a + b for a, b in zip(values[::2], values[1::2])]
        return values[0]

    def total(parts):
        return sum(p.astype(F32) for p in parts)

    gmixes = along_ctx(gmix0)
    down2 = cores_sum(keep_down, send_down)
    up2 = cores_sum(keep_up, send_up)
    down2, up2 = later((down2, up2), *gmixes)
    g_before, g_after = lax.ppermute(glast, "ctx", up), lax.ppermute(gfirst, "ctx", down)
    down_sent, down_more = two_start(*down2)
    up_sent, up_more = one_start(*up2)
    res = call(
        functools.partial(key_back_body, nc),
        [((L, E), F32), ((T, E), BF), ((T, E), BF), ((LL, 2 * E), F32)] + [((LL, 2 * E), BF)] * (nc - 1),
        where, *later(gmixes, up_sent, down_sent), mixer, lval, ekey, land_scale, qkv, land_far, lk_part,
        smem=(0,),
        far_in=(nc + 1, nc + 3, nc + 5, nc + 6),
        scratch=[pltpu.VMEM((L, 2 * E), F32)],
        us=3.0,
        mem=12,
        name="key_back_body",
    )
    gmix, gv, gk, own_part = res[:4]
    parts = [own_part] + [swap(a, "ctx", p + 1) for p, a in enumerate(res[4:])]
    own_mix, gvc, tap_all = call(
        functools.partial(back_body, 9), [((LL, 2 * E), F32), ((T, E), BF), ((H, T + 2 * META), F32)],
        land_far, kt, p_all, w_all, pi_all, mixer, gmix, lval, where,
        row_back, seg_col, gm, g_before, g_after, qkv, v_before, v_after,
        smem=(8,),
        far_in=(0, 1, 2, 3, 4, 5, 9, 10, 14, 15, 16),
        scratch=[pltpu.VMEM((L, 2 * E), F32)],
        us=11.0,
        mem=18,
        name="back_body",
    )
    gq, gk, gv, hb_grad, keep1, send1, keep2, send2 = call(
        functools.partial(grad_body, nc),
        [((T, E), BF)] * 3 + [((2, E), F32)] + [((2, D // 2, 2 * C), BF)] * 4,
        *parts, own_mix, gq, gk, gv, gvc, x, grad_branch, mixed,
        far_in=(nc + 5,),
        us=3.0,
        mem=10,
        name="grad_body",
    )
    down_sent2, down_more2 = two_next(*down2, later(down_more, hb_grad))
    up_sent2, up_more2 = one_next(*up2, later(up_more, hb_grad))
    vo2 = cores_sum(keep2, send2)
    qk2 = cores_sum(keep1, send1)
    vo_sent, vo_more = two_start(*later(vo2, down_sent2, up_sent2))
    qk_sent, qk_more = one_start(*later(qk2, down_sent2, up_sent2))
    rows = -(-KW // 8) * 8 + (7 * D + FL) // META
    rows += -rows % 8
    (small,) = call(
        functools.partial(small_body, rows), [((2, rows, META), F32)], later(tap_all, vo_sent, qk_sent), hb_grad, fb_grad, sums, perm,
        far_in=(0, 4), mem=12, name="small_body",
    )
    small_ctx = along_ctx(small)
    (gx,) = call(
        simple(input_grad_body), [((T, D), BF)], later(gq, small), gk, gv, grad_first, perm, w_full,
        far_in=(4, 5), far_out=(0,), us=4.0, mem=14,
    )
    cuts_ud = ctx_cuts((*up2, *later((up_more, up_more2), gx)), (*down2, down_more, down_more2))
    ctx_ud = ctx_swap(cuts_ud)
    small = pairs(later(small_ctx, *cuts_ud))
    small_got = swap(small, *core_bit)
    vo_sent2, vo_more2 = two_next(*vo2, later(vo_more, small))
    qk_sent2, qk_more2 = one_next(*qk2, later(qk_more, small))
    small = small + later(small_got, vo_sent2, qk_sent2)
    for extra in chip_bits[1:]:
        small = small + swap(small, *extra)
    small_got = [swap(small[0], *bit), swap(small[1], "tp", 1), swap_both(small[1], bit[1])]
    y = later(y, vo_sent2, qk_sent2)
    cuts_q = ctx_cuts((*qk2, qk_more, qk_more2), (*vo2, vo_more, vo_more2))
    ctx_q = ctx_swap(cuts_q)
    small_got = later(small_got, *cuts_q)
    ud_grad = total(later(ctx_ud, *cuts_q))
    qo = total(ctx_q)
    conv_grad, hb_out, fb_out, gains_out, offsets_out = call(
        simple(small_out_body),
        [((KW, HL), F32), ((2, C), F32), ((1, FL), F32), ((2, D), F32), ((4, D), F32)],
        small, *small_got,
    )

    def place(mine):
        other = swap(mine, "tp", 1)
        first = t_i == 0
        return jnp.stack([jnp.where(first, mine, other), jnp.where(first, other, mine)])

    return (
        place(y),
        place(gx),
        qo[:, : 3 * C].reshape(R, 3, C),
        qo[:, 3 * C :],
        ud_grad[:, :FL],
        ud_grad[:, FL:],
        conv_grad,
        hb_out,
        fb_out[0],
        gains_out,
        offsets_out,
    )


def solution(mesh):
    placed = (
        P("fsdp", "ctx", None),
        P("fsdp", "ctx", None),
        P("fsdp", "ctx"),
        P("fsdp", "ctx"),
        P(("fsdp", "ctx"), None, "tp"),
        P(("fsdp", "ctx"), "tp"),
        P(("fsdp", "ctx"), "tp"),
        P(("fsdp", "ctx"), "tp"),
        P(None, "tp"),
        P(None, "tp"),
        P("tp"),
        P(),
        P(),
    )
    return jax.shard_map(
        local,
        mesh=mesh,
        in_specs=placed,
        out_specs=placed[:2] + placed[4:],
        check_vma=False,
    )
```

```python
import functools

import jax
import jax.numpy as jnp
from jax import lax
from jax.experimental import pallas as pl
from jax.experimental.pallas import tpu as pltpu
from jax.sharding import PartitionSpec as P

HEAD_DIM = 64
KW = 33
REACH = KW // 2
NEWTON = 6
EPS = 1e-05
SCALE = HEAD_DIM**-0.5
BLOCK = 256
PACK = BLOCK // HEAD_DIM
META = 128
BF = jnp.bfloat16
F32 = jnp.float32
HI = lax.Precision.HIGHEST


def dot(spec, a, b):
    return jnp.einsum(spec, a, b, preferred_element_type=F32)


def hdot(spec, a, b):
    return jnp.einsum(spec, a, b, preferred_element_type=F32, precision=HI)


def swap(a, axis, mask):
    return lax.ppermute(a, axis, [(i, i ^ mask) for i in range(lax.axis_size(axis))])


def swap_both(a, mask):
    nf = lax.axis_size("fsdp")
    return lax.ppermute(a, ("fsdp", "tp"), [(2 * i + j, 2 * (i ^ mask) + (j ^ 1)) for i in range(nf) for j in range(2)])


def add(*terms):
    return sum(t.astype(F32) for t in terms).astype(BF)


def later(value, *after):
    return lax.optimization_barrier((value, after))[0]


def nn(a, b):
    return lax.dot_general(a, b, (((1,), (0,)), ((), ())), preferred_element_type=F32)


def nt(a, b):
    return lax.dot_general(a, b, (((1,), (1,)), ((), ())), preferred_element_type=F32)


def tn(a, b):
    return lax.dot_general(a, b, (((0,), (0,)), ((), ())), preferred_element_type=F32)


def lane_head(rows):
    return lax.broadcasted_iota(jnp.int32, (rows, BLOCK), 1) // HEAD_DIM


def expand(r):
    head = lane_head(HEAD_DIM)
    wide = r.astype(F32)
    return jnp.concatenate([jnp.where(head == i, wide, 0.0) for i in range(PACK)], 0).astype(r.dtype)


def compress(full):
    head = lane_head(HEAD_DIM)
    out = jnp.zeros((HEAD_DIM, BLOCK), F32)
    for i in range(PACK):
        out = jnp.where(head == i, full[i * HEAD_DIM : (i + 1) * HEAD_DIM], out)
    return out


def split(a):
    high = a.astype(BF)
    return high, (a - high.astype(F32)).astype(BF)


def wide_of(b):
    high, low = split(b)
    return expand(high), expand(low)


def tall_of(a):
    high, low = split(a)
    return jnp.concatenate([high, low], 0)


def times(a, b):
    both = nn(a, b[0])
    return both[:HEAD_DIM] + both[HEAD_DIM:] + nn(a[:HEAD_DIM], b[1])


def times_both(a, c, b):
    high = nn(jnp.concatenate([a, c], 0), b[0])
    low = nn(jnp.concatenate([a[:HEAD_DIM], c[:HEAD_DIM]], 0), b[1])
    parts = [high[i * HEAD_DIM : (i + 1) * HEAD_DIM] for i in range(4)]
    return parts[0] + parts[1] + low[:HEAD_DIM], parts[2] + parts[3] + low[HEAD_DIM:]


def mm3(a, b):
    return times(tall_of(a), wide_of(b))


def tn3(a, b):
    ah, al = split(a)
    bh, bl = split(b)
    return compress(tn(ah, bh) + tn(al, bh) + tn(ah, bl))


def eye_row():
    row = lax.broadcasted_iota(jnp.int32, (HEAD_DIM, BLOCK), 0)
    lane = lax.broadcasted_iota(jnp.int32, (HEAD_DIM, BLOCK), 1)
    return jnp.where(row == lane % HEAD_DIM, 1.0, 0.0)


def head_total(a):
    head = lane_head(1)
    col = jnp.sum(a, axis=0, keepdims=True)
    out = jnp.zeros_like(col)
    for i in range(PACK):
        one = jnp.sum(jnp.where(head == i, col, 0.0), axis=1, keepdims=True)
        out = jnp.where(head == i, one, out)
    return out


def heads_sum(a):
    parts = a.reshape(PACK, HEAD_DIM, a.shape[1])
    return jnp.broadcast_to(jnp.sum(parts, axis=1, keepdims=True), parts.shape).reshape(a.shape)


def heads_max(a):
    parts = a.reshape(PACK, HEAD_DIM, a.shape[1])
    return jnp.broadcast_to(jnp.max(parts, axis=1, keepdims=True), parts.shape).reshape(a.shape)


def tall(mask):
    return jnp.concatenate([mask] * PACK, 0) > 0.5


def group(g):
    return slice(g * BLOCK, (g + 1) * BLOCK)


def as_row(col, lanes, shift=0, flip=False):
    n = col.shape[0]
    row = lax.broadcasted_iota(jnp.int32, (n, lanes), 0)
    lane = lax.broadcasted_iota(jnp.int32, (n, lanes), 1) - shift
    hit = (row + lane == n - 1) if flip else (row == lane)
    return jnp.sum(jnp.where(hit, col, 0.0), axis=0, keepdims=True)


def rows_at(ref, index, count):
    return ref[pl.ds(pl.multiple_of(index * count, count), count), :]


def call(body, outs, *args, us=2.0, raw_in=(), raw_out=(), far_in=(), far_out=(), smem=(), scratch=(), mem=8, name=None):
    n, m = len(args), len(outs)
    far_in, far_out = list(far_in), list(far_out)

    def space(outside):
        return pltpu.HBM if outside else pltpu.VMEM

    ins = [space(i in raw_in or i in far_in) for i in range(n)]
    res = [space(i in raw_out or i in far_out) for i in range(m)]

    def inner(*refs):
        given, made, extra = list(refs[:n]), list(refs[n : n + m]), refs[n + m :]
        vm_in, extra = extra[: len(far_in)], extra[len(far_in) :]
        vm_out, extra = extra[: len(far_out)], extra[len(far_out) :]
        sem_in, sem_out, rest = extra[0], extra[1], extra[2:]
        loads = [pltpu.make_async_copy(given[i], v, sem_in.at[j]) for j, (i, v) in enumerate(zip(far_in, vm_in))]
        stores = [pltpu.make_async_copy(v, made[i], sem_out.at[j]) for j, (i, v) in enumerate(zip(far_out, vm_out))]
        for c in loads:
            c.start()
        for i, v in zip(far_in, vm_in):
            given[i] = v
        for i, v in zip(far_out, vm_out):
            made[i] = v

        def ready(first=0, last=len(loads)):
            for c in loads[first:last]:
                c.wait()

        body(ready, *given, *made, *rest)
        for c in stores:
            c.start()
        for c in stores:
            c.wait()

    return pl.pallas_call(
        inner,
        out_shape=[r(*o) for r, o in zip(res, outs)],
        in_specs=[pl.BlockSpec(memory_space=pltpu.SMEM if i in smem else ins[i]) for i in range(n)],
        out_specs=[pl.BlockSpec(memory_space=r) for r in res],
        scratch_shapes=[pltpu.VMEM(args[i].shape, args[i].dtype) for i in far_in]
        + [pltpu.VMEM(*outs[i]) for i in far_out]
        + [pltpu.SemaphoreType.DMA((max(len(far_in), 1),)), pltpu.SemaphoreType.DMA((max(len(far_out), 1),))]
        + list(scratch),
        compiler_params=pltpu.CompilerParams(vmem_limit_bytes=mem << 20),
        cost_estimate=pl.CostEstimate(flops=int(us * 1e7), bytes_accessed=1024, transcendentals=0),
        name=name or body.__name__,
    )(*[a if i in smem else pltpu.with_memory_space_constraint(a, ins[i]) for i, a in enumerate(args)])


def combine(plan, *arrays, near=True, far_in=()):
    shapes = [
        (arrays[parts[0][0][0]][parts[0][0][1]].shape[:-1], [arrays[p[0][0]][p[0][1]].shape[-1] for p in parts]) for parts in plan
    ]
    if not near:
        return [
            jnp.concatenate([add(*[arrays[i][at] for i, at in terms]) for terms in parts], -1) if len(parts) > 1
            else add(*[arrays[i][at] for i, at in parts[0]])
            for parts in plan
        ]

    def sum_body(ready, *refs):
        ready()
        ins, res = refs[: len(arrays)], refs[len(arrays) :]
        for parts, (_, widths), out in zip(plan, shapes, res):
            col = 0
            for terms, width in zip(parts, widths):
                total = sum(ins[i][at].astype(F32) for i, at in terms).astype(BF)
                out[..., col : col + width] = total
                col += width

    return call(sum_body, [(lead + (sum(w),), BF) for lead, w in shapes], *arrays, far_in=far_in, mem=16)


def simple(body):
    def run(ready, *refs):
        ready()
        body(*refs)

    run.__name__ = body.__name__
    return run


def proj_body(ready, x_ref, hb_ref, doc_ref, first_ref, last_ref, *refs):
    parts, refs = refs[:10], refs[10:]
    q_ref, k_ref, v_ref, qkv_hbm, piece_ref, vfirst_ref, vlast_ref, w_hbm, w_ref, sem, sem_w, sem_f = refs
    rows, wide = parts[0].shape
    loads = []
    for i, part in enumerate(parts):
        kind, core = i % 5, i // 5
        side, chip = (kind > 1) * 1, (kind in (1, 3, 4)) * 1
        cols = pl.ds((kind == 4) * wide // 2, part.shape[1])
        at = pl.ds((2 * core + chip) * rows, rows)
        loads.append(pltpu.make_async_copy(part, w_ref.at[side, at, cols], sem.at[i]))
    for c in loads:
        c.start()
    ready()
    T, D = x_ref.shape
    C = D // 2
    x = x_ref[...]
    LL = piece_ref.shape[0]
    seg_len = T // LL
    row = lax.broadcasted_iota(jnp.int32, (LL, T), 0)
    col = lax.broadcasted_iota(jnp.int32, (LL, T), 1)
    mean = jnp.where(col // seg_len == row, 1.0 / seg_len, 0.0).astype(BF)
    store = pltpu.make_async_copy(w_ref, w_hbm, sem_w)
    for c in loads:
        c.wait()
    store.start()
    for side in range(2):
        cols = slice(side * C, (side + 1) * C)
        q = (nn(x, w_ref[side, :, :C]) + hb_ref[0:1, cols]).astype(BF)
        k = nn(x, w_ref[side, :, C : 2 * C]).astype(BF)
        v = (nn(x, w_ref[side, :, 2 * C : 3 * C]) + hb_ref[1:2, cols]).astype(BF)
        q_ref[:, cols] = q
        k_ref[:, cols] = k
        v_ref[:, cols] = v
        vfirst_ref[:, cols] = v[:REACH]
        vlast_ref[:, cols] = v[T - REACH :]
        piece_ref[:, cols] = nn(mean, q).astype(BF)
        piece_ref[:, D + side * C : D + (side + 1) * C] = nn(mean, k).astype(BF)
    piece_ref[:, 2 * D :] = doc_ref[...]
    vfirst_ref[:, D:] = first_ref[...]
    vlast_ref[:, D:] = last_ref[...]
    extra = [pltpu.make_async_copy(r, qkv_hbm.at[i], sem_f.at[i]) for i, r in enumerate((q_ref, k_ref, v_ref))]
    for c in extra:
        c.start()
    for c in extra:
        c.wait()
    store.wait()


def scores_body(n, ready, where_ref, q_ref, k_ref, v_ref, seg_ref, *refs):
    pieces, (ktok_ref, ekey_ref, pack_ref, land_ref, land_far_ref) = refs[:n], refs[n:]
    ready()
    LL = pieces[0].shape[0]
    E = q_ref.shape[1]
    for p in range(n):
        at = pl.multiple_of((where_ref[1] ^ p) * LL, LL)
        land_ref[pl.ds(at, LL), :] = pieces[p][...]
    doc = land_ref[:, 2 * E : 2 * E + 1].astype(F32)
    land_far_ref[...] = land_ref[...]
    allowed = tall((doc == as_row(seg_ref[...], q_ref.shape[0])).astype(F32))
    lane = lax.broadcasted_iota(jnp.int32, (HEAD_DIM, META), 1)
    stats = jnp.zeros((HEAD_DIM, META), F32)
    heads = E // HEAD_DIM
    for g in range(E // BLOCK):
        s = group(g)
        lq, lk = land_ref[:, s], land_ref[:, E + g * BLOCK : E + (g + 1) * BLOCK]
        z = nt(expand(lk), q_ref[:, s]) * SCALE
        z = jnp.where(allowed, z, -1e30)
        e = jnp.where(allowed, jnp.exp(z - heads_max(z)), 0.0)
        ktok_ref[s, :] = (e / heads_sum(e)).astype(BF)
        z = nt(expand(lq), k_ref[:, s]) * SCALE
        z = jnp.where(allowed, z, -1e30)
        top = jnp.max(z, axis=1, keepdims=True)
        e = jnp.where(allowed, jnp.exp(z - top), 0.0)
        total = jnp.sum(e, axis=1, keepdims=True)
        low = e.astype(BF)
        ekey_ref[s, :] = low
        pack_ref[:, s] = compress(nn(low, v_ref[:, s])).astype(BF)
        for i in range(PACK):
            h = g * PACK + i
            rows = slice(i * HEAD_DIM, (i + 1) * HEAD_DIM)
            stats = jnp.where(lane == h, top[rows], stats)
            stats = jnp.where(lane == heads + h, total[rows], stats)
    first = stats.astype(BF).astype(F32)
    second = (stats - first).astype(BF).astype(F32)
    third = stats - first - second
    pack_ref[:, E:] = (first + pltpu.roll(second, 2 * heads, 1) + pltpu.roll(third, 4 * heads, 1)).astype(BF)


def newton_body(land_ref, kt_ref, mixer_ref, p_ref, w_ref, pi_ref):
    E = kt_ref.shape[1]
    eye = eye_row()
    doc = land_ref[:, 2 * E : 2 * E + 1].astype(F32)
    allowed = jnp.concatenate([(doc == as_row(doc, HEAD_DIM)).astype(F32)] * PACK, 1) > 0.5
    groups = [group(g) for g in range(E // BLOCK)]
    kts, invs, ps, pis = [], [], [], []
    for s in groups:
        lq, lk = land_ref[:, s], land_ref[:, E + s.start : E + s.stop]
        z = nt(lk, expand(lq)) * SCALE
        z = jnp.where(allowed, z, -1e30)
        e = jnp.where(allowed, jnp.exp(z - jnp.max(z, axis=0, keepdims=True)), 0.0)
        kt = e / jnp.sum(e, axis=0, keepdims=True)
        kts.append(kt)
        invs.append(1.0 / head_total(kt * kt))
        kt_ref[:, s] = kt
    ps = [tn3(kt, kt) * inv for kt, inv in zip(kts, invs)]
    for step in range(NEWTON):
        for s, p in zip(groups, ps):
            p_ref[step, :, s] = p
        talls = [tall_of(p) for p in ps]
        p2s = [times(t, wide_of(p)) for t, p in zip(talls, ps)]
        ws = [0.25 * (13.0 * eye - 15.0 * p + mm3(p2, 7.0 * eye - p)) for p, p2 in zip(ps, p2s)]
        wides = [wide_of(w) for w in ws]
        if step == 0:
            ps, pis = [times(t, w) for t, w in zip(talls, wides)], ws
        elif step < NEWTON - 1:
            both = [times_both(t, tall_of(pi), w) for t, pi, w in zip(talls, pis, wides)]
            ps, pis = [b[0] for b in both], [b[1] for b in both]
        else:
            pis = [times(tall_of(pi), w) for pi, w in zip(pis, wides)]
        for s, w, pi in zip(groups, ws, pis):
            w_ref[step, :, s] = w
            pi_ref[step, :, s] = pi
    for s, kt, pi, inv in zip(groups, kts, pis, invs):
        mixer_ref[:, s] = mm3(kt, pi) * inv


def newton_back_body(land_ref, kt_ref, p_ref, w_ref, pi_ref, mixer_ref, gmix_ref, lval_ref, where_ref, own_ref, full_ref):
    E = kt_ref.shape[1]
    groups = [group(g) for g in range(E // BLOCK)]
    many = range(len(groups))
    kts = [kt_ref[:, s] for s in groups]
    invs = [1.0 / head_total(kt * kt) for kt in kts]
    grads = []
    for s in groups:
        gh, gl = split(gmix_ref[:, s])
        vh, vl = split(lval_ref[:, s])
        wide = expand(vh)
        grads.append(nt(gh, wide) + nt(gl, wide) + nt(gh, expand(vl)))
    d_pis = [tn3(kts[i], grads[i]) * invs[i] for i in many]
    d_kts = [mm3(grads[i], pi_ref[NEWTON - 1, :, groups[i]]) * invs[i] for i in many]
    d_cs = [-head_total(grads[i] * mixer_ref[:, groups[i]]) * invs[i] for i in many]
    d_ps = None
    for step in reversed(range(NEWTON)):
        ps = [p_ref[step, :, s] for s in groups]
        ws = [w_ref[step, :, s] for s in groups]
        p_tall = [tall_of(p) for p in ps]
        p_wide = [wide_of(p) for p in ps]
        d_ws = [mm3(pi_ref[step - 1, :, groups[i]], d_pis[i]) for i in many] if step else d_pis
        w_wide = [wide_of(w) for w in ws] if step or d_ps is not None else None
        if d_ps is not None:
            d_ws = [d_ws[i] + times(p_tall[i], wide_of(d_ps[i])) for i in many]
            if step:
                both = [times_both(tall_of(d_ps[i]), tall_of(d_pis[i]), w_wide[i]) for i in many]
                d_ps, d_pis = [b[0] for b in both], [b[1] for b in both]
            else:
                d_ps = [times(tall_of(d_ps[i]), w_wide[i]) for i in many]
        elif step:
            d_pis = [times(tall_of(d_pis[i]), w_wide[i]) for i in many]
        ones = [times(p_tall[i], wide_of(d_ws[i])) for i in many]
        twos = [ones[i] + times(tall_of(d_ws[i]), p_wide[i]) for i in many]
        more = [
            0.25
            * (7.0 * twos[i] - 15.0 * d_ws[i] - times(p_tall[i], wide_of(ones[i])) - times(tall_of(twos[i]), p_wide[i]))
            for i in many
        ]
        d_ps = more if d_ps is None else [d_ps[i] + more[i] for i in many]
    for i in many:
        s, kt, inv = groups[i], kts[i], invs[i]
        lq, lk = land_ref[:, s], land_ref[:, E + s.start : E + s.stop]
        d_c = d_cs[i] - head_total(d_ps[i] * p_ref[0, :, s]) * inv
        kh, kl = split(kt)
        sh, sl = split(d_ps[i] * inv)
        wide = expand(sh)
        thin = expand(sl)
        d_kt = d_kts[i] + nn(kh, wide) + nn(kl, wide) + nn(kh, thin) + nt(kh, wide) + nt(kl, wide) + nt(kh, thin)
        d_kt = d_kt + 2.0 * d_c * kt
        dz = kt * (d_kt - jnp.sum(kt * d_kt, axis=0, keepdims=True)) * SCALE
        zh, zl = split(dz)
        wide = expand(lq)
        full_ref[:, E + s.start : E + s.stop] = nn(zh, wide) + nn(zl, wide)
        full_ref[:, s] = compress(tn(zh, lk) + tn(zl, lk))
    own_ref[...] = rows_at(full_ref, where_ref[1], own_ref.shape[0])


def mix_part(packs, mixer_ref, ktok_ref, conv_ref, mixing_ref, lval_ref, scale_ref, mixed_ref):
    E = mixer_ref.shape[1]
    heads = E // HEAD_DIM
    stats = []
    for p in packs:
        tile = p[:, E:].astype(F32)
        stats.append(tile + pltpu.roll(tile, 128 - 2 * heads, 1) + pltpu.roll(tile, 128 - 4 * heads, 1))
    top = stats[0]
    for t in stats[1:]:
        top = jnp.maximum(top, t)
    lane = lax.broadcasted_iota(jnp.int32, (HEAD_DIM, 128), 1)
    weights = [jnp.where(lane < heads, jnp.exp(jnp.minimum(t - top, 0.0)), 0.0) for t in stats]
    total = sum(w * pltpu.roll(t, 128 - heads, 1) for w, t in zip(weights, stats))
    total = jnp.where(lane < heads, total, 1.0)
    weights = [w / total for w in weights]
    scale_ref[...] = weights[0]
    head = lane_head(HEAD_DIM)
    for g in range(E // BLOCK):
        s = group(g)
        lval = jnp.zeros((HEAD_DIM, BLOCK), F32)
        for w, p in zip(weights, packs):
            spread = jnp.zeros((HEAD_DIM, BLOCK), F32)
            for i in range(PACK):
                h = g * PACK + i
                spread = jnp.where(head == i, w[:, h : h + 1], spread)
            lval = lval + spread * p[:, s].astype(F32)
        lval_ref[:, s] = lval
        mixing = mm3(mixer_ref[:, s], lval)
        mixing_ref[:, s] = mixing
        mh, ml = split(mixing)
        tok = ktok_ref[s, :]
        mixed_ref[:, s] = (tn(tok, expand(mh)) + tn(tok, expand(ml)) + conv_ref[:, s].astype(F32)).astype(BF)


def norm_part(r):
    center = r - jnp.mean(r, axis=1, keepdims=True)
    inv = lax.rsqrt(jnp.mean(center * center, axis=1, keepdims=True) + EPS)
    return center * inv, inv


def norm_back(e, n, inv, gain):
    eg = e * gain
    return (eg - jnp.mean(eg, axis=1, keepdims=True) - n * jnp.mean(eg * n, axis=1, keepdims=True)) * inv


def pair_pick(first, second):
    lane = lax.broadcasted_iota(jnp.int32, first.shape, 1)
    return jnp.where(lane < HEAD_DIM, first, second)


def band_apply(row, band, edge, a_ref, rim_ref, cols):
    T = a_ref.shape[0]
    wide = pltpu.roll(jnp.broadcast_to(row, (T, T)), 0, 1, stride=1, stride_axis=0)
    wide = jnp.where(band, wide, 0.0).astype(BF)
    short = jnp.broadcast_to(row, (REACH, T))
    rims = jnp.concatenate(
        [
            pltpu.roll(short, REACH, 1, stride=1, stride_axis=0),
            pltpu.roll(short, 0, 1, stride=1, stride_axis=0),
        ],
        0,
    )[:, :128]
    rims = jnp.where(edge, rims, 0.0).astype(BF)
    return nn(wide, a_ref[:, cols]), nn(rims, rim_ref[:, cols])


def conv_pair(rows_ref, band, edge, a_ref, rim_ref, out_ref, j):
    T = a_ref.shape[0]
    cols = slice(j * 128, (j + 1) * 128)
    one, one_rim = band_apply(rows_ref[2 * j : 2 * j + 1, :], band, edge, a_ref, rim_ref, cols)
    two, two_rim = band_apply(rows_ref[2 * j + 1 : 2 * j + 2, :], band, edge, a_ref, rim_ref, cols)
    both, rim = pair_pick(one, two), pair_pick(one_rim, two_rim)
    out_ref[:REACH, cols] = (both[:REACH] + rim[:REACH]).astype(BF)
    out_ref[REACH : T - REACH, cols] = both[REACH : T - REACH].astype(BF)
    out_ref[T - REACH :, cols] = (both[T - REACH :] + rim[REACH:]).astype(BF)


def band_of(col_ref, flip):
    T = col_ref.shape[0]
    a = lax.broadcasted_iota(jnp.int32, (T, T), 0)
    b = lax.broadcasted_iota(jnp.int32, (T, T), 1)
    gap = (T - 1 - b - a) if flip else (b - a)
    return (jnp.abs(gap) <= REACH) & (as_row(col_ref[...], T, 0, flip) == col_ref[...])


def edge_of(col_ref, before, after, flip):
    T = col_ref.shape[0]
    row = lax.broadcasted_iota(jnp.int32, (REACH, META), 0)
    lane = lax.broadcasted_iota(jnp.int32, (REACH, META), 1)
    shift = 0 if flip else REACH
    i = (REACH - 1 - lane) if flip else lane
    j = (REACH - 1 - lane) if flip else lane - REACH
    low = (i >= row) & (i < REACH) & (as_row(before, META, 0, flip) == col_ref[:REACH] + 1.0)
    high = (j <= row) & (j >= 0) & (as_row(after, META, shift, flip) == col_ref[T - REACH :] + 1.0)
    return jnp.concatenate([low.astype(F32), high.astype(F32)], 0) > 0.5


def rim_of(before_ref, after_ref, E):
    return jnp.concatenate([before_ref[:, :E], after_ref[:, :E], jnp.zeros((META - 2 * REACH, E), BF)], 0)


def conv_body(rows_ref, seg_col_ref, v_ref, before_ref, after_ref, out_ref):
    E = v_ref.shape[1]
    band = band_of(seg_col_ref, False)
    edge = edge_of(seg_col_ref, before_ref[:, E : E + 1].astype(F32), after_ref[:, E : E + 1].astype(F32), False)
    rim = rim_of(before_ref, after_ref, E)
    for j in range(E // 128):
        conv_pair(rows_ref, band, edge, v_ref, rim, out_ref, j)


def conv_back_body(
    rows_ref, seg_col_ref, g_ref, g_before_ref, g_after_ref, qkv_ref, before_ref, after_ref, out_ref, tap_ref
):
    T, E = g_ref.shape
    v_ref = qkv_ref.at[2]
    seg_before, seg_after = before_ref[:, E : E + 1].astype(F32), after_ref[:, E : E + 1].astype(F32)
    band = band_of(seg_col_ref, False)
    edge = edge_of(seg_col_ref, seg_before, seg_after, False)
    band_rev = band_of(seg_col_ref, True)
    edge_rev = edge_of(seg_col_ref, seg_before, seg_after, True)
    g_rim = rim_of(g_before_ref, g_after_ref, E)
    v_rim = rim_of(before_ref, after_ref, E)
    a = lax.broadcasted_iota(jnp.int32, (T, T), 0)
    b = lax.broadcasted_iota(jnp.int32, (T, T), 1)
    flip = jnp.where(a + b == T - 1, 1.0, 0.0).astype(BF)
    a = lax.broadcasted_iota(jnp.int32, (META, META), 0)
    b = lax.broadcasted_iota(jnp.int32, (META, META), 1)
    flip_before = jnp.where(a + b == REACH - 1, 1.0, 0.0).astype(BF)
    flip_after = jnp.where((a + b == 2 * REACH - 1) & (a < REACH), 1.0, 0.0).astype(BF)
    for j in range(E // 128):
        cols = slice(j * 128, (j + 1) * 128)
        conv_pair(rows_ref, band, edge, g_ref, g_rim, out_ref, j)
        v_rev = nn(flip, v_ref[:, cols]).astype(BF)
        before = nn(flip_before, v_rim[:, cols]).astype(BF)
        after = nn(flip_after, v_rim[:, cols]).astype(BF)
        g = g_ref[:, cols].astype(F32)
        lane = lax.broadcasted_iota(jnp.int32, g.shape, 1)
        for i in range(2):
            mine = jnp.where((lane < HEAD_DIM) == (i == 0), g, 0.0).astype(BF)
            h = 2 * j + i
            cross = jnp.where(band_rev, nt(mine, v_rev), 0.0)
            cross = pltpu.roll(cross, 0, 1, stride=1, stride_axis=0)
            tap_ref[h : h + 1, :T] = jnp.sum(cross, axis=0, keepdims=True)
            low = jnp.where(edge_rev[:REACH], nt(mine[:REACH], before), 0.0)
            low = pltpu.roll(low, 0, 1, stride=1, stride_axis=0)
            tap_ref[h : h + 1, T : T + META] = jnp.sum(low, axis=0, keepdims=True)
            high = jnp.where(edge_rev[REACH:], nt(mine[T - REACH :], after), 0.0)
            high = pltpu.roll(high, 0, 1, stride=1, stride_axis=0)
            tap_ref[h : h + 1, T + META :] = jnp.sum(high, axis=0, keepdims=True)


def piece_at(where_ref, p, row_bits, nc):
    f, c = where_ref[0], where_ref[1]
    for i, (axis, mask) in enumerate(row_bits):
        if p >> i & 1:
            if axis == "fsdp":
                f = f ^ mask
            else:
                c = c ^ mask
    return f * nc + c


def mid_body(n, pieces, row_bits, nc, ready, where_ref, *refs):
    packs, refs = refs[:n], refs[n:]
    mixer_ref, ktok_ref, conv_ref, land_ref, x_ref, cot_ref, perm_ref, vec_ref, fb_ref, qkv_hbm, w_hbm, ud_hbm = refs[:12]
    refs = refs[12:]
    gq_ref, lk_ref, lval_ref, scale_ref, mixed_ref, y_ref, gm_ref, gfirst_ref, glast_ref, gmix_ref, first_ref, gb_ref, sums_ref, fbg_ref = refs[:14]
    ku_ref, su_ref, kd_ref, sd_ref = refs[14:18]
    wo, wu, wd, act_ref, dg_ref, mixing_ref, q_ref, sem_in, sem_o = refs[18:]
    T, D = x_ref.shape
    half = D // 2
    FL = wu.shape[2]
    R = D // pieces
    loads = []
    for side in range(2):
        ups, downs = [], []
        for p in range(pieces):
            if pieces > 1:
                at, half_at = piece_at(where_ref, p, row_bits, nc), where_ref[2] ^ side
            else:
                at, half_at = 0, side
            rows = pl.ds(p * R, R)
            k = side * pieces + p
            ups.append(pltpu.make_async_copy(ud_hbm.at[at, half_at, 0], wu.at[side, rows], sem_in.at[0, k]))
            downs.append(pltpu.make_async_copy(ud_hbm.at[at, half_at, 1], wd.at[side, rows], sem_in.at[1, k]))
        loads.append((ups, downs))
    load_o = pltpu.make_async_copy(w_hbm.at[:, :, pl.ds(3 * half, half)], wo, sem_o.at[0])
    load_q = pltpu.make_async_copy(qkv_hbm.at[pl.ds(0, 1)], q_ref, sem_o.at[1])
    load_o.start()
    load_q.start()
    for ups, downs in loads:
        for c in ups + downs:
            c.start()
    ready()
    mix_part(packs, mixer_ref, ktok_ref, conv_ref, mixing_ref, lval_ref, scale_ref, mixed_ref)
    gain0, gain1 = vec_ref[0:1], vec_ref[1:2]
    mixed = mixed_ref[...]
    load_o.wait()
    branch = nt(mixed[:, :half], wo[0]) + nt(mixed[:, half:], wo[1])
    n1, inv1 = norm_part(x_ref[...].astype(F32) + branch + vec_ref[4:5])
    hidden = n1 * gain0 + vec_ref[2:3]
    low = hidden.astype(BF)
    step = FL // 2
    ffn = jnp.zeros((T, D), F32)
    cubic, lead = 0.044715, 0.7978845608028654
    for side in range(2):
        for c in loads[side][0]:
            c.wait()
        for j in range(FL // step):
            cols = slice(j * step, (j + 1) * step)
            at = slice(side * FL + j * step, side * FL + (j + 1) * step)
            u = nn(low, wu[side, :, cols]) + fb_ref[:, at]
            sq = u * u
            t = jnp.tanh(lead * u * (1.0 + cubic * sq))
            act = (0.5 * u * (1.0 + t)).astype(BF)
            dg_ref[:, at] = 0.5 * (1.0 + t) + 0.5 * u * (1.0 - t * t) * lead * (1.0 + 3.0 * cubic * sq)
            act_ref[:, at] = act
            if j == 0:
                for c in loads[side][1]:
                    c.wait()
            ffn = ffn + nt(act, wd[side, :, cols])
    n2, inv2 = norm_part(hidden + ffn + vec_ref[5:6])
    y_ref[...] = nt((n2 * gain1 + vec_ref[3:4]).astype(BF), perm_ref[...]).astype(BF)
    cot = cot_ref[...].astype(F32)
    second = norm_back(cot, n2, inv2, gain1)
    sums_ref[1:2] = jnp.sum(cot * n2, axis=0, keepdims=True)
    sums_ref[3:4] = jnp.sum(cot, axis=0, keepdims=True)
    gf = second.astype(BF)
    sums_ref[5:6] = jnp.sum(gf.astype(F32), axis=0, keepdims=True)
    gt = gf.astype(F32).T.astype(BF)
    ht = low.astype(F32).T.astype(BF)
    gh = second
    for side in range(2):
        for j in range(FL // step):
            cols = slice(j * step, (j + 1) * step)
            at = slice(side * FL + j * step, side * FL + (j + 1) * step)
            gu = (nn(gf, wd[side, :, cols]) * dg_ref[:, at]).astype(BF)
            fbg_ref[:, at] = jnp.sum(gu.astype(F32), axis=0, keepdims=True)
            ku_ref[side, :, cols] = nn(ht[:half], gu).astype(BF)
            su_ref[side, :, cols] = nn(ht[half:], gu).astype(BF)
            gh = gh + nt(gu, wu[side, :, cols])
            kd_ref[side, :, cols] = nn(gt[:half], act_ref[:, at]).astype(BF)
            sd_ref[side, :, cols] = nn(gt[half:], act_ref[:, at]).astype(BF)
    first = norm_back(gh, n1, inv1, gain0)
    sums_ref[0:1] = jnp.sum(gh * n1, axis=0, keepdims=True)
    sums_ref[2:3] = jnp.sum(gh, axis=0, keepdims=True)
    first_ref[...] = first
    low = first.astype(BF)
    gb_ref[...] = low
    sums_ref[4:5] = jnp.sum(low.astype(F32), axis=0, keepdims=True)
    sums_ref[6:8] = jnp.zeros((2, D), F32)
    for side in range(2):
        gm = nn(low, wo[side]).astype(BF)
        cols = slice(side * half, (side + 1) * half)
        gm_ref[:, cols] = gm
        gfirst_ref[:, cols] = gm[:REACH]
        glast_ref[:, cols] = gm[T - REACH :]
    load_q.wait()
    for g in range(D // BLOCK):
        s = group(g)
        gm = gm_ref[:, s]
        gmix_ref[:, s] = compress(nn(ktok_ref[s, :], gm)).astype(BF)
        mh, ml = split(mixing_ref[:, s])
        gk = nt(expand(mh), gm) + nt(expand(ml), gm)
        tok = ktok_ref[s, :].astype(F32)
        gz = (tok * (gk - heads_sum(tok * gk)) * SCALE).astype(BF)
        gq_ref[:, s] = tn(gz, expand(land_ref[:, D + s.start : D + s.stop])).astype(BF)
        lk_ref[:, s] = compress(nn(gz, q_ref[0, :, s]))


def key_back_body(n, ready, where_ref, *refs):
    gmixes, refs = refs[:n], refs[n:]
    mixer_ref, lval_ref, ekey_ref, scale_ref, qkv_ref, land_ref, lk_ref = refs[:7]
    gmix_ref, gv_ref, gk_ref, own_ref = refs[7:11]
    sends, full_ref = refs[11:-1], refs[-1]
    k_ref, v_ref = qkv_ref.at[1], qkv_ref.at[2]
    ready()
    E = v_ref.shape[1]
    for g in range(E // BLOCK):
        s = group(g)
        gmix = gmixes[0][:, s].astype(F32)
        for other in gmixes[1:]:
            gmix = gmix + other[:, s].astype(F32)
        gmix_ref[:, s] = gmix
        lval = lval_ref[:, s]
        glval = tn3(mixer_ref[:, s], gmix)
        gh, gl = split(glval)
        wide = expand(gh)
        v = v_ref[:, s]
        gkk = nt(wide, v) + nt(expand(gl), v)
        center = jnp.sum(expand(glval * lval), axis=1, keepdims=True)
        scale = jnp.concatenate([scale_ref[:, g * PACK + i : g * PACK + i + 1] for i in range(PACK)], 0)
        kk = ekey_ref[s, :].astype(F32) * scale
        gz = (kk * (gkk - center) * SCALE).astype(BF)
        gv_ref[:, s] = tn(kk.astype(BF), wide).astype(BF)
        gk_ref[:, s] = tn(gz, expand(land_ref[:, s])).astype(BF)
        full_ref[:, s] = compress(nn(gz, k_ref[:, s]))
    full_ref[:, E:] = lk_ref[...]
    LL = own_ref.shape[0]
    own_ref[...] = rows_at(full_ref, where_ref[1], LL)
    for p, ref in enumerate(sends):
        ref[...] = rows_at(full_ref, where_ref[1] ^ (p + 1), LL).astype(BF)


def grad_body(n, ready, *refs):
    owns, refs = refs[: n + 1], refs[n + 1 :]
    gqt_ref, gkt_ref, gvk_ref, gvc_ref, x_ref, gb_ref, mixed_ref = refs[:7]
    gq_ref, gk_ref, gv_ref, hbg_ref = refs[7:11]
    outs = refs[11:15]
    ready()
    T, D = x_ref.shape
    half = D // 2
    own = owns[0][...]
    for other in owns[1:]:
        own = own + other[...].astype(F32)
    LL = own.shape[0]
    seg_len = T // LL
    own = own * (1.0 / seg_len)
    spread = jnp.broadcast_to(own[:, None, :], (LL, seg_len, 2 * D)).reshape(T, 2 * D)
    gq = (gqt_ref[...].astype(F32) + spread[:, :D]).astype(BF)
    gk = (gkt_ref[...].astype(F32) + spread[:, D:]).astype(BF)
    gv = (gvk_ref[...].astype(F32) + gvc_ref[...].astype(F32)).astype(BF)
    gv_ref[...] = gv
    gq_ref[...] = gq
    gk_ref[...] = gk
    hbg_ref[0:1] = jnp.sum(gq.astype(F32), axis=0, keepdims=True)
    hbg_ref[1:2] = jnp.sum(gv.astype(F32), axis=0, keepdims=True)
    xt = x_ref[...].astype(F32).T.astype(BF)
    gt = gb_ref[...].astype(F32).T.astype(BF)
    mixed = mixed_ref[...]
    for side in range(2):
        cols = slice(side * half, (side + 1) * half)
        for r in range(2):
            rows = slice(r * half, (r + 1) * half)
            outs[r][side, :, :half] = nn(xt[rows], gq[:, cols]).astype(BF)
            outs[r][side, :, half:] = nn(xt[rows], gk[:, cols]).astype(BF)
            outs[2 + r][side, :, :half] = nn(xt[rows], gv[:, cols]).astype(BF)
            outs[2 + r][side, :, half:] = nn(gt[rows], mixed[:, cols]).astype(BF)


def input_grad_body(gq_ref, gk_ref, gv_ref, first_ref, perm_ref, w_ref, out_ref):
    half = first_ref.shape[1] // 2
    total = first_ref[...]
    for side in range(2):
        cols = slice(side * half, (side + 1) * half)
        total = total + nt(gq_ref[:, cols], w_ref[side, :, :half])
        total = total + nt(gk_ref[:, cols], w_ref[side, :, half : 2 * half])
        total = total + nt(gv_ref[:, cols], w_ref[side, :, 2 * half : 3 * half])
    out_ref[...] = nt(total.astype(BF), perm_ref[...]).astype(BF)


def back_body(n, ready, *refs):
    first, second, rest = refs[:n], refs[n : n + 8], refs[n + 8 :]
    ready(0, 5)
    conv_back_body(*second, rest[1], rest[2])
    ready(5)
    newton_back_body(*first, rest[0], rest[3])


def small_body(rows, ready, tap_ref, hbg_ref, fbg_ref, sums_ref, perm_ref, out_ref):
    ready()
    heads, width = tap_ref.shape
    T = width - 2 * META
    D = sums_ref.shape[1]
    top = rows - 7 * D // META - fbg_ref.shape[1] // 2 // META
    t = lax.broadcasted_iota(jnp.int32, (top, T), 0)
    lane = lax.broadcasted_iota(jnp.int32, (top, T), 1)
    main = ((lane + t - (REACH - 1)) % T == 0) & (t < KW)
    t = lax.broadcasted_iota(jnp.int32, (top, META), 0)
    lane = lax.broadcasted_iota(jnp.int32, (top, META), 1)
    before = (lane + t == REACH - 1) & (t < REACH)
    after = (lane + t == 3 * REACH - 1) & (t < KW)
    out = [jnp.zeros((top, META), F32), jnp.zeros((top, META), F32)]
    half = heads // 2
    for h in range(heads):
        row = tap_ref[h : h + 1, :]
        col = jnp.sum(jnp.where(main, row[:, :T], 0.0), axis=1, keepdims=True)
        col = col + jnp.sum(jnp.where(before, row[:, T : T + META], 0.0), axis=1, keepdims=True)
        col = col + jnp.sum(jnp.where(after, row[:, T + META :], 0.0), axis=1, keepdims=True)
        out[h // half] = jnp.where(lane == h % half, col, out[h // half])
    first = sums_ref[...].astype(BF)
    rest = sums_ref[...] - first.astype(F32)
    second = rest.astype(BF)
    third = (rest - second.astype(F32)).astype(BF)
    perm = perm_ref[...]
    sums = nt(first, perm) + nt(second, perm) + nt(third, perm)
    FL = fbg_ref.shape[1] // 2
    for side in range(2):
        ref = out_ref.at[side]
        ref[:top, :] = out[side]
        at = top
        for i in range(2):
            for j in range(D // 2 // META):
                col = side * (D // 2) + j * META
                ref[at : at + 1, :] = hbg_ref[i : i + 1, col : col + META]
                at += 1
        for j in range(FL // META):
            ref[at : at + 1, :] = fbg_ref[:, side * FL + j * META : side * FL + (j + 1) * META]
            at += 1
        for i in range(6):
            for j in range(D // META):
                ref[at : at + 1, :] = sums[i : i + 1, j * META : (j + 1) * META]
                at += 1


def fold_body(*refs):
    ins, (mine_ref, other_ref) = refs[:-2], refs[-2:]
    values = [r[...] for r in ins]
    while len(values) > 1:
        values = [a + b for a, b in zip(values[::2], values[1::2])]
    mine_ref[...] = values[0][0]
    other_ref[...] = values[0][1]


def add_body(a_ref, b_ref, c_ref, d_ref, first_ref, second_ref):
    first_ref[...] = a_ref[...] + b_ref[...]
    second_ref[...] = c_ref[...] + d_ref[...]


def small_out_body(a_ref, b_ref, c_ref, d_ref, conv_ref, hb_ref, fb_ref, gains_ref, offsets_ref):
    total = (a_ref[...] + b_ref[...]) + (c_ref[...] + d_ref[...])
    rows = total.shape[0]
    D = gains_ref.shape[1]
    FL = fb_ref.shape[1]
    at = rows - 7 * D // META - FL // META
    conv_ref[...] = total[:KW, : conv_ref.shape[1]]
    for i in range(2):
        for j in range(D // 2 // META):
            hb_ref[i : i + 1, j * META : (j + 1) * META] = total[at : at + 1]
            at += 1
    for j in range(FL // META):
        fb_ref[:, j * META : (j + 1) * META] = total[at : at + 1]
        at += 1
    for i in range(6):
        ref, r = (gains_ref, i) if i < 2 else (offsets_ref, i - 2)
        for j in range(D // META):
            ref[r : r + 1, j * META : (j + 1) * META] = total[at : at + 1]
            at += 1


def local(x_in, out_cot, seg_ids, land_doc, w_qkv, w_out, w_up, w_down, conv_taps, head_bias, ffn_bias, gains, offsets):
    nf, nc, nt_ = lax.axis_size("fsdp"), lax.axis_size("ctx"), lax.axis_size("tp")
    f_i, c_i, t_i = lax.axis_index("fsdp"), lax.axis_index("ctx"), lax.axis_index("tp")
    assert nt_ == 2 and x_in.shape[0] == 2
    ctx_bits = [("ctx", 1 << b) for b in range(nc.bit_length() - 1)]
    chip_bits = [("fsdp", 1 << b) for b in range(1, nf.bit_length() - 1)]
    core_bit = ("fsdp", 1)
    row_bits = ctx_bits + chip_bits + [core_bit]
    T, D = x_in.shape[1:]
    R = w_qkv.shape[0]
    C = w_qkv.shape[2]
    E = 2 * C
    FL = w_up.shape[1]
    HL = C // HEAD_DIM
    H = 2 * HL
    LL = land_doc.shape[1]
    L = LL * nc
    where = jnp.stack([f_i, c_i, t_i]).astype(jnp.int32)

    def along_ctx(own):
        return [own] + [swap(own, "ctx", p) for p in range(1, nc)]

    ud = lax.all_gather(jnp.concatenate([w_up, w_down], axis=0), ("fsdp", "ctx", "tp"), axis=0, tiled=True)
    ud = ud.reshape(nf * nc, 2, 2, R, FL)

    zq = along_ctx(jnp.concatenate([w_qkv.reshape(R, 3 * C), w_out], axis=1))
    x_in, out_cot = later((x_in, out_cot), zq[0])

    q_pos = jnp.arange(D, dtype=jnp.int32)
    piece, inner = q_pos // R, q_pos % R
    mf = jnp.zeros_like(piece)
    mc = jnp.zeros_like(piece)
    for i, (axis, mask) in enumerate(row_bits):
        bit = ((piece >> i) & 1) * mask
        if axis == "fsdp":
            mf = mf ^ bit
        else:
            mc = mc ^ bit
    true_piece = (f_i ^ mf) * nc + (c_i ^ mc)
    perm = (jnp.arange(D, dtype=jnp.int32)[:, None] == (true_piece * R + inner)[None, :]).astype(BF)
    aligned = R % 16 == 0
    if not aligned:
        order = true_piece[::R]
        sides = jnp.stack([t_i, 1 - t_i])
        ud = ud[order][:, sides].transpose(1, 2, 0, 3, 4).reshape(1, 2, 2, D, FL)

    def pick(a):
        return lax.dynamic_index_in_dim(a, t_i, 0, False)

    x = dot("td,dq->tq", pick(x_in), perm).astype(BF)
    cot = dot("td,dq->tq", pick(out_cot), perm).astype(BF)

    own = jnp.concatenate(zq, 0)
    for bit in chip_bits[:-1]:
        own = jnp.concatenate([own, swap(own, *bit)], 0)
    last_bit = chip_bits[-1]
    by_chip, by_half = swap(own, *last_bit), swap(own, "tp", 1)
    both_one, both_two = swap(by_chip[:, : 2 * C], "tp", 1), swap(by_half[:, 2 * C :], *last_bit)

    seg_ids, land_doc, conv_taps, head_bias, ffn_bias = later((seg_ids, land_doc, conv_taps, head_bias, ffn_bias), zq[0])
    seg = pick(seg_ids).astype(F32)
    doc = pick(land_doc).astype(F32)
    seg_col = seg[:, None]

    def meta(col):
        return jnp.where(jnp.arange(META)[None, :] == 0, col[:, None], 0.0).astype(BF)

    par = jnp.concatenate([conv_taps.reshape(-1), head_bias.reshape(-1), ffn_bias.reshape(-1)])
    par2 = jnp.stack([par, swap(par, "tp", 1)])
    taps = par2[:, : KW * HL].reshape(2, KW, HL).transpose(0, 2, 1).reshape(H, KW)
    hb = par2[:, KW * HL : KW * HL + 2 * C].reshape(2, 2, C).transpose(1, 0, 2).reshape(2, 2 * C)
    fb = par2[:, KW * HL + 2 * C :].reshape(1, 2 * FL)
    vec = hdot("vd,dq->vq", jnp.concatenate([gains, offsets], 0), perm.astype(F32))
    gap = jnp.zeros((H, T - KW), F32)
    taps_rev = taps[:, ::-1]
    row_fwd = jnp.concatenate([taps[:, REACH:], gap, taps[:, :REACH]], 1)
    row_back = jnp.concatenate([taps_rev[:, REACH:], gap, taps_rev[:, :REACH]], 1)

    parts = [own, by_chip, by_half, both_one, both_two]
    parts = parts + [swap(a, *core_bit) for a in parts]
    parts = later(parts, hb, fb, vec, row_fwd, row_back, cot)
    q, k, v, qkv, piece0, vfirst, vlast, w_full = call(
        proj_body,
        [((T, E), BF)] * 3 + [((3, T, E), BF), ((LL, 2 * E + META), BF)] + [((REACH, E + META), BF)] * 2 + [((2, D, 4 * C), BF)],
        x, hb, meta(doc), meta(seg[:REACH] + 1.0), meta(seg[T - REACH :] + 1.0), *parts,
        raw_in=range(5, 15),
        raw_out=(3, 7),
        scratch=[pltpu.VMEM((2, D, 4 * C), BF), pltpu.SemaphoreType.DMA((10,)), pltpu.SemaphoreType.DMA, pltpu.SemaphoreType.DMA((3,))],
        mem=14,
    )

    up = [(i, i + 1) for i in range(nc - 1)]
    down = [(i + 1, i) for i in range(nc - 1)]
    pieces = along_ctx(piece0)
    ktok, ekey, pack, land, land_far = call(
        functools.partial(scores_body, nc),
        [((E, T), BF), ((E, T), BF), ((L, E + META), BF), ((L, 2 * E + META), BF), ((L, 2 * E + META), BF)],
        where, q, k, v, seg_col, *pieces, smem=(0,), far_out=(0, 1, 4), name="scores_body",
    )
    packs = along_ctx(pack)
    vlast, vfirst = later((vlast, vfirst), pack)
    v_before, v_after = lax.ppermute(vlast, "ctx", up), lax.ppermute(vfirst, "ctx", down)
    (conv,) = call(simple(conv_body), [((T, E), BF)], row_fwd, seg_col, v, v_before, v_after, far_in=(0, 1), far_out=(0,))
    kt, mixer, p_all, w_all, pi_all = call(
        simple(newton_body), [((L, E), F32), ((L, E), F32)] + [((NEWTON, L, E), F32)] * 3, land, far_out=range(5), us=5.5, mem=10
    )
    n_pieces = D // R if aligned else 1
    res = call(
        functools.partial(mid_body, nc, n_pieces, row_bits, nc),
        [((T, E), BF), ((L, E), F32), ((L, E), F32), ((L, META), F32), ((T, E), BF), ((T, D), BF), ((T, E), BF)]
        + [((REACH, E), BF)] * 2
        + [((L, E), BF), ((T, D), F32), ((T, D), BF), ((8, D), F32), ((1, 2 * FL), F32)]
        + [((2, D // 2, FL), BF)] * 4,
        where, *packs, mixer, ktok, conv, land_far, x, cot, perm, vec, fb, qkv, w_full, ud,
        us=24.0,
        mem=30,
        smem=(0,),
        far_in=range(1, nc + 10),
        raw_in=(nc + 10, nc + 11, nc + 12),
        far_out=(5,),
        scratch=[
            pltpu.VMEM((2, D, C), BF),
            pltpu.VMEM((2, D, FL), BF),
            pltpu.VMEM((2, D, FL), BF),
            pltpu.VMEM((T, 2 * FL), BF),
            pltpu.VMEM((T, 2 * FL), F32),
            pltpu.VMEM((L, E), F32),
            pltpu.VMEM((1, T, E), BF),
            pltpu.SemaphoreType.DMA((2, 2 * n_pieces)),
            pltpu.SemaphoreType.DMA((2,)),
        ],
        name="mid_body",
    )
    gq, lk_part, lval, land_scale, mixed, y, gm, gfirst, glast, gmix0, grad_first, grad_branch, sums, fb_grad = res[:14]
    keep_up, send_up, keep_down, send_down = res[14:]

    every = slice(None)

    def cores_sum(keep, send):
        got = swap(send, *core_bit)
        for bit in reversed(chip_bits[1:]):
            half = keep.shape[1] // 2
            more = swap(add(keep[:, half:], got[:, half:]), *bit)
            keep, got = add(keep[:, :half], got[:, :half]), more
        return keep, got

    bit = chip_bits[0]
    low_rows, high_rows = slice(0, nc * R), slice(nc * R, 2 * nc * R)

    def one_start(keep, got):
        (other,) = combine([[[(0, (1,)), (1, (1,))]]], keep, got, near=aligned)
        return other, swap(other, "tp", 1)

    def two_start(keep, got):
        (send,) = combine([[[(0, (every, high_rows)), (1, (every, high_rows))]]], keep, got, near=aligned)
        return send, swap(send, *bit)

    def one_next(keep, got, more):
        (send,) = combine([[[(0, (0, high_rows)), (1, (0, high_rows)), (2, (high_rows,))]]], keep, got, more, near=aligned)
        return send, swap(send, *bit)

    def two_next(keep, got, more):
        (send,) = combine([[[(0, (1, low_rows)), (1, (1, low_rows)), (2, (1,))]]], keep, got, more, near=aligned)
        return send, swap(send, "tp", 1)

    def ctx_cuts(one, two):
        plan = []
        for p in range(nc):
            rows = slice(p * R, (p + 1) * R)
            plan.append(
                [
                    [(0, (0, rows)), (1, (0, rows)), (2, (rows,)), (3, (rows,))],
                    [(4, (0, rows)), (5, (0, rows)), (6, (0, rows)), (7, (rows,))],
                ]
            )
        return combine(plan, *one, *two, near=aligned)

    def ctx_total(one, two):
        if not aligned:
            cuts = jnp.stack(ctx_cuts(one, two))
            return cuts[c_i ^ jnp.arange(nc)].reshape(nc * R, -1)
        width = one[2].shape[1]

        def total_body(ready, where_ref, *refs):
            ins, out = refs[:8], refs[8]
            for p in range(nc):
                rows = slice(p * R, (p + 1) * R)
                at = pl.ds(pl.multiple_of((where_ref[1] ^ p) * R, R), R)
                for i in range(2):
                    t = ins[4 * i : 4 * i + 4]
                    third = t[2][rows] if i == 0 else t[2][0, rows]
                    total = t[0][0, rows].astype(F32) + t[1][0, rows].astype(F32) + third.astype(F32) + t[3][rows].astype(F32)
                    out[at, i * width : (i + 1) * width] = total.astype(BF)

        (out,) = call(total_body, [((nc * R, 2 * width), BF)], where, *one, *two, smem=(0,), far_out=(0,), mem=16)
        return out

    def ctx_swap(cuts):
        return [cuts[0]] + [swap(cuts[p], "ctx", p) for p in range(1, nc)]

    def pairs(values):
        while len(values) > 1:
            values = [a + b for a, b in zip(values[::2], values[1::2])]
        return values[0]

    def total(parts):
        return sum(p.astype(F32) for p in parts)

    gmixes = along_ctx(gmix0)
    down2 = cores_sum(keep_down, send_down)
    up2 = cores_sum(keep_up, send_up)
    y_other = swap(y, "tp", 1)
    down2, up2 = later((down2, up2), *gmixes)
    up2 = later(up2, y_other)
    down_sent, down_more = two_start(*down2)
    up_sent, up_more = one_start(*up2)
    res = call(
        functools.partial(key_back_body, nc),
        [((L, E), F32), ((T, E), BF), ((T, E), BF), ((LL, 2 * E), F32)] + [((LL, 2 * E), BF)] * (nc - 1),
        where, *later(gmixes, up_sent, down_sent), mixer, lval, ekey, land_scale, qkv, land_far, lk_part,
        smem=(0,),
        far_in=(nc + 1, nc + 3, nc + 5, nc + 6),
        scratch=[pltpu.VMEM((L, 2 * E), F32)],
        us=3.0,
        mem=12,
        name="key_back_body",
    )
    gmix, gv, gk, own_part = res[:4]
    parts = [own_part] + [swap(a, "ctx", p + 1) for p, a in enumerate(res[4:])]
    glast, gfirst = later((glast, gfirst), own_part)
    g_before, g_after = lax.ppermute(glast, "ctx", up), lax.ppermute(gfirst, "ctx", down)
    own_mix, gvc, tap_all = call(
        functools.partial(back_body, 9), [((LL, 2 * E), F32), ((T, E), BF), ((H, T + 2 * META), F32)],
        land_far, kt, p_all, w_all, pi_all, mixer, gmix, lval, where,
        row_back, seg_col, gm, g_before, g_after, qkv, v_before, v_after,
        smem=(8,),
        far_in=(9, 10, 14, 15, 16, 0, 1, 2, 3, 4, 5),
        scratch=[pltpu.VMEM((L, 2 * E), F32)],
        us=11.0,
        mem=18,
        name="back_body",
    )
    gq, gk, gv, hb_grad, keep1, send1, keep2, send2 = call(
        functools.partial(grad_body, nc),
        [((T, E), BF)] * 3 + [((2, E), F32)] + [((2, D // 2, 2 * C), BF)] * 4,
        *parts, own_mix, gq, later(gk, up_more, down_more), gv, gvc, x, grad_branch, mixed,
        far_in=(nc + 5,),
        us=3.0,
        mem=10,
        name="grad_body",
    )
    down_sent2, down_more2 = two_next(*down2, later(down_more, hb_grad))
    up_sent2, up_more2 = one_next(*up2, later(up_more, hb_grad))
    vo2 = cores_sum(keep2, send2)
    qk2 = cores_sum(keep1, send1)
    vo_sent, vo_more = two_start(*later(vo2, down_sent2, up_sent2))
    qk_sent, qk_more = one_start(*later(qk2, down_sent2, up_sent2))
    rows = -(-KW // 8) * 8 + (7 * D + FL) // META
    rows += -rows % 8
    (small,) = call(
        functools.partial(small_body, rows), [((2, rows, META), F32)], later(tap_all, vo_sent, qk_sent), hb_grad, fb_grad, sums, perm,
        far_in=(0, 4), mem=12, name="small_body",
    )
    halves = [((rows, META), F32)] * 2
    (gx,) = call(
        simple(input_grad_body), [((T, D), BF)], later(gq, small), gk, gv, grad_first, perm, w_full,
        far_in=(4, 5), far_out=(0,), us=4.0, mem=14,
    )
    cuts_ud = [ctx_total((*up2, *later((up_more, up_more2), gx)), (*down2, down_more, down_more2))]
    ctx_ud = [lax.psum_scatter(cuts_ud[0], "ctx", scatter_dimension=0, tiled=True)]
    small_ctx = along_ctx(later(small, *cuts_ud))
    small, small_other = call(simple(fold_body), halves, *small_ctx)
    small_got = [swap(small, *core_bit), swap(small_other, *core_bit)]
    vo_sent2, vo_more2 = two_next(*vo2, later(vo_more, small))
    qk_sent2, qk_more2 = one_next(*qk2, later(qk_more, small))
    small_got = later(small_got, vo_sent2, qk_sent2)
    small, small_other = call(simple(add_body), halves, small, small_got[0], small_other, small_got[1])
    for extra in chip_bits[1:]:
        small, small_other = small + swap(small, *extra), small_other + swap(small_other, *extra)
    small_got = [swap(small, *bit), swap(small_other, "tp", 1), swap_both(small_other, bit[1])]
    cuts_q = ctx_cuts((*qk2, qk_more, later(qk_more2, small)), (*vo2, vo_more, vo_more2))
    ctx_q = ctx_swap(cuts_q)
    gx, small_got, ctx_ud, y, y_other = later((gx, small_got, ctx_ud, y, y_other), *cuts_q)
    ud_grad = total(ctx_ud)
    conv_grad, hb_out, fb_out, gains_out, offsets_out = call(
        simple(small_out_body),
        [((KW, HL), F32), ((2, C), F32), ((1, FL), F32), ((2, D), F32), ((4, D), F32)],
        small, *small_got,
    )


    def place(mine, other):
        first = t_i == 0
        return jnp.stack([jnp.where(first, mine, other), jnp.where(first, other, mine)])

    y_all, x_all = place(y, y_other), place(gx, swap(gx, "tp", 1))
    ud_up, ud_down = ud_grad[:, :FL], ud_grad[:, FL:]
    qo = total(later(ctx_q, y_all, x_all, ud_up, ud_down, conv_grad))

    return (
        y_all,
        x_all,
        qo[:, : 3 * C].reshape(R, 3, C),
        qo[:, 3 * C :],
        ud_up,
        ud_down,
        conv_grad,
        hb_out,
        fb_out[0],
        gains_out,
        offsets_out,
    )


def solution(mesh):
    placed = (
        P("fsdp", "ctx", None),
        P("fsdp", "ctx", None),
        P("fsdp", "ctx"),
        P("fsdp", "ctx"),
        P(("fsdp", "ctx"), None, "tp"),
        P(("fsdp", "ctx"), "tp"),
        P(("fsdp", "ctx"), "tp"),
        P(("fsdp", "ctx"), "tp"),
        P(None, "tp"),
        P(None, "tp"),
        P("tp"),
        P(),
        P(),
    )
    return jax.shard_map(
        local,
        mesh=mesh,
        in_specs=placed,
        out_specs=placed[:2] + placed[4:],
        check_vma=False,
    )
```

```python
import functools

import jax
import jax.numpy as jnp
from jax import lax
from jax.experimental import pallas as pl
from jax.experimental.pallas import tpu as pltpu
from jax.sharding import PartitionSpec as P

HEAD_DIM = 64
KW = 33
REACH = KW // 2
NEWTON = 6
EPS = 1e-05
SCALE = HEAD_DIM**-0.5
BLOCK = 256
PACK = BLOCK // HEAD_DIM
META = 128
BF = jnp.bfloat16
F32 = jnp.float32
HI = lax.Precision.HIGHEST


def dot(spec, a, b):
    return jnp.einsum(spec, a, b, preferred_element_type=F32)


def hdot(spec, a, b):
    return jnp.einsum(spec, a, b, preferred_element_type=F32, precision=HI)


def swap(a, axis, mask):
    return lax.ppermute(a, axis, [(i, i ^ mask) for i in range(lax.axis_size(axis))])


def swap_both(a, mask):
    nf = lax.axis_size("fsdp")
    return lax.ppermute(a, ("fsdp", "tp"), [(2 * i + j, 2 * (i ^ mask) + (j ^ 1)) for i in range(nf) for j in range(2)])


def add(*terms):
    return sum(t.astype(F32) for t in terms).astype(BF)


def later(value, *after):
    return lax.optimization_barrier((value, after))[0]


def nn(a, b):
    return lax.dot_general(a, b, (((1,), (0,)), ((), ())), preferred_element_type=F32)


def nt(a, b):
    return lax.dot_general(a, b, (((1,), (1,)), ((), ())), preferred_element_type=F32)


def tn(a, b):
    return lax.dot_general(a, b, (((0,), (0,)), ((), ())), preferred_element_type=F32)


def lane_head(rows):
    return lax.broadcasted_iota(jnp.int32, (rows, BLOCK), 1) // HEAD_DIM


def expand(r):
    head = lane_head(HEAD_DIM)
    wide = r.astype(F32)
    return jnp.concatenate([jnp.where(head == i, wide, 0.0) for i in range(PACK)], 0).astype(r.dtype)


def compress(full):
    head = lane_head(HEAD_DIM)
    out = jnp.zeros((HEAD_DIM, BLOCK), F32)
    for i in range(PACK):
        out = jnp.where(head == i, full[i * HEAD_DIM : (i + 1) * HEAD_DIM], out)
    return out


def split(a):
    high = a.astype(BF)
    return high, (a - high.astype(F32)).astype(BF)


def wide_of(b):
    high, low = split(b)
    return expand(high), expand(low)


def tall_of(a):
    high, low = split(a)
    return jnp.concatenate([high, low], 0)


def times(a, b):
    both = nn(a, b[0])
    return both[:HEAD_DIM] + both[HEAD_DIM:] + nn(a[:HEAD_DIM], b[1])


def times_both(a, c, b):
    high = nn(jnp.concatenate([a, c], 0), b[0])
    low = nn(jnp.concatenate([a[:HEAD_DIM], c[:HEAD_DIM]], 0), b[1])
    parts = [high[i * HEAD_DIM : (i + 1) * HEAD_DIM] for i in range(4)]
    return parts[0] + parts[1] + low[:HEAD_DIM], parts[2] + parts[3] + low[HEAD_DIM:]


def mm3(a, b):
    return times(tall_of(a), wide_of(b))


def tn3(a, b):
    ah, al = split(a)
    bh, bl = split(b)
    return compress(tn(ah, bh) + tn(al, bh) + tn(ah, bl))


def eye_row():
    row = lax.broadcasted_iota(jnp.int32, (HEAD_DIM, BLOCK), 0)
    lane = lax.broadcasted_iota(jnp.int32, (HEAD_DIM, BLOCK), 1)
    return jnp.where(row == lane % HEAD_DIM, 1.0, 0.0)


def head_total(a):
    head = lane_head(1)
    col = jnp.sum(a, axis=0, keepdims=True)
    out = jnp.zeros_like(col)
    for i in range(PACK):
        one = jnp.sum(jnp.where(head == i, col, 0.0), axis=1, keepdims=True)
        out = jnp.where(head == i, one, out)
    return out


def heads_sum(a):
    parts = a.reshape(PACK, HEAD_DIM, a.shape[1])
    return jnp.broadcast_to(jnp.sum(parts, axis=1, keepdims=True), parts.shape).reshape(a.shape)


def heads_max(a):
    parts = a.reshape(PACK, HEAD_DIM, a.shape[1])
    return jnp.broadcast_to(jnp.max(parts, axis=1, keepdims=True), parts.shape).reshape(a.shape)


def tall(mask):
    return jnp.concatenate([mask] * PACK, 0) > 0.5


def group(g):
    return slice(g * BLOCK, (g + 1) * BLOCK)


def as_row(col, lanes, shift=0, flip=False):
    n = col.shape[0]
    row = lax.broadcasted_iota(jnp.int32, (n, lanes), 0)
    lane = lax.broadcasted_iota(jnp.int32, (n, lanes), 1) - shift
    hit = (row + lane == n - 1) if flip else (row == lane)
    return jnp.sum(jnp.where(hit, col, 0.0), axis=0, keepdims=True)


def rows_at(ref, index, count):
    return ref[pl.ds(pl.multiple_of(index * count, count), count), :]


def call(body, outs, *args, us=2.0, raw_in=(), raw_out=(), far_in=(), far_out=(), smem=(), scratch=(), mem=8, name=None):
    n, m = len(args), len(outs)
    far_in, far_out = list(far_in), list(far_out)

    def space(outside):
        return pltpu.HBM if outside else pltpu.VMEM

    ins = [space(i in raw_in or i in far_in) for i in range(n)]
    res = [space(i in raw_out or i in far_out) for i in range(m)]

    def inner(*refs):
        given, made, extra = list(refs[:n]), list(refs[n : n + m]), refs[n + m :]
        vm_in, extra = extra[: len(far_in)], extra[len(far_in) :]
        vm_out, extra = extra[: len(far_out)], extra[len(far_out) :]
        sem_in, sem_out, rest = extra[0], extra[1], extra[2:]
        loads = [pltpu.make_async_copy(given[i], v, sem_in.at[j]) for j, (i, v) in enumerate(zip(far_in, vm_in))]
        stores = [pltpu.make_async_copy(v, made[i], sem_out.at[j]) for j, (i, v) in enumerate(zip(far_out, vm_out))]
        for c in loads:
            c.start()
        for i, v in zip(far_in, vm_in):
            given[i] = v
        for i, v in zip(far_out, vm_out):
            made[i] = v

        def ready(first=0, last=len(loads)):
            for c in loads[first:last]:
                c.wait()

        body(ready, *given, *made, *rest)
        for c in stores:
            c.start()
        for c in stores:
            c.wait()

    return pl.pallas_call(
        inner,
        out_shape=[r(*o) for r, o in zip(res, outs)],
        in_specs=[pl.BlockSpec(memory_space=pltpu.SMEM if i in smem else ins[i]) for i in range(n)],
        out_specs=[pl.BlockSpec(memory_space=r) for r in res],
        scratch_shapes=[pltpu.VMEM(args[i].shape, args[i].dtype) for i in far_in]
        + [pltpu.VMEM(*outs[i]) for i in far_out]
        + [pltpu.SemaphoreType.DMA((max(len(far_in), 1),)), pltpu.SemaphoreType.DMA((max(len(far_out), 1),))]
        + list(scratch),
        compiler_params=pltpu.CompilerParams(vmem_limit_bytes=mem << 20),
        cost_estimate=pl.CostEstimate(flops=int(us * 1e7), bytes_accessed=1024, transcendentals=0),
        name=name or body.__name__,
    )(*[a if i in smem else pltpu.with_memory_space_constraint(a, ins[i]) for i, a in enumerate(args)])


def combine(plan, *arrays, near=True, far_in=()):
    shapes = [
        (arrays[parts[0][0][0]][parts[0][0][1]].shape[:-1], [arrays[p[0][0]][p[0][1]].shape[-1] for p in parts]) for parts in plan
    ]
    if not near:
        return [
            jnp.concatenate([add(*[arrays[i][at] for i, at in terms]) for terms in parts], -1) if len(parts) > 1
            else add(*[arrays[i][at] for i, at in parts[0]])
            for parts in plan
        ]

    def sum_body(ready, *refs):
        ready()
        ins, res = refs[: len(arrays)], refs[len(arrays) :]
        for parts, (_, widths), out in zip(plan, shapes, res):
            col = 0
            for terms, width in zip(parts, widths):
                total = sum(ins[i][at].astype(F32) for i, at in terms).astype(BF)
                out[..., col : col + width] = total
                col += width

    return call(sum_body, [(lead + (sum(w),), BF) for lead, w in shapes], *arrays, far_in=far_in, mem=16)


def simple(body):
    def run(ready, *refs):
        ready()
        body(*refs)

    run.__name__ = body.__name__
    return run


def proj_body(ready, x_ref, hb_ref, doc_ref, first_ref, last_ref, *refs):
    parts, refs = refs[:10], refs[10:]
    q_ref, k_ref, v_ref, qkv_hbm, piece_ref, vfirst_ref, vlast_ref, w_hbm, w_ref, sem, sem_w, sem_f = refs
    rows, wide = parts[0].shape
    loads = []
    for i, part in enumerate(parts):
        kind, core = i % 5, i // 5
        side, chip = (kind > 1) * 1, (kind in (1, 3, 4)) * 1
        cols = pl.ds((kind == 4) * wide // 2, part.shape[1])
        at = pl.ds((2 * core + chip) * rows, rows)
        loads.append(pltpu.make_async_copy(part, w_ref.at[side, at, cols], sem.at[i]))
    for c in loads:
        c.start()
    ready()
    T, D = x_ref.shape
    C = D // 2
    x = x_ref[...]
    LL = piece_ref.shape[0]
    seg_len = T // LL
    row = lax.broadcasted_iota(jnp.int32, (LL, T), 0)
    col = lax.broadcasted_iota(jnp.int32, (LL, T), 1)
    mean = jnp.where(col // seg_len == row, 1.0 / seg_len, 0.0).astype(BF)
    store = pltpu.make_async_copy(w_ref, w_hbm, sem_w)
    for c in loads:
        c.wait()
    store.start()
    for side in range(2):
        cols = slice(side * C, (side + 1) * C)
        q = (nn(x, w_ref[side, :, :C]) + hb_ref[0:1, cols]).astype(BF)
        k = nn(x, w_ref[side, :, C : 2 * C]).astype(BF)
        v = (nn(x, w_ref[side, :, 2 * C : 3 * C]) + hb_ref[1:2, cols]).astype(BF)
        q_ref[:, cols] = q
        k_ref[:, cols] = k
        v_ref[:, cols] = v
        vfirst_ref[:, cols] = v[:REACH]
        vlast_ref[:, cols] = v[T - REACH :]
        piece_ref[:, cols] = nn(mean, q).astype(BF)
        piece_ref[:, D + side * C : D + (side + 1) * C] = nn(mean, k).astype(BF)
    piece_ref[:, 2 * D :] = doc_ref[...]
    vfirst_ref[:, D:] = first_ref[...]
    vlast_ref[:, D:] = last_ref[...]
    extra = [pltpu.make_async_copy(r, qkv_hbm.at[i], sem_f.at[i]) for i, r in enumerate((q_ref, k_ref, v_ref))]
    for c in extra:
        c.start()
    for c in extra:
        c.wait()
    store.wait()


def scores_body(n, ready, where_ref, q_ref, k_ref, v_ref, seg_ref, *refs):
    pieces, (ktok_ref, ekey_ref, pack_ref, land_ref, land_far_ref) = refs[:n], refs[n:]
    ready()
    LL = pieces[0].shape[0]
    E = q_ref.shape[1]
    for p in range(n):
        at = pl.multiple_of((where_ref[1] ^ p) * LL, LL)
        land_ref[pl.ds(at, LL), :] = pieces[p][...]
    doc = land_ref[:, 2 * E : 2 * E + 1].astype(F32)
    land_far_ref[...] = land_ref[...]
    allowed = tall((doc == as_row(seg_ref[...], q_ref.shape[0])).astype(F32))
    lane = lax.broadcasted_iota(jnp.int32, (HEAD_DIM, META), 1)
    stats = jnp.zeros((HEAD_DIM, META), F32)
    heads = E // HEAD_DIM
    for g in range(E // BLOCK):
        s = group(g)
        lq, lk = land_ref[:, s], land_ref[:, E + g * BLOCK : E + (g + 1) * BLOCK]
        z = nt(expand(lk), q_ref[:, s]) * SCALE
        z = jnp.where(allowed, z, -1e30)
        e = jnp.where(allowed, jnp.exp(z - heads_max(z)), 0.0)
        ktok_ref[s, :] = (e / heads_sum(e)).astype(BF)
        z = nt(expand(lq), k_ref[:, s]) * SCALE
        z = jnp.where(allowed, z, -1e30)
        top = jnp.max(z, axis=1, keepdims=True)
        e = jnp.where(allowed, jnp.exp(z - top), 0.0)
        total = jnp.sum(e, axis=1, keepdims=True)
        low = e.astype(BF)
        ekey_ref[s, :] = low
        pack_ref[:, s] = compress(nn(low, v_ref[:, s])).astype(BF)
        for i in range(PACK):
            h = g * PACK + i
            rows = slice(i * HEAD_DIM, (i + 1) * HEAD_DIM)
            stats = jnp.where(lane == h, top[rows], stats)
            stats = jnp.where(lane == heads + h, total[rows], stats)
    first = stats.astype(BF).astype(F32)
    second = (stats - first).astype(BF).astype(F32)
    third = stats - first - second
    pack_ref[:, E:] = (first + pltpu.roll(second, 2 * heads, 1) + pltpu.roll(third, 4 * heads, 1)).astype(BF)


def newton_body(land_ref, kt_ref, mixer_ref, p_ref, w_ref, pi_ref):
    E = kt_ref.shape[1]
    eye = eye_row()
    doc = land_ref[:, 2 * E : 2 * E + 1].astype(F32)
    allowed = jnp.concatenate([(doc == as_row(doc, HEAD_DIM)).astype(F32)] * PACK, 1) > 0.5
    groups = [group(g) for g in range(E // BLOCK)]
    kts, invs, ps, pis = [], [], [], []
    for s in groups:
        lq, lk = land_ref[:, s], land_ref[:, E + s.start : E + s.stop]
        z = nt(lk, expand(lq)) * SCALE
        z = jnp.where(allowed, z, -1e30)
        e = jnp.where(allowed, jnp.exp(z - jnp.max(z, axis=0, keepdims=True)), 0.0)
        kt = e / jnp.sum(e, axis=0, keepdims=True)
        kts.append(kt)
        invs.append(1.0 / head_total(kt * kt))
        kt_ref[:, s] = kt
    ps = [tn3(kt, kt) * inv for kt, inv in zip(kts, invs)]
    for step in range(NEWTON):
        for s, p in zip(groups, ps):
            p_ref[step, :, s] = p
        talls = [tall_of(p) for p in ps]
        p2s = [times(t, wide_of(p)) for t, p in zip(talls, ps)]
        ws = [0.25 * (13.0 * eye - 15.0 * p + mm3(p2, 7.0 * eye - p)) for p, p2 in zip(ps, p2s)]
        wides = [wide_of(w) for w in ws]
        if step == 0:
            ps, pis = [times(t, w) for t, w in zip(talls, wides)], ws
        elif step < NEWTON - 1:
            both = [times_both(t, tall_of(pi), w) for t, pi, w in zip(talls, pis, wides)]
            ps, pis = [b[0] for b in both], [b[1] for b in both]
        else:
            pis = [times(tall_of(pi), w) for pi, w in zip(pis, wides)]
        for s, w, pi in zip(groups, ws, pis):
            w_ref[step, :, s] = w
            pi_ref[step, :, s] = pi
    for s, kt, pi, inv in zip(groups, kts, pis, invs):
        mixer_ref[:, s] = mm3(kt, pi) * inv


def newton_back_body(land_ref, kt_ref, p_ref, w_ref, pi_ref, mixer_ref, gmix_ref, lval_ref, where_ref, own_ref, full_ref):
    E = kt_ref.shape[1]
    groups = [group(g) for g in range(E // BLOCK)]
    many = range(len(groups))
    kts = [kt_ref[:, s] for s in groups]
    invs = [1.0 / head_total(kt * kt) for kt in kts]
    grads = []
    for s in groups:
        gh, gl = split(gmix_ref[:, s])
        vh, vl = split(lval_ref[:, s])
        wide = expand(vh)
        grads.append(nt(gh, wide) + nt(gl, wide) + nt(gh, expand(vl)))
    d_pis = [tn3(kts[i], grads[i]) * invs[i] for i in many]
    d_kts = [mm3(grads[i], pi_ref[NEWTON - 1, :, groups[i]]) * invs[i] for i in many]
    d_cs = [-head_total(grads[i] * mixer_ref[:, groups[i]]) * invs[i] for i in many]
    d_ps = None
    for step in reversed(range(NEWTON)):
        ps = [p_ref[step, :, s] for s in groups]
        ws = [w_ref[step, :, s] for s in groups]
        p_tall = [tall_of(p) for p in ps]
        p_wide = [wide_of(p) for p in ps]
        d_ws = [mm3(pi_ref[step - 1, :, groups[i]], d_pis[i]) for i in many] if step else d_pis
        w_wide = [wide_of(w) for w in ws] if step or d_ps is not None else None
        if d_ps is not None:
            d_ws = [d_ws[i] + times(p_tall[i], wide_of(d_ps[i])) for i in many]
            if step:
                both = [times_both(tall_of(d_ps[i]), tall_of(d_pis[i]), w_wide[i]) for i in many]
                d_ps, d_pis = [b[0] for b in both], [b[1] for b in both]
            else:
                d_ps = [times(tall_of(d_ps[i]), w_wide[i]) for i in many]
        elif step:
            d_pis = [times(tall_of(d_pis[i]), w_wide[i]) for i in many]
        ones = [times(p_tall[i], wide_of(d_ws[i])) for i in many]
        twos = [ones[i] + times(tall_of(d_ws[i]), p_wide[i]) for i in many]
        more = [
            0.25
            * (7.0 * twos[i] - 15.0 * d_ws[i] - times(p_tall[i], wide_of(ones[i])) - times(tall_of(twos[i]), p_wide[i]))
            for i in many
        ]
        d_ps = more if d_ps is None else [d_ps[i] + more[i] for i in many]
    for i in many:
        s, kt, inv = groups[i], kts[i], invs[i]
        lq, lk = land_ref[:, s], land_ref[:, E + s.start : E + s.stop]
        d_c = d_cs[i] - head_total(d_ps[i] * p_ref[0, :, s]) * inv
        kh, kl = split(kt)
        sh, sl = split(d_ps[i] * inv)
        wide = expand(sh)
        thin = expand(sl)
        d_kt = d_kts[i] + nn(kh, wide) + nn(kl, wide) + nn(kh, thin) + nt(kh, wide) + nt(kl, wide) + nt(kh, thin)
        d_kt = d_kt + 2.0 * d_c * kt
        dz = kt * (d_kt - jnp.sum(kt * d_kt, axis=0, keepdims=True)) * SCALE
        zh, zl = split(dz)
        wide = expand(lq)
        full_ref[:, E + s.start : E + s.stop] = nn(zh, wide) + nn(zl, wide)
        full_ref[:, s] = compress(tn(zh, lk) + tn(zl, lk))
    own_ref[...] = rows_at(full_ref, where_ref[1], own_ref.shape[0])


def mix_part(packs, mixer_ref, ktok_ref, conv_ref, mixing_ref, lval_ref, scale_ref, mixed_ref):
    E = mixer_ref.shape[1]
    heads = E // HEAD_DIM
    stats = []
    for p in packs:
        tile = p[:, E:].astype(F32)
        stats.append(tile + pltpu.roll(tile, 128 - 2 * heads, 1) + pltpu.roll(tile, 128 - 4 * heads, 1))
    top = stats[0]
    for t in stats[1:]:
        top = jnp.maximum(top, t)
    lane = lax.broadcasted_iota(jnp.int32, (HEAD_DIM, 128), 1)
    weights = [jnp.where(lane < heads, jnp.exp(jnp.minimum(t - top, 0.0)), 0.0) for t in stats]
    total = sum(w * pltpu.roll(t, 128 - heads, 1) for w, t in zip(weights, stats))
    total = jnp.where(lane < heads, total, 1.0)
    weights = [w / total for w in weights]
    scale_ref[...] = weights[0]
    head = lane_head(HEAD_DIM)
    for g in range(E // BLOCK):
        s = group(g)
        lval = jnp.zeros((HEAD_DIM, BLOCK), F32)
        for w, p in zip(weights, packs):
            spread = jnp.zeros((HEAD_DIM, BLOCK), F32)
            for i in range(PACK):
                h = g * PACK + i
                spread = jnp.where(head == i, w[:, h : h + 1], spread)
            lval = lval + spread * p[:, s].astype(F32)
        lval_ref[:, s] = lval
        mixing = mm3(mixer_ref[:, s], lval)
        mixing_ref[:, s] = mixing
        mh, ml = split(mixing)
        tok = ktok_ref[s, :]
        mixed_ref[:, s] = (tn(tok, expand(mh)) + tn(tok, expand(ml)) + conv_ref[:, s].astype(F32)).astype(BF)


def norm_part(r):
    center = r - jnp.mean(r, axis=1, keepdims=True)
    inv = lax.rsqrt(jnp.mean(center * center, axis=1, keepdims=True) + EPS)
    return center * inv, inv


def norm_back(e, n, inv, gain):
    eg = e * gain
    return (eg - jnp.mean(eg, axis=1, keepdims=True) - n * jnp.mean(eg * n, axis=1, keepdims=True)) * inv


def pair_pick(first, second):
    lane = lax.broadcasted_iota(jnp.int32, first.shape, 1)
    return jnp.where(lane < HEAD_DIM, first, second)


def band_apply(row, band, edge, a_ref, rim_ref, cols):
    T = a_ref.shape[0]
    wide = pltpu.roll(jnp.broadcast_to(row, (T, T)), 0, 1, stride=1, stride_axis=0)
    wide = jnp.where(band, wide, 0.0).astype(BF)
    short = jnp.broadcast_to(row, (REACH, T))
    rims = jnp.concatenate(
        [
            pltpu.roll(short, REACH, 1, stride=1, stride_axis=0),
            pltpu.roll(short, 0, 1, stride=1, stride_axis=0),
        ],
        0,
    )[:, :128]
    rims = jnp.where(edge, rims, 0.0).astype(BF)
    return nn(wide, a_ref[:, cols]), nn(rims, rim_ref[:, cols])


def conv_pair(rows_ref, band, edge, a_ref, rim_ref, out_ref, j):
    T = a_ref.shape[0]
    cols = slice(j * 128, (j + 1) * 128)
    one, one_rim = band_apply(rows_ref[2 * j : 2 * j + 1, :], band, edge, a_ref, rim_ref, cols)
    two, two_rim = band_apply(rows_ref[2 * j + 1 : 2 * j + 2, :], band, edge, a_ref, rim_ref, cols)
    both, rim = pair_pick(one, two), pair_pick(one_rim, two_rim)
    out_ref[:REACH, cols] = (both[:REACH] + rim[:REACH]).astype(BF)
    out_ref[REACH : T - REACH, cols] = both[REACH : T - REACH].astype(BF)
    out_ref[T - REACH :, cols] = (both[T - REACH :] + rim[REACH:]).astype(BF)


def band_of(col_ref, flip):
    T = col_ref.shape[0]
    a = lax.broadcasted_iota(jnp.int32, (T, T), 0)
    b = lax.broadcasted_iota(jnp.int32, (T, T), 1)
    gap = (T - 1 - b - a) if flip else (b - a)
    return (jnp.abs(gap) <= REACH) & (as_row(col_ref[...], T, 0, flip) == col_ref[...])


def edge_of(col_ref, before, after, flip):
    T = col_ref.shape[0]
    row = lax.broadcasted_iota(jnp.int32, (REACH, META), 0)
    lane = lax.broadcasted_iota(jnp.int32, (REACH, META), 1)
    shift = 0 if flip else REACH
    i = (REACH - 1 - lane) if flip else lane
    j = (REACH - 1 - lane) if flip else lane - REACH
    low = (i >= row) & (i < REACH) & (as_row(before, META, 0, flip) == col_ref[:REACH] + 1.0)
    high = (j <= row) & (j >= 0) & (as_row(after, META, shift, flip) == col_ref[T - REACH :] + 1.0)
    return jnp.concatenate([low.astype(F32), high.astype(F32)], 0) > 0.5


def rim_of(before_ref, after_ref, E):
    return jnp.concatenate([before_ref[:, :E], after_ref[:, :E], jnp.zeros((META - 2 * REACH, E), BF)], 0)


def conv_body(rows_ref, seg_col_ref, v_ref, before_ref, after_ref, out_ref):
    E = v_ref.shape[1]
    band = band_of(seg_col_ref, False)
    edge = edge_of(seg_col_ref, before_ref[:, E : E + 1].astype(F32), after_ref[:, E : E + 1].astype(F32), False)
    rim = rim_of(before_ref, after_ref, E)
    for j in range(E // 128):
        conv_pair(rows_ref, band, edge, v_ref, rim, out_ref, j)


def conv_back_body(
    rows_ref, seg_col_ref, g_ref, g_before_ref, g_after_ref, qkv_ref, before_ref, after_ref, out_ref, tap_ref
):
    T, E = g_ref.shape
    v_ref = qkv_ref.at[2]
    seg_before, seg_after = before_ref[:, E : E + 1].astype(F32), after_ref[:, E : E + 1].astype(F32)
    band = band_of(seg_col_ref, False)
    edge = edge_of(seg_col_ref, seg_before, seg_after, False)
    band_rev = band_of(seg_col_ref, True)
    edge_rev = edge_of(seg_col_ref, seg_before, seg_after, True)
    g_rim = rim_of(g_before_ref, g_after_ref, E)
    v_rim = rim_of(before_ref, after_ref, E)
    a = lax.broadcasted_iota(jnp.int32, (T, T), 0)
    b = lax.broadcasted_iota(jnp.int32, (T, T), 1)
    flip = jnp.where(a + b == T - 1, 1.0, 0.0).astype(BF)
    a = lax.broadcasted_iota(jnp.int32, (META, META), 0)
    b = lax.broadcasted_iota(jnp.int32, (META, META), 1)
    flip_before = jnp.where(a + b == REACH - 1, 1.0, 0.0).astype(BF)
    flip_after = jnp.where((a + b == 2 * REACH - 1) & (a < REACH), 1.0, 0.0).astype(BF)
    for j in range(E // 128):
        cols = slice(j * 128, (j + 1) * 128)
        conv_pair(rows_ref, band, edge, g_ref, g_rim, out_ref, j)
        v_rev = nn(flip, v_ref[:, cols]).astype(BF)
        before = nn(flip_before, v_rim[:, cols]).astype(BF)
        after = nn(flip_after, v_rim[:, cols]).astype(BF)
        g = g_ref[:, cols].astype(F32)
        lane = lax.broadcasted_iota(jnp.int32, g.shape, 1)
        for i in range(2):
            mine = jnp.where((lane < HEAD_DIM) == (i == 0), g, 0.0).astype(BF)
            h = 2 * j + i
            cross = jnp.where(band_rev, nt(mine, v_rev), 0.0)
            cross = pltpu.roll(cross, 0, 1, stride=1, stride_axis=0)
            tap_ref[h : h + 1, :T] = jnp.sum(cross, axis=0, keepdims=True)
            low = jnp.where(edge_rev[:REACH], nt(mine[:REACH], before), 0.0)
            low = pltpu.roll(low, 0, 1, stride=1, stride_axis=0)
            tap_ref[h : h + 1, T : T + META] = jnp.sum(low, axis=0, keepdims=True)
            high = jnp.where(edge_rev[REACH:], nt(mine[T - REACH :], after), 0.0)
            high = pltpu.roll(high, 0, 1, stride=1, stride_axis=0)
            tap_ref[h : h + 1, T + META :] = jnp.sum(high, axis=0, keepdims=True)


def piece_at(where_ref, p, row_bits, nc):
    f, c = where_ref[0], where_ref[1]
    for i, (axis, mask) in enumerate(row_bits):
        if p >> i & 1:
            if axis == "fsdp":
                f = f ^ mask
            else:
                c = c ^ mask
    return f * nc + c


def mid_body(n, pieces, row_bits, nc, ready, where_ref, *refs):
    packs, refs = refs[:n], refs[n:]
    mixer_ref, ktok_ref, conv_ref, land_ref, x_ref, cot_ref, perm_ref, vec_ref, fb_ref, qkv_hbm, w_hbm, ud_hbm = refs[:12]
    refs = refs[12:]
    gq_ref, lk_ref, lval_ref, scale_ref, mixed_ref, y_ref, gm_ref, gfirst_ref, glast_ref, gmix_ref, first_ref, gb_ref, sums_ref, fbg_ref = refs[:14]
    ku_ref, su_ref, kd_ref, sd_ref = refs[14:18]
    wo, wu, wd, act_ref, dg_ref, mixing_ref, q_ref, sem_in, sem_o = refs[18:]
    T, D = x_ref.shape
    half = D // 2
    FL = wu.shape[2]
    R = D // pieces
    loads = []
    for side in range(2):
        ups, downs = [], []
        for p in range(pieces):
            if pieces > 1:
                at, half_at = piece_at(where_ref, p, row_bits, nc), where_ref[2] ^ side
            else:
                at, half_at = 0, side
            rows = pl.ds(p * R, R)
            k = side * pieces + p
            ups.append(pltpu.make_async_copy(ud_hbm.at[at, half_at, 0], wu.at[side, rows], sem_in.at[0, k]))
            downs.append(pltpu.make_async_copy(ud_hbm.at[at, half_at, 1], wd.at[side, rows], sem_in.at[1, k]))
        loads.append((ups, downs))
    load_o = pltpu.make_async_copy(w_hbm.at[:, :, pl.ds(3 * half, half)], wo, sem_o.at[0])
    load_q = pltpu.make_async_copy(qkv_hbm.at[pl.ds(0, 1)], q_ref, sem_o.at[1])
    load_o.start()
    load_q.start()
    for ups, downs in loads:
        for c in ups + downs:
            c.start()
    ready()
    mix_part(packs, mixer_ref, ktok_ref, conv_ref, mixing_ref, lval_ref, scale_ref, mixed_ref)
    gain0, gain1 = vec_ref[0:1], vec_ref[1:2]
    mixed = mixed_ref[...]
    load_o.wait()
    branch = nt(mixed[:, :half], wo[0]) + nt(mixed[:, half:], wo[1])
    n1, inv1 = norm_part(x_ref[...].astype(F32) + branch + vec_ref[4:5])
    hidden = n1 * gain0 + vec_ref[2:3]
    low = hidden.astype(BF)
    step = FL // 2
    ffn = jnp.zeros((T, D), F32)
    cubic, lead = 0.044715, 0.7978845608028654
    for side in range(2):
        for c in loads[side][0]:
            c.wait()
        for j in range(FL // step):
            cols = slice(j * step, (j + 1) * step)
            at = slice(side * FL + j * step, side * FL + (j + 1) * step)
            u = nn(low, wu[side, :, cols]) + fb_ref[:, at]
            sq = u * u
            t = jnp.tanh(lead * u * (1.0 + cubic * sq))
            act = (0.5 * u * (1.0 + t)).astype(BF)
            dg_ref[:, at] = 0.5 * (1.0 + t) + 0.5 * u * (1.0 - t * t) * lead * (1.0 + 3.0 * cubic * sq)
            act_ref[:, at] = act
            if j == 0:
                for c in loads[side][1]:
                    c.wait()
            ffn = ffn + nt(act, wd[side, :, cols])
    n2, inv2 = norm_part(hidden + ffn + vec_ref[5:6])
    y_ref[...] = nt((n2 * gain1 + vec_ref[3:4]).astype(BF), perm_ref[...]).astype(BF)
    cot = cot_ref[...].astype(F32)
    second = norm_back(cot, n2, inv2, gain1)
    sums_ref[1:2] = jnp.sum(cot * n2, axis=0, keepdims=True)
    sums_ref[3:4] = jnp.sum(cot, axis=0, keepdims=True)
    gf = second.astype(BF)
    sums_ref[5:6] = jnp.sum(gf.astype(F32), axis=0, keepdims=True)
    gt = gf.astype(F32).T.astype(BF)
    ht = low.astype(F32).T.astype(BF)
    gh = second
    for side in range(2):
        for j in range(FL // step):
            cols = slice(j * step, (j + 1) * step)
            at = slice(side * FL + j * step, side * FL + (j + 1) * step)
            gu = (nn(gf, wd[side, :, cols]) * dg_ref[:, at]).astype(BF)
            fbg_ref[:, at] = jnp.sum(gu.astype(F32), axis=0, keepdims=True)
            ku_ref[side, :, cols] = nn(ht[:half], gu).astype(BF)
            su_ref[side, :, cols] = nn(ht[half:], gu).astype(BF)
            gh = gh + nt(gu, wu[side, :, cols])
            kd_ref[side, :, cols] = nn(gt[:half], act_ref[:, at]).astype(BF)
            sd_ref[side, :, cols] = nn(gt[half:], act_ref[:, at]).astype(BF)
    first = norm_back(gh, n1, inv1, gain0)
    sums_ref[0:1] = jnp.sum(gh * n1, axis=0, keepdims=True)
    sums_ref[2:3] = jnp.sum(gh, axis=0, keepdims=True)
    first_ref[...] = first
    low = first.astype(BF)
    gb_ref[...] = low
    sums_ref[4:5] = jnp.sum(low.astype(F32), axis=0, keepdims=True)
    sums_ref[6:8] = jnp.zeros((2, D), F32)
    for side in range(2):
        gm = nn(low, wo[side]).astype(BF)
        cols = slice(side * half, (side + 1) * half)
        gm_ref[:, cols] = gm
        gfirst_ref[:, cols] = gm[:REACH]
        glast_ref[:, cols] = gm[T - REACH :]
    load_q.wait()
    for g in range(D // BLOCK):
        s = group(g)
        gm = gm_ref[:, s]
        gmix_ref[:, s] = compress(nn(ktok_ref[s, :], gm)).astype(BF)
        mh, ml = split(mixing_ref[:, s])
        gk = nt(expand(mh), gm) + nt(expand(ml), gm)
        tok = ktok_ref[s, :].astype(F32)
        gz = (tok * (gk - heads_sum(tok * gk)) * SCALE).astype(BF)
        gq_ref[:, s] = tn(gz, expand(land_ref[:, D + s.start : D + s.stop])).astype(BF)
        lk_ref[:, s] = compress(nn(gz, q_ref[0, :, s]))


def key_back_body(n, ready, where_ref, *refs):
    gmixes, refs = refs[:n], refs[n:]
    mixer_ref, lval_ref, ekey_ref, scale_ref, qkv_ref, land_ref, lk_ref = refs[:7]
    gmix_ref, gv_ref, gk_ref, own_ref = refs[7:11]
    sends, full_ref = refs[11:-1], refs[-1]
    k_ref, v_ref = qkv_ref.at[1], qkv_ref.at[2]
    ready()
    E = v_ref.shape[1]
    for g in range(E // BLOCK):
        s = group(g)
        gmix = gmixes[0][:, s].astype(F32)
        for other in gmixes[1:]:
            gmix = gmix + other[:, s].astype(F32)
        gmix_ref[:, s] = gmix
        lval = lval_ref[:, s]
        glval = tn3(mixer_ref[:, s], gmix)
        gh, gl = split(glval)
        wide = expand(gh)
        v = v_ref[:, s]
        gkk = nt(wide, v) + nt(expand(gl), v)
        center = jnp.sum(expand(glval * lval), axis=1, keepdims=True)
        scale = jnp.concatenate([scale_ref[:, g * PACK + i : g * PACK + i + 1] for i in range(PACK)], 0)
        kk = ekey_ref[s, :].astype(F32) * scale
        gz = (kk * (gkk - center) * SCALE).astype(BF)
        gv_ref[:, s] = tn(kk.astype(BF), wide).astype(BF)
        gk_ref[:, s] = tn(gz, expand(land_ref[:, s])).astype(BF)
        full_ref[:, s] = compress(nn(gz, k_ref[:, s]))
    full_ref[:, E:] = lk_ref[...]
    LL = own_ref.shape[0]
    own_ref[...] = rows_at(full_ref, where_ref[1], LL)
    for p, ref in enumerate(sends):
        ref[...] = rows_at(full_ref, where_ref[1] ^ (p + 1), LL).astype(BF)


def grad_body(n, ready, *refs):
    owns, refs = refs[: n + 1], refs[n + 1 :]
    gqt_ref, gkt_ref, gvk_ref, gvc_ref, x_ref, gb_ref, mixed_ref = refs[:7]
    gq_ref, gk_ref, gv_ref, hbg_ref = refs[7:11]
    outs = refs[11:15]
    ready()
    T, D = x_ref.shape
    half = D // 2
    own = owns[0][...]
    for other in owns[1:]:
        own = own + other[...].astype(F32)
    LL = own.shape[0]
    seg_len = T // LL
    own = own * (1.0 / seg_len)
    spread = jnp.broadcast_to(own[:, None, :], (LL, seg_len, 2 * D)).reshape(T, 2 * D)
    gq = (gqt_ref[...].astype(F32) + spread[:, :D]).astype(BF)
    gk = (gkt_ref[...].astype(F32) + spread[:, D:]).astype(BF)
    gv = (gvk_ref[...].astype(F32) + gvc_ref[...].astype(F32)).astype(BF)
    gv_ref[...] = gv
    gq_ref[...] = gq
    gk_ref[...] = gk
    hbg_ref[0:1] = jnp.sum(gq.astype(F32), axis=0, keepdims=True)
    hbg_ref[1:2] = jnp.sum(gv.astype(F32), axis=0, keepdims=True)
    xt = x_ref[...].astype(F32).T.astype(BF)
    gt = gb_ref[...].astype(F32).T.astype(BF)
    mixed = mixed_ref[...]
    for side in range(2):
        cols = slice(side * half, (side + 1) * half)
        for r in range(2):
            rows = slice(r * half, (r + 1) * half)
            outs[r][side, :, :half] = nn(xt[rows], gq[:, cols]).astype(BF)
            outs[r][side, :, half:] = nn(xt[rows], gk[:, cols]).astype(BF)
            outs[2 + r][side, :, :half] = nn(xt[rows], gv[:, cols]).astype(BF)
            outs[2 + r][side, :, half:] = nn(gt[rows], mixed[:, cols]).astype(BF)


def input_grad_body(gq_ref, gk_ref, gv_ref, first_ref, perm_ref, w_ref, out_ref):
    half = first_ref.shape[1] // 2
    total = first_ref[...]
    for side in range(2):
        cols = slice(side * half, (side + 1) * half)
        total = total + nt(gq_ref[:, cols], w_ref[side, :, :half])
        total = total + nt(gk_ref[:, cols], w_ref[side, :, half : 2 * half])
        total = total + nt(gv_ref[:, cols], w_ref[side, :, 2 * half : 3 * half])
    out_ref[...] = nt(total.astype(BF), perm_ref[...]).astype(BF)


def back_body(n, ready, *refs):
    first, second, rest = refs[:n], refs[n : n + 8], refs[n + 8 :]
    ready(0, 5)
    conv_back_body(*second, rest[1], rest[2])
    ready(5)
    newton_back_body(*first, rest[0], rest[3])


def small_body(rows, ready, tap_ref, hbg_ref, fbg_ref, sums_ref, perm_ref, out_ref):
    ready()
    heads, width = tap_ref.shape
    T = width - 2 * META
    D = sums_ref.shape[1]
    top = rows - 7 * D // META - fbg_ref.shape[1] // 2 // META
    t = lax.broadcasted_iota(jnp.int32, (top, T), 0)
    lane = lax.broadcasted_iota(jnp.int32, (top, T), 1)
    main = ((lane + t - (REACH - 1)) % T == 0) & (t < KW)
    t = lax.broadcasted_iota(jnp.int32, (top, META), 0)
    lane = lax.broadcasted_iota(jnp.int32, (top, META), 1)
    before = (lane + t == REACH - 1) & (t < REACH)
    after = (lane + t == 3 * REACH - 1) & (t < KW)
    out = [jnp.zeros((top, META), F32), jnp.zeros((top, META), F32)]
    half = heads // 2
    for h in range(heads):
        row = tap_ref[h : h + 1, :]
        col = jnp.sum(jnp.where(main, row[:, :T], 0.0), axis=1, keepdims=True)
        col = col + jnp.sum(jnp.where(before, row[:, T : T + META], 0.0), axis=1, keepdims=True)
        col = col + jnp.sum(jnp.where(after, row[:, T + META :], 0.0), axis=1, keepdims=True)
        out[h // half] = jnp.where(lane == h % half, col, out[h // half])
    first = sums_ref[...].astype(BF)
    rest = sums_ref[...] - first.astype(F32)
    second = rest.astype(BF)
    third = (rest - second.astype(F32)).astype(BF)
    perm = perm_ref[...]
    sums = nt(first, perm) + nt(second, perm) + nt(third, perm)
    FL = fbg_ref.shape[1] // 2
    for side in range(2):
        ref = out_ref.at[side]
        ref[:top, :] = out[side]
        at = top
        for i in range(2):
            for j in range(D // 2 // META):
                col = side * (D // 2) + j * META
                ref[at : at + 1, :] = hbg_ref[i : i + 1, col : col + META]
                at += 1
        for j in range(FL // META):
            ref[at : at + 1, :] = fbg_ref[:, side * FL + j * META : side * FL + (j + 1) * META]
            at += 1
        for i in range(6):
            for j in range(D // META):
                ref[at : at + 1, :] = sums[i : i + 1, j * META : (j + 1) * META]
                at += 1


def fold_body(*refs):
    ins, (mine_ref, other_ref) = refs[:-2], refs[-2:]
    values = [r[...] for r in ins]
    while len(values) > 1:
        values = [a + b for a, b in zip(values[::2], values[1::2])]
    mine_ref[...] = values[0][0]
    other_ref[...] = values[0][1]


def add_body(a_ref, b_ref, c_ref, d_ref, first_ref, second_ref):
    first_ref[...] = a_ref[...] + b_ref[...]
    second_ref[...] = c_ref[...] + d_ref[...]


def small_out_body(a_ref, b_ref, c_ref, d_ref, conv_ref, hb_ref, fb_ref, gains_ref, offsets_ref):
    total = (a_ref[...] + b_ref[...]) + (c_ref[...] + d_ref[...])
    rows = total.shape[0]
    D = gains_ref.shape[1]
    FL = fb_ref.shape[1]
    at = rows - 7 * D // META - FL // META
    conv_ref[...] = total[:KW, : conv_ref.shape[1]]
    for i in range(2):
        for j in range(D // 2 // META):
            hb_ref[i : i + 1, j * META : (j + 1) * META] = total[at : at + 1]
            at += 1
    for j in range(FL // META):
        fb_ref[:, j * META : (j + 1) * META] = total[at : at + 1]
        at += 1
    for i in range(6):
        ref, r = (gains_ref, i) if i < 2 else (offsets_ref, i - 2)
        for j in range(D // META):
            ref[r : r + 1, j * META : (j + 1) * META] = total[at : at + 1]
            at += 1


def local(x_in, out_cot, seg_ids, land_doc, w_qkv, w_out, w_up, w_down, conv_taps, head_bias, ffn_bias, gains, offsets):
    nf, nc, nt_ = lax.axis_size("fsdp"), lax.axis_size("ctx"), lax.axis_size("tp")
    f_i, c_i, t_i = lax.axis_index("fsdp"), lax.axis_index("ctx"), lax.axis_index("tp")
    assert nt_ == 2 and x_in.shape[0] == 2
    ctx_bits = [("ctx", 1 << b) for b in range(nc.bit_length() - 1)]
    chip_bits = [("fsdp", 1 << b) for b in range(1, nf.bit_length() - 1)]
    core_bit = ("fsdp", 1)
    row_bits = ctx_bits + chip_bits + [core_bit]
    T, D = x_in.shape[1:]
    R = w_qkv.shape[0]
    C = w_qkv.shape[2]
    E = 2 * C
    FL = w_up.shape[1]
    HL = C // HEAD_DIM
    H = 2 * HL
    LL = land_doc.shape[1]
    L = LL * nc
    where = jnp.stack([f_i, c_i, t_i]).astype(jnp.int32)

    def along_ctx(own):
        return [own] + [swap(own, "ctx", p) for p in range(1, nc)]

    ud = lax.all_gather(jnp.concatenate([w_up, w_down], axis=0), ("fsdp", "ctx", "tp"), axis=0, tiled=True)
    ud = ud.reshape(nf * nc, 2, 2, R, FL)

    zq = along_ctx(jnp.concatenate([w_qkv.reshape(R, 3 * C), w_out], axis=1))
    x_in, out_cot = later((x_in, out_cot), zq[0])

    q_pos = jnp.arange(D, dtype=jnp.int32)
    piece, inner = q_pos // R, q_pos % R
    mf = jnp.zeros_like(piece)
    mc = jnp.zeros_like(piece)
    for i, (axis, mask) in enumerate(row_bits):
        bit = ((piece >> i) & 1) * mask
        if axis == "fsdp":
            mf = mf ^ bit
        else:
            mc = mc ^ bit
    true_piece = (f_i ^ mf) * nc + (c_i ^ mc)
    perm = (jnp.arange(D, dtype=jnp.int32)[:, None] == (true_piece * R + inner)[None, :]).astype(BF)
    aligned = R % 16 == 0
    if not aligned:
        order = true_piece[::R]
        sides = jnp.stack([t_i, 1 - t_i])
        ud = ud[order][:, sides].transpose(1, 2, 0, 3, 4).reshape(1, 2, 2, D, FL)

    def pick(a):
        return lax.dynamic_index_in_dim(a, t_i, 0, False)

    x = dot("td,dq->tq", pick(x_in), perm).astype(BF)
    cot = dot("td,dq->tq", pick(out_cot), perm).astype(BF)

    own = jnp.concatenate(zq, 0)
    for bit in chip_bits[:-1]:
        own = jnp.concatenate([own, swap(own, *bit)], 0)
    last_bit = chip_bits[-1]
    by_chip, by_half = swap(own, *last_bit), swap(own, "tp", 1)
    both_one, both_two = swap(by_chip[:, : 2 * C], "tp", 1), swap(by_half[:, 2 * C :], *last_bit)

    seg_ids, land_doc, conv_taps, head_bias, ffn_bias = later((seg_ids, land_doc, conv_taps, head_bias, ffn_bias), zq[0])
    seg = pick(seg_ids).astype(F32)
    doc = pick(land_doc).astype(F32)
    seg_col = seg[:, None]

    def meta(col):
        return jnp.where(jnp.arange(META)[None, :] == 0, col[:, None], 0.0).astype(BF)

    par = jnp.concatenate([conv_taps.reshape(-1), head_bias.reshape(-1), ffn_bias.reshape(-1)])
    par2 = jnp.stack([par, swap(par, "tp", 1)])
    taps = par2[:, : KW * HL].reshape(2, KW, HL).transpose(0, 2, 1).reshape(H, KW)
    hb = par2[:, KW * HL : KW * HL + 2 * C].reshape(2, 2, C).transpose(1, 0, 2).reshape(2, 2 * C)
    fb = par2[:, KW * HL + 2 * C :].reshape(1, 2 * FL)
    vec = hdot("vd,dq->vq", jnp.concatenate([gains, offsets], 0), perm.astype(F32))
    gap = jnp.zeros((H, T - KW), F32)
    taps_rev = taps[:, ::-1]
    row_fwd = jnp.concatenate([taps[:, REACH:], gap, taps[:, :REACH]], 1)
    row_back = jnp.concatenate([taps_rev[:, REACH:], gap, taps_rev[:, :REACH]], 1)

    parts = [own, by_chip, by_half, both_one, both_two]
    parts = parts + [swap(a, *core_bit) for a in parts]
    parts = later(parts, hb, fb, vec, row_fwd, row_back, cot)
    q, k, v, qkv, piece0, vfirst, vlast, w_full = call(
        proj_body,
        [((T, E), BF)] * 3 + [((3, T, E), BF), ((LL, 2 * E + META), BF)] + [((REACH, E + META), BF)] * 2 + [((2, D, 4 * C), BF)],
        x, hb, meta(doc), meta(seg[:REACH] + 1.0), meta(seg[T - REACH :] + 1.0), *parts,
        raw_in=range(5, 15),
        raw_out=(3, 7),
        scratch=[pltpu.VMEM((2, D, 4 * C), BF), pltpu.SemaphoreType.DMA((10,)), pltpu.SemaphoreType.DMA, pltpu.SemaphoreType.DMA((3,))],
        mem=14,
    )

    up = [(i, i + 1) for i in range(nc - 1)]
    down = [(i + 1, i) for i in range(nc - 1)]
    pieces = along_ctx(piece0)
    ktok, ekey, pack, land, land_far = call(
        functools.partial(scores_body, nc),
        [((E, T), BF), ((E, T), BF), ((L, E + META), BF), ((L, 2 * E + META), BF), ((L, 2 * E + META), BF)],
        where, q, k, v, seg_col, *pieces, smem=(0,), far_out=(0, 1, 4), name="scores_body",
    )
    packs = along_ctx(pack)
    vlast, vfirst = later((vlast, vfirst), pack)
    v_before, v_after = lax.ppermute(vlast, "ctx", up), lax.ppermute(vfirst, "ctx", down)
    (conv,) = call(simple(conv_body), [((T, E), BF)], row_fwd, seg_col, v, v_before, v_after, far_in=(0, 1), far_out=(0,))
    kt, mixer, p_all, w_all, pi_all = call(
        simple(newton_body), [((L, E), F32), ((L, E), F32)] + [((NEWTON, L, E), F32)] * 3, land, far_out=range(5), us=5.5, mem=10
    )
    n_pieces = D // R if aligned else 1
    res = call(
        functools.partial(mid_body, nc, n_pieces, row_bits, nc),
        [((T, E), BF), ((L, E), F32), ((L, E), F32), ((L, META), F32), ((T, E), BF), ((T, D), BF), ((T, E), BF)]
        + [((REACH, E), BF)] * 2
        + [((L, E), BF), ((T, D), F32), ((T, D), BF), ((8, D), F32), ((1, 2 * FL), F32)]
        + [((2, D // 2, FL), BF)] * 4,
        where, *packs, mixer, ktok, conv, land_far, x, cot, perm, vec, fb, qkv, w_full, ud,
        us=24.0,
        mem=30,
        smem=(0,),
        far_in=range(1, nc + 10),
        raw_in=(nc + 10, nc + 11, nc + 12),
        far_out=(5,),
        scratch=[
            pltpu.VMEM((2, D, C), BF),
            pltpu.VMEM((2, D, FL), BF),
            pltpu.VMEM((2, D, FL), BF),
            pltpu.VMEM((T, 2 * FL), BF),
            pltpu.VMEM((T, 2 * FL), F32),
            pltpu.VMEM((L, E), F32),
            pltpu.VMEM((1, T, E), BF),
            pltpu.SemaphoreType.DMA((2, 2 * n_pieces)),
            pltpu.SemaphoreType.DMA((2,)),
        ],
        name="mid_body",
    )
    gq, lk_part, lval, land_scale, mixed, y, gm, gfirst, glast, gmix0, grad_first, grad_branch, sums, fb_grad = res[:14]
    keep_up, send_up, keep_down, send_down = res[14:]

    every = slice(None)

    def cores_sum(keep, send):
        got = swap(send, *core_bit)
        for bit in reversed(chip_bits[1:]):
            half = keep.shape[1] // 2
            more = swap(add(keep[:, half:], got[:, half:]), *bit)
            keep, got = add(keep[:, :half], got[:, :half]), more
        return keep, got

    bit = chip_bits[0]
    low_rows, high_rows = slice(0, nc * R), slice(nc * R, 2 * nc * R)

    def one_start(keep, got):
        (other,) = combine([[[(0, (1,)), (1, (1,))]]], keep, got, near=aligned)
        return other, swap(other, "tp", 1)

    def two_start(keep, got):
        (send,) = combine([[[(0, (every, high_rows)), (1, (every, high_rows))]]], keep, got, near=aligned)
        return send, swap(send, *bit)

    def one_next(keep, got, more):
        (send,) = combine([[[(0, (0, high_rows)), (1, (0, high_rows)), (2, (high_rows,))]]], keep, got, more, near=aligned)
        return send, swap(send, *bit)

    def two_next(keep, got, more):
        (send,) = combine([[[(0, (1, low_rows)), (1, (1, low_rows)), (2, (1,))]]], keep, got, more, near=aligned)
        return send, swap(send, "tp", 1)

    def ctx_cuts(one, two, far_in=()):
        plan = []
        for p in range(nc):
            rows = slice(p * R, (p + 1) * R)
            plan.append(
                [
                    [(0, (0, rows)), (1, (0, rows)), (2, (rows,)), (3, (rows,))],
                    [(4, (0, rows)), (5, (0, rows)), (6, (0, rows)), (7, (rows,))],
                ]
            )
        return combine(plan, *one, *two, near=aligned, far_in=far_in)

    def ctx_total(one, two):
        if not aligned:
            cuts = jnp.stack(ctx_cuts(one, two))
            return cuts[c_i ^ jnp.arange(nc)].reshape(nc * R, -1)
        width = one[2].shape[1]

        def total_body(ready, where_ref, *refs):
            ins, out = refs[:8], refs[8]
            for p in range(nc):
                rows = slice(p * R, (p + 1) * R)
                at = pl.ds(pl.multiple_of((where_ref[1] ^ p) * R, R), R)
                for i in range(2):
                    t = ins[4 * i : 4 * i + 4]
                    third = t[2][rows] if i == 0 else t[2][0, rows]
                    total = t[0][0, rows].astype(F32) + t[1][0, rows].astype(F32) + third.astype(F32) + t[3][rows].astype(F32)
                    out[at, i * width : (i + 1) * width] = total.astype(BF)

        (out,) = call(total_body, [((nc * R, 2 * width), BF)], where, *one, *two, smem=(0,), far_out=(0,), mem=16)
        return out

    def ctx_swap(cuts):
        return [cuts[0]] + [swap(cuts[p], "ctx", p) for p in range(1, nc)]

    def pairs(values):
        while len(values) > 1:
            values = [a + b for a, b in zip(values[::2], values[1::2])]
        return values[0]

    def total(parts):
        return sum(p.astype(F32) for p in parts)

    gmixes = along_ctx(gmix0)
    down2 = cores_sum(keep_down, send_down)
    up2 = cores_sum(keep_up, send_up)
    y_other = swap(y, "tp", 1)
    down2, up2 = later((down2, up2), *gmixes)
    up2 = later(up2, y_other)
    down_sent, down_more = two_start(*down2)
    up_sent, up_more = one_start(*up2)
    res = call(
        functools.partial(key_back_body, nc),
        [((L, E), F32), ((T, E), BF), ((T, E), BF), ((LL, 2 * E), F32)] + [((LL, 2 * E), BF)] * (nc - 1),
        where, *later(gmixes, up_sent, down_sent), mixer, lval, ekey, land_scale, qkv, land_far, lk_part,
        smem=(0,),
        far_in=(nc + 1, nc + 3, nc + 5, nc + 6),
        scratch=[pltpu.VMEM((L, 2 * E), F32)],
        us=3.0,
        mem=12,
        name="key_back_body",
    )
    gmix, gv, gk, own_part = res[:4]
    parts = [own_part] + [swap(a, "ctx", p + 1) for p, a in enumerate(res[4:])]
    glast, gfirst = later((glast, gfirst), own_part)
    g_before, g_after = lax.ppermute(glast, "ctx", up), lax.ppermute(gfirst, "ctx", down)
    own_mix, gvc, tap_all = call(
        functools.partial(back_body, 9), [((LL, 2 * E), F32), ((T, E), BF), ((H, T + 2 * META), F32)],
        land_far, kt, p_all, w_all, pi_all, mixer, gmix, lval, where,
        row_back, seg_col, gm, g_before, g_after, qkv, v_before, v_after,
        smem=(8,),
        far_in=(9, 10, 14, 15, 16, 0, 1, 2, 3, 4, 5),
        scratch=[pltpu.VMEM((L, 2 * E), F32)],
        us=11.0,
        mem=18,
        name="back_body",
    )
    gq, gk, gv, hb_grad, keep1, send1, keep2, send2 = call(
        functools.partial(grad_body, nc),
        [((T, E), BF)] * 3 + [((2, E), F32)] + [((2, D // 2, 2 * C), BF)] * 4,
        *parts, own_mix, gq, later(gk, up_more, down_more), gv, gvc, x, grad_branch, mixed,
        far_in=(nc + 5,),
        us=3.0,
        mem=10,
        name="grad_body",
    )
    down_sent2, down_more2 = two_next(*down2, later(down_more, hb_grad))
    up_sent2, up_more2 = one_next(*up2, later(up_more, hb_grad))
    vo2 = cores_sum(keep2, send2)
    qk2 = cores_sum(keep1, send1)
    vo_sent, vo_more = two_start(*later(vo2, down_sent2, up_sent2))
    qk_sent, qk_more = one_start(*later(qk2, down_sent2, up_sent2))
    rows = -(-KW // 8) * 8 + (7 * D + FL) // META
    rows += -rows % 8
    (small,) = call(
        functools.partial(small_body, rows), [((2, rows, META), F32)], later(tap_all, vo_sent, qk_sent), hb_grad, fb_grad, sums, perm,
        far_in=(0, 4), mem=12, name="small_body",
    )
    halves = [((rows, META), F32)] * 2
    (gx,) = call(
        simple(input_grad_body), [((T, D), BF)], later(gq, small), gk, gv, grad_first, perm, w_full,
        far_in=(4, 5), far_out=(0,), us=4.0, mem=14,
    )
    cuts_ud = [ctx_total((*up2, *later((up_more, up_more2), gx)), (*down2, down_more, down_more2))]
    ctx_ud = [lax.psum_scatter(cuts_ud[0], "ctx", scatter_dimension=0, tiled=True)]
    small_ctx = along_ctx(later(small, *cuts_ud))
    small, small_other = call(simple(fold_body), halves, *small_ctx)
    small_got = [swap(small, *core_bit), swap(small_other, *core_bit)]
    vo_sent2, vo_more2 = two_next(*vo2, later(vo_more, small))
    qk_sent2, qk_more2 = one_next(*qk2, later(qk_more, small))
    small_got = later(small_got, vo_sent2, qk_sent2)
    small, small_other = call(simple(add_body), halves, small, small_got[0], small_other, small_got[1])
    for extra in chip_bits[1:]:
        small, small_other = small + swap(small, *extra), small_other + swap(small_other, *extra)
    small_got = [swap(small, *bit), swap(small_other, "tp", 1), swap_both(small_other, bit[1])]
    cuts_q = ctx_cuts((*qk2, qk_more, later(qk_more2, small)), (*vo2, vo_more, vo_more2), (1, 2, 6))
    ctx_q = ctx_swap(cuts_q)
    gx, small_got, ctx_ud, y, y_other = later((gx, small_got, ctx_ud, y, y_other), *cuts_q)
    ud_grad = total(ctx_ud)
    conv_grad, hb_out, fb_out, gains_out, offsets_out = call(
        simple(small_out_body),
        [((KW, HL), F32), ((2, C), F32), ((1, FL), F32), ((2, D), F32), ((4, D), F32)],
        small, *small_got,
    )


    def place(mine, other):
        first = t_i == 0
        return jnp.stack([jnp.where(first, mine, other), jnp.where(first, other, mine)])

    y_all, x_all = place(y, y_other), place(gx, swap(gx, "tp", 1))
    ud_up, ud_down = ud_grad[:, :FL], ud_grad[:, FL:]
    qo = total(later(ctx_q, y_all, x_all, ud_up, ud_down, conv_grad))

    return (
        y_all,
        x_all,
        qo[:, : 3 * C].reshape(R, 3, C),
        qo[:, 3 * C :],
        ud_up,
        ud_down,
        conv_grad,
        hb_out,
        fb_out[0],
        gains_out,
        offsets_out,
    )


def solution(mesh):
    placed = (
        P("fsdp", "ctx", None),
        P("fsdp", "ctx", None),
        P("fsdp", "ctx"),
        P("fsdp", "ctx"),
        P(("fsdp", "ctx"), None, "tp"),
        P(("fsdp", "ctx"), "tp"),
        P(("fsdp", "ctx"), "tp"),
        P(("fsdp", "ctx"), "tp"),
        P(None, "tp"),
        P(None, "tp"),
        P("tp"),
        P(),
        P(),
    )
    return jax.shard_map(
        local,
        mesh=mesh,
        in_specs=placed,
        out_specs=placed[:2] + placed[4:],
        check_vma=False,
    )
```
